512 devices in a mesh: gy: 16 (over z), gx: 32 (over x, y, core).
Axes of the slice: x: 4, y: 4, z: 16, core: 2. Of those that a mesh axis runs over, the one named last changes fastest.
Arguments:
- observed: float32 [16, 512, 4096], P(None, 'gy', 'gx'), may hold values from 0 to 20, as said below
- profiles: float32 [64, 3, 9], replicated, may hold values from 0.03 to 0.25
- tile_index: int32 [16, 32], replicated, may hold values from 0 to 63
Outputs:
- estimate: float32 [16, 512, 4096], P(None, 'gy', 'gx')
The draws below stay inside these ranges and needn't reach their ends.
Inputs may be any that keep to these rules, and one draw needn't show every extreme that they name: `observed`: nonnegative intensities.
All inputs are finite; a program needn't handle non-finite values.
Results may differ from the reference program's by a relative error of at most 0.0003.
Values sent between devices are 32-bit elements; how exact they have to be, the bound alone decides.
A program may use at most 64 MiB of HBM per device.

```python
import math
import jax
import jax.numpy as jnp
from jax import lax

Z = 16
CY = 32
CX = 128
ITERS = 2
TAPS = 9
KERNELS = 64
NY = 512
NX = 4096
GRID_ROWS = 16
GRID_COLS = 32
N_GY = 16
N_GX = 32


def draw_observed(key, part):
    uniform_key = jax.random.fold_in(key, 0)
    uniform_part = jax.random.uniform(uniform_key, (Z, NY, NX), jnp.float32)
    rising = (1.0 + 2.0 * jnp.arange(NY, dtype=jnp.float32) / NY)[:, None] * (1.0 + 0.5 * jnp.arange(NX, dtype=jnp.float32) / NX)[None, :]
    return uniform_part * rising[None]


def plant(result, stream_key, low, largest):
    place = [jax.random.randint(jax.random.fold_in(stream_key, axis), (), 0, length) for axis, length in enumerate(result.shape)]
    main_axis = result.shape.index(max(result.shape))
    beside = place[:main_axis] + [(place[main_axis] + 1) % result.shape[main_axis]] + place[main_axis + 1:]
    return result.at[tuple(place)].set(low).at[tuple(beside)].set(largest)


def setup_inputs(seed: int = 0) -> dict:
    splits = jax.random.split(jax.random.key(seed), 4)
    observed = draw_observed(jax.random.fold_in(splits[3], 71), 0)
    profiles = jnp.clip(jnp.exp(jax.random.uniform(splits[1], (KERNELS, 3, TAPS), jnp.float32, math.log(0.03), math.log(0.25))), 0.03, 0.25)
    tile_index = plant(jax.random.randint(splits[2], (GRID_ROWS, GRID_COLS), 0, KERNELS), jax.random.fold_in(splits[2], 1), 0, KERNELS - 1).astype(jnp.int32)
    return dict(observed=observed, profiles=profiles, tile_index=tile_index)


WEIGHT_TV = 0.02
SMOOTHING = 0.1
DAMPING = 0.05
START_STEP = 0.5

def shifted_sum(padded, profile, dimension, extent):
    radius = (profile.shape[0] - 1) // 2
    summed = jnp.zeros_like(lax.slice_in_dim(padded, 0, extent, axis=dimension))
    for offset in range(profile.shape[0]):
        opening = 2 * radius - offset
        summed = summed + profile[offset] * lax.slice_in_dim(padded, opening, opening + extent, axis=dimension)
    return summed

def blur_window(window, profile):
    radius = (profile.shape[1] - 1) // 2
    depth_padded = jnp.pad(window, ((radius, radius), (0, 0), (0, 0)))
    along_depth = shifted_sum(depth_padded, profile[0], 0, Z)
    along_rows = shifted_sum(along_depth, profile[1], 1, CY)
    return shifted_sum(along_rows, profile[2], 2, CX)

def blur_volume(estimate, profiles, tile_index):
    radius = (profiles.shape[2] - 1) // 2
    padded = jnp.pad(estimate, ((0, 0), (radius, radius), (radius, radius)))

    def one_block(number):
        block_row = number // N_GX
        block_col = number % N_GX
        window = lax.dynamic_slice(padded, (jnp.int32(0), (block_row * CY).astype(jnp.int32), (block_col * CX).astype(jnp.int32)), (Z, CY + 2 * radius, CX + 2 * radius))
        return blur_window(window, profiles[tile_index[block_row, block_col]])
    blocks = lax.map(one_block, jnp.arange(N_GY * N_GX, dtype=jnp.int32))
    blocks = blocks.reshape(N_GY, N_GX, Z, CY, CX).transpose(2, 0, 3, 1, 4)
    return blocks.reshape(Z, N_GY * CY, N_GX * CX)

def variation(estimate):
    diff_depth = jnp.concatenate([estimate[1:] - estimate[:-1], jnp.zeros_like(estimate[:1])], 0)
    diff_rows = jnp.concatenate([estimate[:, 1:] - estimate[:, :-1], jnp.zeros_like(estimate[:, :1])], 1)
    diff_cols = jnp.concatenate([estimate[:, :, 1:] - estimate[:, :, :-1], jnp.zeros_like(estimate[:, :, :1])], 2)
    return jnp.sum(jnp.sqrt(diff_depth * diff_depth + diff_rows * diff_rows + diff_cols * diff_cols + SMOOTHING * SMOOTHING))

def gradient(estimate, observed, profiles, tile_index):
    blurred, pullback = jax.vjp(lambda value: blur_volume(value, profiles, tile_index), estimate)
    pulled = pullback(blurred - observed)[0]
    return pulled + WEIGHT_TV * jax.grad(variation)(estimate) + DAMPING * estimate

def reference(observed, profiles, tile_index):
    previous = observed
    prev_descent = gradient(previous, observed, profiles, tile_index)
    current = previous - START_STEP * prev_descent
    for iteration in range(ITERS):
        descent = gradient(current, observed, profiles, tile_index)
        change = current - previous
        growth = descent - prev_descent
        step_size = jnp.sum(change * change) / jnp.sum(change * growth)
        previous, prev_descent = (current, descent)
        current = current - step_size * descent
    return current
```

```python
import functools

import jax
import jax.numpy as jnp
from jax import lax
from jax.experimental import pallas as pl
from jax.experimental.pallas import tpu as pltpu
from jax.sharding import PartitionSpec as P

WEIGHT_TV = 0.02
SMOOTHING = 0.1
DAMPING = 0.05
START_STEP = 0.5
RADIUS = 4
TAPS = 9
Z, CY, CX = 16, 32, 128
EXT = CY + 16
MESH = pl.DeviceIdType.MESH
F32 = jnp.float32
BF16 = jnp.bfloat16
SIDES = ((-1, 0), (1, 0), (0, -1), (0, 1), (-1, -1), (-1, 1), (1, -1), (1, 1))


def kernel(
    ny, nx,
    obs_hbm, prof, tiles, out_ref,
    u_ext, g_ext, grad, tv, resid, back, spread, blur_in, blur_y, flux,
    fwd_hi, fwd_lo, bwd_hi, bwd_lo, lhs_hi, lhs_lo,
    ux, gx_halo, own_edge, edge_pad, edge_spill,
    send_y, recv_y, send_x, recv_x,
    part, all_x, part_y, all_y,
    load_sem, send_sem, recv_sem, ar_send, ar_recv,
):
    row = lax.axis_index("gy")
    col = lax.axis_index("gx")

    def at(dy, dx):
        return {
            "gy": lax.rem(row + dy + ny, ny),
            "gx": lax.rem(col + dx + nx, nx),
        }

    load = pltpu.make_async_copy(obs_hbm, u_ext.at[:, pl.ds(8, CY), :], load_sem)
    load.start()

    barrier = pltpu.get_barrier_semaphore()

    def greet_x(i, c):
        pl.semaphore_signal(barrier, inc=1, device_id=at(0, i), device_id_type=MESH)
        return c

    def greet_y(i, c):
        pl.semaphore_signal(barrier, inc=1, device_id=at(i, 0), device_id_type=MESH)
        return c

    lax.fori_loop(1, nx, greet_x, 0)
    lax.fori_loop(1, ny, greet_y, 0)
    for dy in (-1, 1):
        for dx in (-1, 1):
            pl.semaphore_signal(barrier, inc=1, device_id=at(dy, dx), device_id_type=MESH)

    number = tiles[row, col]
    depth = [prof[a, 0, number] for a in range(TAPS)]
    along = [prof[a, 1, number] for a in range(TAPS)]
    across = [prof[a, 2, number] for a in range(TAPS)]

    lane = lax.broadcasted_iota(jnp.int32, (1, CX), 1)
    sub8 = lax.broadcasted_iota(jnp.int32, (8, CX), 0)
    low_half = sub8 < 4
    plane_of = lane // 8
    place = lane - plane_of * 8
    first_row, last_row = row == 0, row == ny - 1
    first_col, last_col = col == 0, col == nx - 1

    mk = lax.broadcasted_iota(jnp.int32, (CX, CX), 0)
    mn = lax.broadcasted_iota(jnp.int32, (CX, CX), 1)

    def band(diff, offset):
        total = jnp.zeros((CX, CX), F32)
        for c in range(TAPS):
            total = jnp.where(diff == c - offset, across[c], total)
        return total

    def wrapped(diff):
        total = jnp.zeros((CX, CX), F32)
        for c in range(TAPS):
            hit = (diff == c - RADIUS - CX) | (diff == c - RADIUS + CX)
            total = jnp.where(hit, across[c], total)
        return total

    def halves(value):
        high = value.astype(BF16)
        return high, (value - high.astype(F32)).astype(BF16)

    ahead = mn - mk
    for part_no, w in enumerate((band(ahead, RADIUS), wrapped(ahead))):
        high, low = halves(w)
        fwd_hi[pl.ds(part_no * CX, CX), :] = high
        fwd_lo[pl.ds(part_no * CX, CX), :] = low
    behind = mk - mn
    for part_no, w in enumerate((band(behind, RADIUS), wrapped(behind))):
        high, low = halves(w)
        bwd_hi[:, pl.ds(part_no * CX, CX)] = high
        bwd_lo[:, pl.ds(part_no * CX, CX)] = low

    back[:, pl.ds(0, 16), :] = jnp.zeros((Z, 16, CX), F32)
    back[:, pl.ds(16 + CY, 16), :] = jnp.zeros((Z, 16, CX), F32)
    edge_pad[pl.ds(0, 16), :] = jnp.zeros((16, CX), F32)
    edge_pad[pl.ds(16 + CY, 16), :] = jnp.zeros((16, CX), F32)

    load.wait()
    pl.semaphore_wait(barrier, nx - 1 + ny - 1 + 4)

    def planes(body, init, step=4):
        def some(i, carry):
            for k in range(step):
                carry = body(i * step + k, carry)
            return carry

        return lax.fori_loop(0, Z // step, some, init)

    def pack_columns(read):
        def body(p, total):
            turned = pltpu.roll(read(p), 8 * p + 4, 1)
            return jnp.where(plane_of == p, turned, total)

        return planes(body, jnp.zeros((CY, CX), F32))

    def copies(r):
        made = []
        for k, (dy, dx) in enumerate(SIDES):
            if dx == 0:
                src = send_y.at[r, 0 if dy < 0 else 1]
                dst = recv_y.at[r, 1 if dy < 0 else 0]
            else:
                start, size = {-1: (0, 8), 0: (8, CY), 1: (8 + CY, 8)}[dy]
                land = {-1: 8 + CY, 0: 8, 1: 0}[dy]
                src = send_x.at[r, pl.ds(start, size), :]
                dst = recv_x.at[r, 1 if dx < 0 else 0, pl.ds(land, size), :]
            made.append(
                pltpu.make_async_remote_copy(
                    src_ref=src, dst_ref=dst,
                    send_sem=send_sem.at[r, k], recv_sem=recv_sem.at[r, k],
                    device_id=at(dy, dx), device_id_type=MESH,
                )
            )
        return made

    def send(r):
        made = copies(r)
        for k in (4, 5, 6, 7, 2, 3, 0, 1):
            made[k].start()
        return made

    def halo_send(r, ext, edges_out):
        edge = pack_columns(lambda p: ext[p, pl.ds(8, CY), :])
        edges_out[...] = edge
        send_x[r, pl.ds(8, CY), :] = edge
        send_x[r, pl.ds(0, 8), :] = edge[0:8]
        send_x[r, pl.ds(8 + CY, 8), :] = edge[CY - 8 : CY]
        for q in range(8):
            top, top2 = ext[q, pl.ds(8, 8), :], ext[q + 8, pl.ds(8, 8), :]
            send_y[r, 0, q] = jnp.where(low_half, top, pltpu.roll(top2, 4, 0))
            low, low2 = ext[q, pl.ds(CY, 8), :], ext[q + 8, pl.ds(CY, 8), :]
            send_y[r, 1, q] = jnp.where(low_half, pltpu.roll(low, 4, 0), low2)
        return send(r)

    def halo_wait(r, made, ext, halo):
        for c in made:
            c.wait_recv()
        for q in range(8):
            above = jnp.where(first_row, 0.0, recv_y[r, 0, q])
            ext[q, pl.ds(0, 8), :] = pltpu.roll(above, 4, 0)
            ext[q + 8, pl.ds(0, 8), :] = above
            below = jnp.where(last_row, 0.0, recv_y[r, 1, q])
            ext[q, pl.ds(8 + CY, 8), :] = below
            ext[q + 8, pl.ds(8 + CY, 8), :] = pltpu.roll(below, 4, 0)
        halo[...] = sides(r, place < 4)

    def sides(r, from_left):
        left = jnp.where(first_col, 0.0, recv_x[r, 0])
        right = jnp.where(last_col, 0.0, recv_x[r, 1])
        both = jnp.where(from_left, left, right)
        at_row = lax.broadcasted_iota(jnp.int32, (EXT, CX), 0)
        both = jnp.where(first_row & (at_row < 8), 0.0, both)
        return jnp.where(last_row & (at_row >= 8 + CY), 0.0, both)

    def depth_blur(read, write, transposed):
        for t in range(CY // 8):
            value = [read(p, t) for p in range(Z)]
            for p in range(Z):
                total = None
                for a in range(TAPS):
                    source = p - RADIUS + a if transposed else p + RADIUS - a
                    if 0 <= source < Z:
                        term = depth[a] * value[source]
                        total = term if total is None else total + term
                write(p, t, total)

    def blur(ext, halo, write):
        edge = jnp.zeros((CY, CX), F32)
        for b in range(TAPS):
            edge = edge + along[b] * halo[pl.ds(8 + RADIUS - b, CY), :]

        def body(p, c):
            total = along[0] * ext[p, pl.ds(8 + RADIUS, CY), :]
            for b in range(1, TAPS):
                total = total + along[b] * ext[p, pl.ds(8 + RADIUS - b, CY), :]
            here = pl.ds(pl.multiple_of(p * CY, CY), CY)
            high, low = halves(total)
            lhs_hi[here, pl.ds(0, CX)] = high
            lhs_lo[here, pl.ds(0, CX)] = low
            high, low = halves(pltpu.roll(edge, 124 - 8 * p, 1))
            lhs_hi[here, pl.ds(CX, CX)] = high
            lhs_lo[here, pl.ds(CX, CX)] = low
            return c

        planes(body, 0)
        mixed = jnp.dot(lhs_hi[...], fwd_hi[...], preferred_element_type=F32)
        mixed = mixed + jnp.dot(lhs_lo[...], fwd_hi[...], preferred_element_type=F32)
        mixed = mixed + jnp.dot(lhs_hi[...], fwd_lo[...], preferred_element_type=F32)
        blur_y[:, pl.ds(0, CX)] = mixed
        depth_blur(lambda p, t: blur_y[pl.ds(p * CY + t * 8, 8), pl.ds(0, CX)], write, False)

    def spill_send(r, field):
        def keep(p, t, value):
            high, low = halves(value)
            here = pl.ds(p * CY + t * 8, 8)
            blur_in[p, pl.ds(t * 8, 8), :] = value

        depth_blur(lambda p, t: field[p, pl.ds(t * 8, 8), :], keep, True)
        whole = blur_in[...].reshape(Z * CY, CX)
        high, low = halves(whole)
        mixed = jnp.dot(high, bwd_hi[...], preferred_element_type=F32)
        mixed = mixed + jnp.dot(low, bwd_hi[...], preferred_element_type=F32)
        mixed = mixed + jnp.dot(high, bwd_lo[...], preferred_element_type=F32)
        blur_y[...] = mixed

        def split(p, total):
            here = pl.ds(pl.multiple_of(p * CY, CY), CY)
            back[p, pl.ds(16, CY), :] = blur_y[here, pl.ds(0, CX)]
            turned = pltpu.roll(blur_y[here, pl.ds(CX, CX)], 8 * p + 4, 1)
            return jnp.where(plane_of == p, turned, total)

        edge_pad[pl.ds(16, CY), :] = planes(split, jnp.zeros((CY, CX), F32))
        edge = along[0] * edge_pad[pl.ds(4, EXT), :]
        for b in range(1, TAPS):
            edge = edge + along[b] * edge_pad[pl.ds(4 + b, EXT), :]
        edge_spill[...] = edge
        send_x[r] = edge

        def body(p, c):
            total = along[0] * back[p, pl.ds(4, EXT), :]
            for b in range(1, TAPS):
                total = total + along[b] * back[p, pl.ds(4 + b, EXT), :]
            spread[p] = total
            return c

        planes(body, 0)
        for q in range(8):
            top, top2 = spread[q, pl.ds(0, 8), :], spread[q + 8, pl.ds(0, 8), :]
            send_y[r, 0, q] = jnp.where(low_half, pltpu.roll(top, 4, 0), top2)
            low, low2 = spread[q, pl.ds(8 + CY, 8), :], spread[q + 8, pl.ds(8 + CY, 8), :]
            send_y[r, 1, q] = jnp.where(low_half, low, pltpu.roll(low2, 4, 0))
        return send(r)

    def spill_wait(r, made):
        for c in made:
            c.wait_recv()
        both = sides(r, place >= 4)
        top = both[8:16] + both[0:8]
        low = both[CY : CY + 8] + both[CY + 8 : CY + 16]
        edge = jnp.concatenate([top, both[16:CY], low], axis=0)
        border = (lane < 4) | (lane >= CX - 4)
        for q in range(8):
            above = jnp.where(first_row, 0.0, recv_y[r, 0, q])
            below = jnp.where(last_row, 0.0, recv_y[r, 1, q])
            t, b = pl.ds(8, 8), pl.ds(CY, 8)
            spread[q, t, :] = spread[q, t, :] + jnp.where(low_half, above, 0.0)
            spread[q + 8, t, :] = spread[q + 8, t, :] + jnp.where(low_half, pltpu.roll(above, 4, 0), 0.0)
            spread[q, b, :] = spread[q, b, :] + jnp.where(low_half, 0.0, pltpu.roll(below, 4, 0))
            spread[q + 8, b, :] = spread[q + 8, b, :] + jnp.where(low_half, 0.0, below)

        def body(p, c):
            extra = jnp.where(border, pltpu.roll(edge, 124 - 8 * p, 1), 0.0)
            spread[p, pl.ds(8, CY), :] = spread[p, pl.ds(8, CY), :] + extra
            return c

        planes(body, 0)

    rows40 = lax.broadcasted_iota(jnp.int32, (40, CX), 0)
    rows32 = lax.broadcasted_iota(jnp.int32, (CY, CX), 0)
    no_row_diff = last_row & (rows40 == 39)
    no_row_flux = first_row & (rows40 == 7)
    no_col_diff = last_col & (lane == CX - 1)

    def inverse_size(dx, dy, dz):
        return lax.rsqrt(dx * dx + dy * dy + dz * dz + SMOOTHING * SMOOTHING)

    def variation(ext, halo, edges, write):
        here = halo[pl.ds(8, CY), :]
        dx = pltpu.roll(edges, CX - 1, 1) - here
        dy = halo[pl.ds(9, CY), :] - here
        dy = jnp.where(last_row & (rows32 == CY - 1), 0.0, dy)
        dz = jnp.where(plane_of == Z - 1, 0.0, pltpu.roll(here, CX - 8, 1) - here)
        side = jnp.where(first_col, 0.0, dx * inverse_size(dx, dy, dz))
        around = halo[pl.ds(0, 40), :]

        def body(p, before):
            u = ext[p, pl.ds(0, 40), :]
            dy = jnp.where(no_row_diff, 0.0, ext[p, pl.ds(1, 40), :] - u)
            beyond = pltpu.roll(around, 124 - 8 * p, 1)
            dx = pltpu.roll(jnp.where(lane == 0, beyond, u), CX - 1, 1) - u
            dx = jnp.where(no_col_diff, 0.0, dx)
            after = ext[jnp.minimum(p + 1, Z - 1), pl.ds(0, 40), :]
            dz = after - u
            inverse = inverse_size(dx, dy, dz)
            fy = jnp.where(no_row_flux, 0.0, dy * inverse)
            flux[...] = fy
            fx = (dx * inverse)[8:40]
            fz = (dz * inverse)[8:40]
            fx_side = pltpu.roll(side, 124 - 8 * p, 1)
            fx_before = pltpu.roll(jnp.where(lane == CX - 1, fx_side, fx), 1, 1)
            slope = (before - fz) + (flux[pl.ds(7, CY), :] - fy[8:40]) + (fx_before - fx)
            write(p, slope)
            return fz

        planes(body, jnp.zeros((CY, CX), F32), 2)

    def fold(values):
        total = jnp.zeros((1, CX), F32)
        for i, value in enumerate(values):
            v = jnp.sum(value, axis=0, keepdims=True)
            v = v + pltpu.roll(v, 64, 1)
            v = v + pltpu.roll(v, 32, 1)
            total = jnp.where(lane // 32 == i, v, total)
        return total

    def reduce_start(a, values):
        mine = fold(values)
        part[a] = mine
        all_x[a, pl.ds(col, 1)] = mine.reshape(1, 1, CX)

        def go(i, c):
            pltpu.make_async_remote_copy(
                src_ref=part.at[a], dst_ref=all_x.at[a, col],
                send_sem=ar_send.at[a, 0], recv_sem=ar_recv.at[a, 0],
                device_id=at(0, i), device_id_type=MESH,
            ).start()
            return c

        lax.fori_loop(1, nx, go, 0)

    def reduce_middle(a):
        got = all_x.at[a, pl.ds(0, nx - 1)]
        pltpu.make_async_copy(got, got, ar_recv.at[a, 0]).wait()
        mine = jnp.sum(all_x[a], axis=0)
        part_y[a] = mine
        all_y[a, pl.ds(row, 1)] = mine.reshape(1, 1, CX)

        def go(i, c):
            pltpu.make_async_remote_copy(
                src_ref=part_y.at[a], dst_ref=all_y.at[a, row],
                send_sem=ar_send.at[a, 1], recv_sem=ar_recv.at[a, 1],
                device_id=at(i, 0), device_id_type=MESH,
            ).start()
            return c

        lax.fori_loop(1, ny, go, 0)

    def reduce_end(a):
        got = all_y.at[a, pl.ds(0, ny - 1)]
        pltpu.make_async_copy(got, got, ar_recv.at[a, 1]).wait()
        total = jnp.sum(all_y[a], axis=0)
        return [jnp.sum(jnp.where(lane // 32 == i, total, 0.0), axis=1, keepdims=True) for i in range(3)]

    def rows8(value):
        return value[0:8] + value[8:16] + value[16:24] + value[24:32]

    zero8 = jnp.zeros((8, CX), F32)
    main = pl.ds(8, CY)

    waiting = []
    made = halo_send(0, u_ext, own_edge.at[0])
    waiting += made
    halo_wait(0, made, u_ext, ux)

    def keep_residual(p, t, value):
        here = pl.ds(t * 8, 8)
        resid[p, here, :] = value - u_ext[p, pl.ds(8 + t * 8, 8), :]

    blur(u_ext, ux, keep_residual)
    made = spill_send(1, resid)
    waiting += made

    def keep_tv(p, slope):
        tv[p] = slope

    variation(u_ext, ux, own_edge[0], keep_tv)
    spill_wait(1, made)

    def gradient(target):
        def body(p, c):
            target[p, main, :] = (
                spread[p, main, :] + WEIGHT_TV * tv[p] + DAMPING * u_ext[p, main, :]
            )
            return c

        planes(body, 0)

    gradient(g_ext)
    made = halo_send(2, g_ext, own_edge.at[1])
    waiting += made
    halo_wait(2, made, g_ext, gx_halo)

    def advance(step):
        def body(p, c):
            u_ext[p] = u_ext[p] - step * g_ext[p]
            return c

        planes(body, 0)
        ux[...] = ux[...] - step * gx_halo[...]
        own_edge[0] = own_edge[0] - step * own_edge[1]

    def blur_gradient():
        def keep(p, t, value):
            grad[p, pl.ds(t * 8, 8), :] = value

        blur(g_ext, gx_halo, keep)

    def sums_of_gradient():
        def body(p, c):
            g = g_ext[p, main, :]
            h = grad[p]
            return c[0] + rows8(g * g), c[1] + rows8(h * h)

        return planes(body, (zero8, zero8))

    def variation_change():
        def keep(p, slope):
            blur_in[p] = slope

        variation(u_ext, ux, own_edge[0], keep)

        def body(p, c):
            new = blur_in[p]
            c = c + rows8(g_ext[p, main, :] * (new - tv[p]))
            tv[p] = new
            return c

        return planes(body, zero8)

    advance(START_STEP)
    blur_gradient()
    gg, hh = sums_of_gradient()
    gt = variation_change()
    reduce_start(0, (gg, hh, gt))

    def body(p, c):
        resid[p] = resid[p] - START_STEP * grad[p]
        return c

    planes(body, 0)
    made = spill_send(3, resid)
    waiting += made
    reduce_middle(0)
    spill_wait(3, made)
    gradient(g_ext)
    def keep_spread(p, c):
        resid[p] = spread[p, main, :]
        return c

    planes(keep_spread, 0)
    made = halo_send(4, g_ext, own_edge.at[1])
    waiting += made
    halo_wait(4, made, g_ext, gx_halo)
    blur_gradient()
    gg, hh = sums_of_gradient()
    made = spill_send(5, grad)
    waiting += made
    g2, h2, t2 = reduce_end(0)
    change_sq = START_STEP * START_STEP * g2
    change_growth = START_STEP * START_STEP * (h2 + DAMPING * g2) - START_STEP * WEIGHT_TV * t2
    step = change_sq / change_growth

    advance(step)
    gt = variation_change()
    reduce_start(1, (gg, hh, gt))
    spill_wait(5, made)

    def last(p, c):
        pulled = resid[p] - step * spread[p, main, :]
        g_ext[p, main, :] = pulled + WEIGHT_TV * tv[p] + DAMPING * u_ext[p, main, :]
        return c

    reduce_middle(1)
    planes(last, 0)
    g2, h2, t2 = reduce_end(1)
    change_sq = step * step * g2
    change_growth = step * step * (h2 + DAMPING * g2) - step * WEIGHT_TV * t2
    step = change_sq / change_growth

    def finish(p, c):
        out_ref[p] = u_ext[p, main, :] - step * g_ext[p, main, :]
        return c

    planes(finish, 0)

    for c in waiting:
        c.wait_send()
    for a in range(2):
        got = all_x.at[a, pl.ds(0, nx - 1)]
        pltpu.make_async_copy(got, got, ar_send.at[a, 0]).wait()
        got = all_y.at[a, pl.ds(0, ny - 1)]
        pltpu.make_async_copy(got, got, ar_send.at[a, 1]).wait()


def per_device(ny, nx, observed, profiles, tile_index):
    field = pltpu.VMEM((Z, CY, CX), F32)
    extended = pltpu.VMEM((Z, EXT, CX), F32)
    rounds = 6
    scratch = [
        extended, extended, field, field, field,
        pltpu.VMEM((Z, CY + 32, CX), F32), extended, field,
        pltpu.VMEM((Z * CY, 2 * CX), F32), pltpu.VMEM((40, CX), F32),
        pltpu.VMEM((2 * CX, CX), BF16), pltpu.VMEM((2 * CX, CX), BF16),
        pltpu.VMEM((CX, 2 * CX), BF16), pltpu.VMEM((CX, 2 * CX), BF16),
        pltpu.VMEM((Z * CY, 2 * CX), BF16), pltpu.VMEM((Z * CY, 2 * CX), BF16),
        pltpu.VMEM((EXT, CX), F32), pltpu.VMEM((EXT, CX), F32),
        pltpu.VMEM((2, CY, CX), F32), pltpu.VMEM((CY + 32, CX), F32),
        pltpu.VMEM((EXT, CX), F32),
        pltpu.VMEM((rounds, 2, 8, 8, CX), F32), pltpu.VMEM((rounds, 2, 8, 8, CX), F32),
        pltpu.VMEM((rounds, EXT, CX), F32), pltpu.VMEM((rounds, 2, EXT, CX), F32),
        pltpu.VMEM((2, 1, CX), F32), pltpu.VMEM((2, nx, 1, CX), F32),
        pltpu.VMEM((2, 1, CX), F32), pltpu.VMEM((2, ny, 1, CX), F32),
        pltpu.SemaphoreType.DMA,
        pltpu.SemaphoreType.DMA((rounds, 8)), pltpu.SemaphoreType.DMA((rounds, 8)),
        pltpu.SemaphoreType.DMA((2, 2)), pltpu.SemaphoreType.DMA((2, 2)),
    ]
    return pl.pallas_call(
        functools.partial(kernel, ny, nx),
        out_shape=jax.ShapeDtypeStruct((Z, CY, CX), F32),
        in_specs=[
            pl.BlockSpec(memory_space=pl.ANY),
            pl.BlockSpec(memory_space=pltpu.SMEM),
            pl.BlockSpec(memory_space=pltpu.SMEM),
        ],
        out_specs=pl.BlockSpec(memory_space=pltpu.VMEM),
        scratch_shapes=scratch,
        compiler_params=pltpu.CompilerParams(collective_id=0, has_side_effects=True),
    )(observed, jnp.transpose(profiles, (2, 1, 0)), tile_index)


def solution(mesh):
    ny, nx = mesh.shape["gy"], mesh.shape["gx"]
    return jax.shard_map(
        functools.partial(per_device, ny, nx), mesh=mesh,
        in_specs=(P(None, "gy", "gx"), P(), P()),
        out_specs=P(None, "gy", "gx"), check_vma=False,
    )
```

```python
import functools

import jax
import jax.numpy as jnp
from jax import lax
from jax.experimental import pallas as pl
from jax.experimental.pallas import tpu as pltpu
from jax.sharding import PartitionSpec as P

WEIGHT_TV = 0.02
SMOOTHING = 0.1
DAMPING = 0.05
START_STEP = 0.5
RADIUS = 4
TAPS = 9
Z, CY, CX = 16, 32, 128
EXT = CY + 16
MESH = pl.DeviceIdType.MESH
F32 = jnp.float32
BF16 = jnp.bfloat16
SIDES = ((-1, 0), (1, 0), (0, -1), (0, 1), (-1, -1), (-1, 1), (1, -1), (1, 1))


def kernel(
    ny, nx,
    obs_hbm, prof, tiles, out_ref,
    u_ext, g_ext, grad, tv, resid, back, spread, blur_in, blur_y, flux,
    fwd, bwd, bwd_lo, lhs_hi, lhs_lo,
    ux, gx_halo, own_edge, edge_pad,
    send_y, recv_y, send_x, recv_x,
    part, all_x, part_y, all_y,
    load_sem, send_sem, recv_sem, ar_send, ar_recv, known,
):
    row = lax.axis_index("gy")
    col = lax.axis_index("gx")

    def at(dy, dx):
        return {
            "gy": lax.rem(row + dy + ny, ny),
            "gx": lax.rem(col + dx + nx, nx),
        }

    load = pltpu.make_async_copy(obs_hbm, u_ext.at[:, pl.ds(8, CY), :], load_sem)
    load.start()

    barrier = pltpu.get_barrier_semaphore()

    for dy, dx in SIDES:
        pl.semaphore_signal(barrier, inc=1, device_id=at(dy, dx), device_id_type=MESH)

    number = tiles[row, col]
    depth = [prof[a, 0, number] for a in range(TAPS)]
    along = [prof[a, 1, number] for a in range(TAPS)]
    across = [prof[a, 2, number] for a in range(TAPS)]

    lane = lax.broadcasted_iota(jnp.int32, (1, CX), 1)
    sub8 = lax.broadcasted_iota(jnp.int32, (8, CX), 0)
    low_half = sub8 < 4
    plane_of = lane // 8
    place = lane - plane_of * 8
    first_row, last_row = row == 0, row == ny - 1
    first_col, last_col = col == 0, col == nx - 1

    load.wait()

    def halves(value):
        high = value.astype(BF16)
        return high, (value - high.astype(F32)).astype(BF16)

    def prepare():
        mk = lax.broadcasted_iota(jnp.int32, (CX, CX), 0)
        mn = lax.broadcasted_iota(jnp.int32, (CX, CX), 1)

        def band(diff, offset):
            total = jnp.zeros((CX, CX), F32)
            for c in range(TAPS):
                total = jnp.where(diff == c - offset, across[c], total)
            return total

        def wrapped(diff):
            total = jnp.zeros((CX, CX), F32)
            for c in range(TAPS):
                hit = (diff == c - RADIUS - CX) | (diff == c - RADIUS + CX)
                total = jnp.where(hit, across[c], total)
            return total

        ahead = mn - mk
        for part_no, w in enumerate((band(ahead, RADIUS), wrapped(ahead))):
            high, low = halves(w)
            fwd[pl.ds(part_no * CX, CX), pl.ds(0, CX)] = high
            fwd[pl.ds(part_no * CX, CX), pl.ds(CX, CX)] = low
        behind = mk - mn
        for part_no, w in enumerate((band(behind, RADIUS), wrapped(behind))):
            high, low = halves(w)
            bwd[pl.ds(0, CX), pl.ds(part_no * CX, CX)] = high
            bwd[pl.ds(CX, CX), pl.ds(part_no * CX, CX)] = high
            bwd_lo[:, pl.ds(part_no * CX, CX)] = low

        back[:, pl.ds(0, 16), :] = jnp.zeros((Z, 16, CX), F32)
        back[:, pl.ds(16 + CY, 16), :] = jnp.zeros((Z, 16, CX), F32)
        edge_pad[pl.ds(0, 16), :] = jnp.zeros((16, CX), F32)
        edge_pad[pl.ds(16 + CY, 16), :] = jnp.zeros((16, CX), F32)

    def planes(body, init, step=4):
        if step == Z:
            for p in range(Z):
                init = body(p, init)
            return init

        def some(i, carry):
            for k in range(step):
                carry = body(i * step + k, carry)
            return carry

        return lax.fori_loop(0, Z // step, some, init)

    def pack_columns(read):
        def body(p, total):
            turned = pltpu.roll(read(p), 8 * p + 4, 1)
            return jnp.where(plane_of == p, turned, total)

        return planes(body, jnp.zeros((CY, CX), F32), Z)

    def copies(r):
        made = []
        for k, (dy, dx) in enumerate(SIDES):
            if dx == 0:
                src = send_y.at[r, 0 if dy < 0 else 1]
                dst = recv_y.at[r, 1 if dy < 0 else 0]
            else:
                start, size = {-1: (0, 8), 0: (8, CY), 1: (8 + CY, 8)}[dy]
                land = {-1: 8 + CY, 0: 8, 1: 0}[dy]
                src = send_x.at[r, pl.ds(start, size), :]
                dst = recv_x.at[r, 1 if dx < 0 else 0, pl.ds(land, size), :]
            made.append(
                pltpu.make_async_remote_copy(
                    src_ref=src, dst_ref=dst,
                    send_sem=send_sem.at[r, k], recv_sem=recv_sem.at[r, k],
                    device_id=at(dy, dx), device_id_type=MESH,
                )
            )
        return made

    def send(r):
        made = copies(r)
        for k in (4, 5, 6, 7, 2, 3, 0, 1):
            made[k].start()
        return made

    def halo_stage(r, ext, edges_out):
        edge = pack_columns(lambda p: ext[p, pl.ds(8, CY), :])
        edges_out[...] = edge
        send_x[r, pl.ds(8, CY), :] = edge
        send_x[r, pl.ds(0, 8), :] = edge[0:8]
        send_x[r, pl.ds(8 + CY, 8), :] = edge[CY - 8 : CY]
        for q in range(8):
            top, top2 = ext[q, pl.ds(8, 8), :], ext[q + 8, pl.ds(8, 8), :]
            send_y[r, 0, q] = jnp.where(low_half, top, pltpu.roll(top2, 4, 0))
            low, low2 = ext[q, pl.ds(CY, 8), :], ext[q + 8, pl.ds(CY, 8), :]
            send_y[r, 1, q] = jnp.where(low_half, pltpu.roll(low, 4, 0), low2)

    def halo_wait(r, made, ext, halo):
        for c in made:
            c.wait_recv()
        for q in range(8):
            above = jnp.where(first_row, 0.0, recv_y[r, 0, q])
            ext[q, pl.ds(0, 8), :] = pltpu.roll(above, 4, 0)
            ext[q + 8, pl.ds(0, 8), :] = above
            below = jnp.where(last_row, 0.0, recv_y[r, 1, q])
            ext[q, pl.ds(8 + CY, 8), :] = below
            ext[q + 8, pl.ds(8 + CY, 8), :] = pltpu.roll(below, 4, 0)
        halo[...] = sides(r, place < 4)

    def sides(r, from_left):
        left = jnp.where(first_col, 0.0, recv_x[r, 0])
        right = jnp.where(last_col, 0.0, recv_x[r, 1])
        both = jnp.where(from_left, left, right)
        at_row = lax.broadcasted_iota(jnp.int32, (EXT, CX), 0)
        both = jnp.where(first_row & (at_row < 8), 0.0, both)
        return jnp.where(last_row & (at_row >= 8 + CY), 0.0, both)

    def depth_blur(read, write, transposed):
        for t in range(CY // 8):
            value = [read(p, t) for p in range(Z)]
            for p in range(Z):
                total = None
                for a in range(TAPS):
                    source = p - RADIUS + a if transposed else p + RADIUS - a
                    if 0 <= source < Z:
                        term = depth[a] * value[source]
                        total = term if total is None else total + term
                write(p, t, total)

    def blur(ext, halo, write):
        edge = jnp.zeros((CY, CX), F32)
        for b in range(TAPS):
            edge = edge + along[b] * halo[pl.ds(8 + RADIUS - b, CY), :]

        def body(p, c):
            total = along[0] * ext[p, pl.ds(8 + RADIUS, CY), :]
            for b in range(1, TAPS):
                total = total + along[b] * ext[p, pl.ds(8 + RADIUS - b, CY), :]
            here = pl.ds(p * CY if isinstance(p, int) else pl.multiple_of(p * CY, CY), CY)
            high, low = halves(total)
            lhs_hi[here, pl.ds(0, CX)] = high
            lhs_lo[here, pl.ds(0, CX)] = low
            high, low = halves(pltpu.roll(edge, 124 - 8 * p, 1))
            lhs_hi[here, pl.ds(CX, CX)] = high
            lhs_lo[here, pl.ds(CX, CX)] = low
            return c

        planes(body, 0)
        both = jnp.dot(lhs_hi[...], fwd[...], preferred_element_type=F32)
        mixed = jnp.dot(lhs_lo[...], fwd[:, pl.ds(0, CX)], preferred_element_type=F32)
        blur_y[:, pl.ds(0, CX)] = mixed + both[:, 0:CX] + both[:, CX : 2 * CX]
        depth_blur(lambda p, t: blur_y[pl.ds(p * CY + t * 8, 8), pl.ds(0, CX)], write, False)

    def spill_send(r, field):
        def keep(p, t, value):
            high, low = halves(value)
            here = pl.ds(p * CY + t * 8, 8)
            lhs_hi[here, pl.ds(0, CX)] = high
            lhs_hi[here, pl.ds(CX, CX)] = low

        depth_blur(lambda p, t: field[p, pl.ds(t * 8, 8), :], keep, True)
        mixed = jnp.dot(lhs_hi[...], bwd[...], preferred_element_type=F32)
        mixed = mixed + jnp.dot(lhs_hi[:, pl.ds(0, CX)], bwd_lo[...], preferred_element_type=F32)
        blur_y[...] = mixed

        def split(p, total):
            here = pl.ds(p * CY if isinstance(p, int) else pl.multiple_of(p * CY, CY), CY)
            back[p, pl.ds(16, CY), :] = blur_y[here, pl.ds(0, CX)]
            turned = pltpu.roll(blur_y[here, pl.ds(CX, CX)], 8 * p + 4, 1)
            return jnp.where(plane_of == p, turned, total)

        edge_pad[pl.ds(16, CY), :] = planes(split, jnp.zeros((CY, CX), F32), Z)
        edge = along[0] * edge_pad[pl.ds(4, EXT), :]
        for b in range(1, TAPS):
            edge = edge + along[b] * edge_pad[pl.ds(4 + b, EXT), :]
        send_x[r] = edge

        def body(p, c):
            total = along[0] * back[p, pl.ds(4, EXT), :]
            for b in range(1, TAPS):
                total = total + along[b] * back[p, pl.ds(4 + b, EXT), :]
            spread[p] = total
            return c

        planes(body, 0)
        for q in range(8):
            top, top2 = spread[q, pl.ds(0, 8), :], spread[q + 8, pl.ds(0, 8), :]
            send_y[r, 0, q] = jnp.where(low_half, pltpu.roll(top, 4, 0), top2)
            low, low2 = spread[q, pl.ds(8 + CY, 8), :], spread[q + 8, pl.ds(8 + CY, 8), :]
            send_y[r, 1, q] = jnp.where(low_half, low, pltpu.roll(low2, 4, 0))
        return send(r)

    def spill_wait(r, made):
        for c in made:
            c.wait_recv()
        both = sides(r, place >= 4)
        top = both[8:16] + both[0:8]
        low = both[CY : CY + 8] + both[CY + 8 : CY + 16]
        edge = jnp.concatenate([top, both[16:CY], low], axis=0)
        border = (lane < 4) | (lane >= CX - 4)
        for q in range(8):
            above = jnp.where(first_row, 0.0, recv_y[r, 0, q])
            below = jnp.where(last_row, 0.0, recv_y[r, 1, q])
            t, b = pl.ds(8, 8), pl.ds(CY, 8)
            spread[q, t, :] = spread[q, t, :] + jnp.where(low_half, above, 0.0)
            spread[q + 8, t, :] = spread[q + 8, t, :] + jnp.where(low_half, pltpu.roll(above, 4, 0), 0.0)
            spread[q, b, :] = spread[q, b, :] + jnp.where(low_half, 0.0, pltpu.roll(below, 4, 0))
            spread[q + 8, b, :] = spread[q + 8, b, :] + jnp.where(low_half, 0.0, below)

        def body(p, c):
            extra = jnp.where(border, pltpu.roll(edge, 124 - 8 * p, 1), 0.0)
            spread[p, pl.ds(8, CY), :] = spread[p, pl.ds(8, CY), :] + extra
            return c

        planes(body, 0)

    rows40 = lax.broadcasted_iota(jnp.int32, (40, CX), 0)
    rows32 = lax.broadcasted_iota(jnp.int32, (CY, CX), 0)
    no_row_diff = last_row & (rows40 == 39)
    no_row_flux = first_row & (rows40 == 7)
    no_col_diff = last_col & (lane == CX - 1)

    def inverse_size(dx, dy, dz):
        return lax.rsqrt(dx * dx + dy * dy + dz * dz + SMOOTHING * SMOOTHING)

    def variation(ext, halo, edges, write):
        here = halo[pl.ds(8, CY), :]
        dx = pltpu.roll(edges, CX - 1, 1) - here
        dy = halo[pl.ds(9, CY), :] - here
        dy = jnp.where(last_row & (rows32 == CY - 1), 0.0, dy)
        dz = jnp.where(plane_of == Z - 1, 0.0, pltpu.roll(here, CX - 8, 1) - here)
        side = jnp.where(first_col, 0.0, dx * inverse_size(dx, dy, dz))
        around = halo[pl.ds(0, 40), :]

        def body(p, before):
            u = ext[p, pl.ds(0, 40), :]
            dy = jnp.where(no_row_diff, 0.0, ext[p, pl.ds(1, 40), :] - u)
            beyond = pltpu.roll(around, 124 - 8 * p, 1)
            dx = pltpu.roll(jnp.where(lane == 0, beyond, u), CX - 1, 1) - u
            dx = jnp.where(no_col_diff, 0.0, dx)
            after = ext[min(p + 1, Z - 1) if isinstance(p, int) else jnp.minimum(p + 1, Z - 1), pl.ds(0, 40), :]
            dz = after - u
            inverse = inverse_size(dx, dy, dz)
            fy = jnp.where(no_row_flux, 0.0, dy * inverse)
            flux[...] = fy
            fx = (dx * inverse)[8:40]
            fz = (dz * inverse)[8:40]
            fx_side = pltpu.roll(side, 124 - 8 * p, 1)
            fx_before = pltpu.roll(jnp.where(lane == CX - 1, fx_side, fx), 1, 1)
            slope = (before - fz) + (flux[pl.ds(7, CY), :] - fy[8:40]) + (fx_before - fx)
            write(p, slope)
            return fz

        planes(body, jnp.zeros((CY, CX), F32), 4)

    def rows8(value):
        return value[0:8] + value[8:16] + value[16:24] + value[24:32]

    def variation_dot(ext, halo, other, other_halo):
        around, other_around = halo[pl.ds(8, CY), :], other_halo[pl.ds(8, CY), :]
        final_row = last_row & (rows32 == CY - 1)

        def shifted(u, side, p):
            beyond = pltpu.roll(side, 124 - 8 * p, 1)
            return pltpu.roll(jnp.where(lane == 0, beyond, u), CX - 1, 1) - u

        def body(p, total):
            u, g = ext[p, pl.ds(8, CY), :], other[p, pl.ds(8, CY), :]
            after = min(p + 1, Z - 1) if isinstance(p, int) else jnp.minimum(p + 1, Z - 1)
            dz = ext[after, pl.ds(8, CY), :] - u
            ez = other[after, pl.ds(8, CY), :] - g
            dy = jnp.where(final_row, 0.0, ext[p, pl.ds(9, CY), :] - u)
            ey = other[p, pl.ds(9, CY), :] - g
            dx = jnp.where(no_col_diff, 0.0, shifted(u, around, p))
            ex = shifted(g, other_around, p)
            return total + rows8((dx * ex + dy * ey + dz * ez) * inverse_size(dx, dy, dz))

        return planes(body, jnp.zeros((8, CX), F32), 4)

    def fold(values):
        total = jnp.zeros((1, CX), F32)
        for i, value in enumerate(values):
            v = jnp.sum(value, axis=0, keepdims=True)
            v = v + pltpu.roll(v, 64, 1)
            v = v + pltpu.roll(v, 32, 1)
            total = jnp.where(lane // 32 == i, v, total)
        return total

    def far_first_x():
        if nx != 32:
            return [lax.rem(col + i, nx) for i in range(1, nx)]
        x, y, core = col // 8, lax.rem(col // 2, 4), lax.rem(col, 2)
        xs = [lax.rem(x + i, 4) * 8 for i in range(4)]
        ys = [lax.rem(y + i, 4) * 2 for i in range(4)]
        cores = [core, 1 - core]
        ring = (0, 1, 2, 1)
        moves = [(i, j, k) for i in range(4) for j in range(4) for k in range(2)][1:]
        moves.sort(key=lambda m: -(ring[m[0]] + ring[m[1]] + 0.3 * m[2]))
        return [xs[i] + ys[j] + cores[k] for i, j, k in moves]

    def reduce_start(a, values):
        mine = fold(values)
        part[a] = mine
        all_x[a, pl.ds(col, 1)] = mine.reshape(1, 1, CX)

        for peer in far_first_x():
            pltpu.make_async_remote_copy(
                src_ref=part.at[a], dst_ref=all_x.at[a, col],
                send_sem=ar_send.at[a, 0], recv_sem=ar_recv.at[a, 0],
                device_id={"gy": row, "gx": peer}, device_id_type=MESH,
            ).start()

    def reduce_middle(a):
        got = all_x.at[a, pl.ds(0, nx - 1)]
        pltpu.make_async_copy(got, got, ar_recv.at[a, 0]).wait()
        mine = jnp.sum(all_x[a], axis=0)
        part_y[a] = mine
        all_y[a, pl.ds(row, 1)] = mine.reshape(1, 1, CX)

        for i in sorted(range(1, ny), key=lambda i: -min(i, ny - i)):
            pltpu.make_async_remote_copy(
                src_ref=part_y.at[a], dst_ref=all_y.at[a, row],
                send_sem=ar_send.at[a, 1], recv_sem=ar_recv.at[a, 1],
                device_id=at(i, 0), device_id_type=MESH,
            ).start()

    def reduce_end(a):
        got = all_y.at[a, pl.ds(0, ny - 1)]
        pltpu.make_async_copy(got, got, ar_recv.at[a, 1]).wait()
        total = jnp.sum(all_y[a], axis=0)
        return [jnp.sum(jnp.where(lane // 32 == i, total, 0.0), axis=1, keepdims=True) for i in range(3)]

    zero8 = jnp.zeros((8, CX), F32)
    main = pl.ds(8, CY)

    def tell(level, distance):
        for axis, n in enumerate((ny, nx)):
            if n // 2 > distance:
                for d in (-distance, distance):
                    pl.semaphore_signal(
                        known.at[axis, level], inc=1,
                        device_id=at(d, 0) if axis == 0 else at(0, d), device_id_type=MESH,
                    )

    def hear(level, distance):
        for axis, n in enumerate((ny, nx)):
            if n // 2 > distance:
                pl.semaphore_wait(known.at[axis, level], 2)

    def keep_residual(p, t, value):
        here = pl.ds(t * 8, 8)
        resid[p, here, :] = value - u_ext[p, pl.ds(8 + t * 8, 8), :]

    def keep_tv(p, slope):
        tv[p] = slope

    def gradient(target):
        def body(p, c):
            target[p, main, :] = (
                spread[p, main, :] + WEIGHT_TV * tv[p] + DAMPING * u_ext[p, main, :]
            )
            return c

        planes(body, 0)

    def advance(step):
        def body(p, c):
            u_ext[p] = u_ext[p] - step * g_ext[p]
            return c

        planes(body, 0)
        ux[...] = ux[...] - step * gx_halo[...]
        own_edge[0] = own_edge[0] - step * own_edge[1]

    def blur_gradient():
        def keep(p, t, value):
            grad[p, pl.ds(t * 8, 8), :] = value

        blur(g_ext, gx_halo, keep)

    def sums_of_gradient():
        def body(p, c):
            g = g_ext[p, main, :]
            h = grad[p]
            return c[0] + rows8(g * g), c[1] + rows8(h * h), c[2] + rows8(g * tv[p])

        return planes(body, (zero8, zero8, zero8))

    waiting = []
    halo_stage(0, u_ext, own_edge.at[0])
    pl.semaphore_wait(barrier, len(SIDES))
    made = send(0)
    waiting += made
    prepare()
    halo_wait(0, made, u_ext, ux)
    tell(0, 2)
    blur(u_ext, ux, keep_residual)
    made = spill_send(1, resid)
    waiting += made
    variation(u_ext, ux, own_edge[0], keep_tv)
    spill_wait(1, made)
    hear(0, 2)
    tell(1, 4)
    gradient(g_ext)
    halo_stage(2, g_ext, own_edge.at[1])
    made = send(2)
    waiting += made
    halo_wait(2, made, g_ext, gx_halo)
    hear(1, 4)
    tell(2, 8)

    advance(START_STEP)
    blur_gradient()
    gg, hh, gt = sums_of_gradient()
    gt = variation_dot(u_ext, ux, g_ext, gx_halo) - gt
    hear(2, 8)
    reduce_start(0, (gg, hh, gt))

    def body(p, c):
        resid[p] = resid[p] - START_STEP * grad[p]
        return c

    planes(body, 0)
    made = spill_send(3, resid)
    waiting += made
    variation(u_ext, ux, own_edge[0], keep_tv)
    reduce_middle(0)
    spill_wait(3, made)
    gradient(g_ext)
    halo_stage(4, g_ext, own_edge.at[1])
    made = send(4)
    waiting += made

    def keep_spread(p, c):
        resid[p] = spread[p, main, :]
        return c

    planes(keep_spread, 0)
    halo_wait(4, made, g_ext, gx_halo)
    blur_gradient()
    gg, hh, gt = sums_of_gradient()
    g2, h2, t2 = reduce_end(0)
    change_sq = START_STEP * START_STEP * g2
    change_growth = START_STEP * START_STEP * (h2 + DAMPING * g2) - START_STEP * WEIGHT_TV * t2
    step = change_sq / change_growth

    advance(step)
    gt = variation_dot(u_ext, ux, g_ext, gx_halo) - gt
    reduce_start(1, (gg, hh, gt))

    made = spill_send(5, grad)
    waiting += made
    variation(u_ext, ux, own_edge[0], keep_tv)
    reduce_middle(1)
    spill_wait(5, made)

    def last(p, c):
        pulled = resid[p] - step * spread[p, main, :]
        g_ext[p, main, :] = pulled + WEIGHT_TV * tv[p] + DAMPING * u_ext[p, main, :]
        return c

    planes(last, 0)
    g2, h2, t2 = reduce_end(1)
    change_sq = step * step * g2
    change_growth = step * step * (h2 + DAMPING * g2) - step * WEIGHT_TV * t2
    step = change_sq / change_growth

    def finish(p, c):
        out_ref[p] = u_ext[p, main, :] - step * g_ext[p, main, :]
        return c

    planes(finish, 0)

    for c in waiting:
        c.wait_send()
    for a in range(2):
        got = all_x.at[a, pl.ds(0, nx - 1)]
        pltpu.make_async_copy(got, got, ar_send.at[a, 0]).wait()
        got = all_y.at[a, pl.ds(0, ny - 1)]
        pltpu.make_async_copy(got, got, ar_send.at[a, 1]).wait()


def per_device(ny, nx, observed, profiles, tile_index):
    field = pltpu.VMEM((Z, CY, CX), F32)
    extended = pltpu.VMEM((Z, EXT, CX), F32)
    rounds = 6
    scratch = [
        extended, extended, field, field, field,
        pltpu.VMEM((Z, CY + 32, CX), F32), extended, field,
        pltpu.VMEM((Z * CY, 2 * CX), F32), pltpu.VMEM((40, CX), F32),
        pltpu.VMEM((2 * CX, 2 * CX), BF16), pltpu.VMEM((2 * CX, 2 * CX), BF16),
        pltpu.VMEM((CX, 2 * CX), BF16),
        pltpu.VMEM((Z * CY, 2 * CX), BF16), pltpu.VMEM((Z * CY, 2 * CX), BF16),
        pltpu.VMEM((EXT, CX), F32), pltpu.VMEM((EXT, CX), F32),
        pltpu.VMEM((2, CY, CX), F32), pltpu.VMEM((CY + 32, CX), F32),
        pltpu.VMEM((rounds, 2, 8, 8, CX), F32), pltpu.VMEM((rounds, 2, 8, 8, CX), F32),
        pltpu.VMEM((rounds, EXT, CX), F32), pltpu.VMEM((rounds, 2, EXT, CX), F32),
        pltpu.VMEM((2, 1, CX), F32), pltpu.VMEM((2, nx, 1, CX), F32),
        pltpu.VMEM((2, 1, CX), F32), pltpu.VMEM((2, ny, 1, CX), F32),
        pltpu.SemaphoreType.DMA,
        pltpu.SemaphoreType.DMA((rounds, 8)), pltpu.SemaphoreType.DMA((rounds, 8)),
        pltpu.SemaphoreType.DMA((2, 2)), pltpu.SemaphoreType.DMA((2, 2)),
        pltpu.SemaphoreType.REGULAR((2, 3)),
    ]
    return pl.pallas_call(
        functools.partial(kernel, ny, nx),
        out_shape=jax.ShapeDtypeStruct((Z, CY, CX), F32),
        in_specs=[
            pl.BlockSpec(memory_space=pl.ANY),
            pl.BlockSpec(memory_space=pltpu.SMEM),
            pl.BlockSpec(memory_space=pltpu.SMEM),
        ],
        out_specs=pl.BlockSpec(memory_space=pltpu.VMEM),
        scratch_shapes=scratch,
        compiler_params=pltpu.CompilerParams(collective_id=0, has_side_effects=True),
    )(observed, jnp.transpose(profiles, (2, 1, 0)), tile_index)


def solution(mesh):
    ny, nx = mesh.shape["gy"], mesh.shape["gx"]
    return jax.shard_map(
        functools.partial(per_device, ny, nx), mesh=mesh,
        in_specs=(P(None, "gy", "gx"), P(), P()),
        out_specs=P(None, "gy", "gx"), check_vma=False,
    )
```

```python
import functools

import jax
import jax.numpy as jnp
from jax import lax
from jax.experimental import pallas as pl
from jax.experimental.pallas import tpu as pltpu
from jax.sharding import PartitionSpec as P

WEIGHT_TV = 0.02
SMOOTHING = 0.1
DAMPING = 0.05
START_STEP = 0.5
RADIUS = 4
TAPS = 9
Z, CY, CX = 16, 32, 128
EXT = CY + 16
MESH = pl.DeviceIdType.MESH
F32 = jnp.float32
BF16 = jnp.bfloat16
SIDES = ((-1, 0), (1, 0), (0, -1), (0, 1), (-1, -1), (-1, 1), (1, -1), (1, 1))


def kernel(
    ny, nx,
    obs_hbm, prof, tiles, out_ref,
    u_ext, g_ext, grad, tv, resid, back, spread, blur_y, flux,
    fwd, bwd, side_fwd, side_bwd, twice, y_fix, x_fix,
    ux, gx_halo, own_edge, edge_pad,
    send_y, recv_y, send_x, recv_x,
    part, all_x, part_y, all_y,
    load_sem, send_sem, recv_sem, ar_send, ar_recv, known,
):
    row = lax.axis_index("gy")
    col = lax.axis_index("gx")

    def at(dy, dx):
        return {
            "gy": lax.rem(row + dy + ny, ny),
            "gx": lax.rem(col + dx + nx, nx),
        }

    load = pltpu.make_async_copy(obs_hbm, u_ext.at[:, pl.ds(8, CY), :], load_sem)
    load.start()

    barrier = pltpu.get_barrier_semaphore()

    for dy, dx in SIDES:
        pl.semaphore_signal(barrier, inc=1, device_id=at(dy, dx), device_id_type=MESH)

    number = tiles[row, col]
    depth = [prof[a, 0, number] for a in range(TAPS)]
    along = [prof[a, 1, number] for a in range(TAPS)]
    across = [prof[a, 2, number] for a in range(TAPS)]

    lane = lax.broadcasted_iota(jnp.int32, (1, CX), 1)
    sub8 = lax.broadcasted_iota(jnp.int32, (8, CX), 0)
    low_half = sub8 < 4
    plane_of = lane // 8
    place = lane - plane_of * 8
    first_row, last_row = row == 0, row == ny - 1
    first_col, last_col = col == 0, col == nx - 1

    back[:, pl.ds(0, 16), :] = jnp.zeros((Z, 16, CX), F32)
    back[:, pl.ds(16 + CY, 16), :] = jnp.zeros((Z, 16, CX), F32)
    edge_pad[pl.ds(0, 16), :] = jnp.zeros((16, CX), F32)
    edge_pad[pl.ds(16 + CY, 16), :] = jnp.zeros((16, CX), F32)
    load.wait()

    def halves(value):
        high = value.astype(BF16)
        return high, (value - high.astype(F32)).astype(BF16)

    def prepare():
        mk = lax.broadcasted_iota(jnp.int32, (CX, CX), 0)
        mn = lax.broadcasted_iota(jnp.int32, (CX, CX), 1)

        def band(diff, taps, keep=None):
            total = jnp.zeros((CX, CX), F32)
            for c in range(TAPS):
                total = jnp.where(diff == c - RADIUS, taps[c], total)
            return total if keep is None else jnp.where(keep, total, 0.0)

        ahead = mn - mk
        planes_ahead = mn // 8 - mk // 8
        places_ahead = ahead - 8 * planes_ahead
        crossing = (mn // 4 + mk // 4) % 2 == 1
        for ref, sign in ((fwd, 1), (bwd, -1)):
            split_matrix(ref, band(sign * ahead, across))
        for ref, sign in ((side_fwd, 1), (side_bwd, -1)):
            split_matrix(
                ref, band(sign * planes_ahead, depth) * band(sign * places_ahead, across, crossing)
            )

    def split_matrix(ref, w):
        high, low = halves(w)
        ref[pl.ds(0, CX), pl.ds(0, CX)] = high
        ref[pl.ds(CX, CX), pl.ds(0, CX)] = high
        ref[pl.ds(0, CX), pl.ds(CX, CX)] = low
        ref[pl.ds(CX, CX), pl.ds(CX, CX)] = jnp.zeros((CX, CX), BF16)

    def times(value, ref):
        high, low = halves(value)
        both = jnp.dot(jnp.concatenate([high, low], axis=1), ref[...], preferred_element_type=F32)
        return both[:, 0:CX] + both[:, CX : 2 * CX]

    def planes(body, init, step=4):
        if step == Z:
            for p in range(Z):
                init = body(p, init)
            return init

        def some(i, carry):
            for k in range(step):
                carry = body(i * step + k, carry)
            return carry

        return lax.fori_loop(0, Z // step, some, init)

    def pack_columns(read):
        def body(p, total):
            turned = pltpu.roll(read(p), 8 * p + 4, 1)
            return jnp.where(plane_of == p, turned, total)

        return planes(body, jnp.zeros((CY, CX), F32), Z)

    def copies(r):
        made = []
        for k, (dy, dx) in enumerate(SIDES):
            if dx == 0:
                src = send_y.at[r, 0 if dy < 0 else 1]
                dst = recv_y.at[r, 1 if dy < 0 else 0]
            else:
                start, size = {-1: (0, 8), 0: (8, CY), 1: (8 + CY, 8)}[dy]
                land = {-1: 8 + CY, 0: 8, 1: 0}[dy]
                src = send_x.at[r, pl.ds(start, size), :]
                dst = recv_x.at[r, 1 if dx < 0 else 0, pl.ds(land, size), :]
            made.append(
                pltpu.make_async_remote_copy(
                    src_ref=src, dst_ref=dst,
                    send_sem=send_sem.at[r, k], recv_sem=recv_sem.at[r, k],
                    device_id=at(dy, dx), device_id_type=MESH,
                )
            )
        return made

    def send(r):
        made = copies(r)
        for k in (4, 5, 6, 7, 2, 3, 0, 1):
            made[k].start()
        return made

    border = (lane < 4) | (lane >= CX - 4)

    def mixing(taps):
        limits = {1: (sub8 <= 0, 5), 2: (sub8 <= 1, 6), 3: (sub8 <= 2, 7), 5: (sub8 >= 5, 1), 6: (sub8 >= 6, 2), 7: (sub8 >= 7, 3)}
        weights = {s: jnp.where(mask, taps[b], 0.0) for s, (mask, b) in limits.items()}
        weights[4] = jnp.where(low_half, taps[8], taps[0])
        return weights

    def put_rows(rows, first, second):
        for q in range(8):
            a, b = rows[q], pltpu.roll(rows[q + 8], 4, 0)
            first[q] = jnp.where(low_half, a, b)
            second[q] = jnp.where(low_half, b, a)

    def get_rows(first, second, no_first, no_second):
        near, far = [], []
        for q in range(8):
            a = jnp.where(no_first, 0.0, first[q])
            b = jnp.where(no_second, 0.0, second[q])
            near.append(jnp.where(low_half, a, b))
            far.append(pltpu.roll(jnp.where(low_half, b, a), 4, 0))
        return near + far

    def cross(rows, taps, transposed, ref):
        for p in range(Z):
            twice[p, pl.ds(0, 8), :] = rows[p]
            twice[p, pl.ds(8, 8), :] = rows[p]
        weights = mixing(taps)
        mixed = []
        for p in range(Z):
            total = weights[4] * twice[p, pl.ds(4, 8), :]
            for s in (1, 2, 3, 5, 6, 7):
                total = total + weights[s] * twice[p, pl.ds(8 - s, 8), :]
            mixed.append(total)
        return times(jnp.concatenate(depth_sum(mixed, transposed), axis=0), ref)

    def edge_rows(read):
        return [jnp.where(low_half, read(p, 0), read(p, CY - 8)) for p in range(Z)]

    def halo_send(r, rows, edge):
        put_rows(rows, send_y.at[r, 0], send_y.at[r, 1])
        send_x[r, pl.ds(8, CY), :] = edge
        send_x[r, pl.ds(0, 8), :] = edge[0:8]
        send_x[r, pl.ds(8 + CY, 8), :] = edge[CY - 8 : CY]
        return send(r)

    def halo_fix(r, made, ext, halo):
        for c in made:
            c.wait_recv()
        rows = get_rows(recv_y.at[r, 1], recv_y.at[r, 0], last_row, first_row)
        for p in range(Z):
            ext[p, pl.ds(0, 8), :] = rows[p]
            ext[p, pl.ds(8 + CY, 8), :] = rows[p]
        halo[...] = sides(r, place < 4)
        edge = along[0] * halo[pl.ds(8 + RADIUS, CY), :]
        for b in range(1, TAPS):
            edge = edge + along[b] * halo[pl.ds(8 + RADIUS - b, CY), :]
        x_fix[...] = times(edge, side_fwd)
        y_fix[...] = cross(rows, along, False, fwd)

    def spill_send(r, rows, edge):
        edge_pad[pl.ds(16, CY), :] = times(edge, side_bwd)
        spilled = cross(rows, along[::-1], True, bwd)
        put_rows([spilled[8 * p : 8 * p + 8] for p in range(Z)], send_y.at[r, 1], send_y.at[r, 0])
        total = along[0] * edge_pad[pl.ds(4, EXT), :]
        for b in range(1, TAPS):
            total = total + along[b] * edge_pad[pl.ds(4 + b, EXT), :]
        send_x[r] = total
        return send(r)

    def spill_fix(r, made):
        for c in made:
            c.wait_recv()
        rows = get_rows(recv_y.at[r, 0], recv_y.at[r, 1], first_row, last_row)
        y_fix[...] = jnp.concatenate(rows, axis=0)
        both = sides(r, place >= 4)
        x_fix[pl.ds(0, 8), :] = both[8:16] + both[0:8]
        x_fix[pl.ds(8, 16), :] = both[16:CY]
        x_fix[pl.ds(24, 8), :] = both[CY : CY + 8] + both[CY + 8 : CY + 16]

    def fixed_edges(read, edge):
        extra = x_fix[...]
        ends = jnp.where(low_half, extra[0:8], extra[CY - 8 : CY])
        rows, packed = edge_rows(read), jnp.zeros((8, CX), F32)
        for p in range(Z):
            y = y_fix[pl.ds(8 * p, 8), :]
            packed = jnp.where(plane_of == p, pltpu.roll(y, 8 * p + 4, 1), packed)
            rows[p] = rows[p] + y + jnp.where(border, pltpu.roll(ends, 124 - 8 * p, 1), 0.0)
        edge = edge + extra
        top = edge[0:8] + jnp.where(low_half, packed, 0.0)
        low = edge[CY - 8 : CY] + jnp.where(low_half, 0.0, packed)
        return rows, jnp.concatenate([top, edge[8 : CY - 8], low], axis=0)

    def with_fix(add):
        extra = x_fix[...]
        for p in range(Z):
            e = jnp.where(border, pltpu.roll(extra, 124 - 8 * p, 1), 0.0)
            y = y_fix[pl.ds(8 * p, 8), :]
            top = e[0:8] + jnp.where(low_half, y, 0.0)
            low = e[CY - 8 : CY] + jnp.where(low_half, 0.0, y)
            add(p, jnp.concatenate([top, e[8 : CY - 8], low], axis=0))

    def sides(r, from_left):
        left = jnp.where(first_col, 0.0, recv_x[r, 0])
        right = jnp.where(last_col, 0.0, recv_x[r, 1])
        both = jnp.where(from_left, left, right)
        at_row = lax.broadcasted_iota(jnp.int32, (EXT, CX), 0)
        both = jnp.where(first_row & (at_row < 8), 0.0, both)
        return jnp.where(last_row & (at_row >= 8 + CY), 0.0, both)

    def depth_sum(value, transposed):
        out = []
        for p in range(Z):
            total = None
            for a in range(TAPS):
                source = p - RADIUS + a if transposed else p + RADIUS - a
                if 0 <= source < Z:
                    term = depth[a] * value[source]
                    total = term if total is None else total + term
            out.append(total)
        return out

    def clear_border(ext):
        for p in range(Z):
            ext[p, pl.ds(0, 8), :] = jnp.zeros((8, CX), F32)
            ext[p, pl.ds(8 + CY, 8), :] = jnp.zeros((8, CX), F32)

    def blur_inside(ext, write):
        for group in range(4):
            rows = []
            for p in range(4 * group, 4 * group + 4):
                total = along[0] * ext[p, pl.ds(8 + RADIUS, CY), :]
                for b in range(1, TAPS):
                    total = total + along[b] * ext[p, pl.ds(8 + RADIUS - b, CY), :]
                rows.append(total)
            blur_y[pl.ds(group * 128, 128), :] = times(jnp.concatenate(rows, axis=0), fwd)
        for t in range(CY // 8):
            value = [blur_y[pl.ds(p * CY + t * 8, 8), :] for p in range(Z)]
            for p, total in enumerate(depth_sum(value, False)):
                write(p, t, total)

    def spread_inside(field, write):
        for t in range(CY // 8):
            value = [field[p, pl.ds(t * 8, 8), :] for p in range(Z)]
            out = times(jnp.concatenate(depth_sum(value, True), axis=0), bwd)
            for p in range(Z):
                back[p, pl.ds(16 + t * 8, 8), :] = out[8 * p : 8 * p + 8]

        for p in range(Z):
            total = along[0] * back[p, pl.ds(12, CY), :]
            for b in range(1, TAPS):
                total = total + along[b] * back[p, pl.ds(12 + b, CY), :]
            write(p, total)

    rows40 = lax.broadcasted_iota(jnp.int32, (40, CX), 0)
    rows32 = lax.broadcasted_iota(jnp.int32, (CY, CX), 0)
    no_row_diff = last_row & (rows40 == 39)
    no_row_flux = first_row & (rows40 == 7)
    no_col_diff = last_col & (lane == CX - 1)

    def inverse_size(dx, dy, dz):
        return lax.rsqrt(dx * dx + dy * dy + dz * dz + SMOOTHING * SMOOTHING)

    def variation(ext, halo, edges, write):
        here = halo[pl.ds(8, CY), :]
        dx = pltpu.roll(edges, CX - 1, 1) - here
        dy = halo[pl.ds(9, CY), :] - here
        dy = jnp.where(last_row & (rows32 == CY - 1), 0.0, dy)
        dz = jnp.where(plane_of == Z - 1, 0.0, pltpu.roll(here, CX - 8, 1) - here)
        side = jnp.where(first_col, 0.0, dx * inverse_size(dx, dy, dz))
        around = halo[pl.ds(0, 40), :]

        def body(p, before):
            u = ext[p, pl.ds(0, 40), :]
            dy = jnp.where(no_row_diff, 0.0, ext[p, pl.ds(1, 40), :] - u)
            beyond = pltpu.roll(around, 124 - 8 * p, 1)
            dx = pltpu.roll(jnp.where(lane == 0, beyond, u), CX - 1, 1) - u
            dx = jnp.where(no_col_diff, 0.0, dx)
            after = ext[min(p + 1, Z - 1) if isinstance(p, int) else jnp.minimum(p + 1, Z - 1), pl.ds(0, 40), :]
            dz = after - u
            inverse = inverse_size(dx, dy, dz)
            fy = jnp.where(no_row_flux, 0.0, dy * inverse)
            flux[...] = fy
            fx = (dx * inverse)[8:40]
            fz = (dz * inverse)[8:40]
            fx_side = pltpu.roll(side, 124 - 8 * p, 1)
            fx_before = pltpu.roll(jnp.where(lane == CX - 1, fx_side, fx), 1, 1)
            slope = (before - fz) + (flux[pl.ds(7, CY), :] - fy[8:40]) + (fx_before - fx)
            write(p, slope)
            return fz

        planes(body, jnp.zeros((CY, CX), F32), 4)

    def rows8(value):
        return value[0:8] + value[8:16] + value[16:24] + value[24:32]

    def variation_dot(ext, halo, other, other_halo):
        around, other_around = halo[pl.ds(8, CY), :], other_halo[pl.ds(8, CY), :]
        final_row = last_row & (rows32 == CY - 1)

        def shifted(u, side, p):
            beyond = pltpu.roll(side, 124 - 8 * p, 1)
            return pltpu.roll(jnp.where(lane == 0, beyond, u), CX - 1, 1) - u

        def body(p, total):
            u, g = ext[p, pl.ds(8, CY), :], other[p, pl.ds(8, CY), :]
            after = min(p + 1, Z - 1) if isinstance(p, int) else jnp.minimum(p + 1, Z - 1)
            dz = ext[after, pl.ds(8, CY), :] - u
            ez = other[after, pl.ds(8, CY), :] - g
            dy = jnp.where(final_row, 0.0, ext[p, pl.ds(9, CY), :] - u)
            ey = other[p, pl.ds(9, CY), :] - g
            dx = jnp.where(no_col_diff, 0.0, shifted(u, around, p))
            ex = shifted(g, other_around, p)
            return total + rows8((dx * ex + dy * ey + dz * ez) * inverse_size(dx, dy, dz))

        return planes(body, jnp.zeros((8, CX), F32), 4)

    def fold(values):
        total = jnp.zeros((1, CX), F32)
        for i, value in enumerate(values):
            v = jnp.sum(value, axis=0, keepdims=True)
            v = v + pltpu.roll(v, 64, 1)
            v = v + pltpu.roll(v, 32, 1)
            total = jnp.where(lane // 32 == i, v, total)
        return total

    def far_first_x():
        if nx != 32:
            return [lax.rem(col + i, nx) for i in range(1, nx)]
        x, y, core = col // 8, lax.rem(col // 2, 4), lax.rem(col, 2)
        xs = [lax.rem(x + i, 4) * 8 for i in range(4)]
        ys = [lax.rem(y + i, 4) * 2 for i in range(4)]
        cores = [core, 1 - core]
        ring = (0, 1, 2, 1)
        moves = [(i, j, k) for i in range(4) for j in range(4) for k in range(2)][1:]
        moves.sort(key=lambda m: -(ring[m[0]] + ring[m[1]] + 0.3 * m[2]))
        return [xs[i] + ys[j] + cores[k] for i, j, k in moves]

    def reduce_start(a, values):
        mine = fold(values)
        part[a] = mine
        all_x[a, pl.ds(col, 1)] = mine.reshape(1, 1, CX)

        for peer in far_first_x():
            pltpu.make_async_remote_copy(
                src_ref=part.at[a], dst_ref=all_x.at[a, col],
                send_sem=ar_send.at[a, 0], recv_sem=ar_recv.at[a, 0],
                device_id={"gy": row, "gx": peer}, device_id_type=MESH,
            ).start()

    def reduce_middle(a):
        got = all_x.at[a, pl.ds(0, nx - 1)]
        pltpu.make_async_copy(got, got, ar_recv.at[a, 0]).wait()
        mine = jnp.sum(all_x[a], axis=0)
        part_y[a] = mine
        all_y[a, pl.ds(row, 1)] = mine.reshape(1, 1, CX)

        for i in sorted(range(1, ny), key=lambda i: -min(i, ny - i)):
            pltpu.make_async_remote_copy(
                src_ref=part_y.at[a], dst_ref=all_y.at[a, row],
                send_sem=ar_send.at[a, 1], recv_sem=ar_recv.at[a, 1],
                device_id=at(i, 0), device_id_type=MESH,
            ).start()

    def reduce_end(a):
        got = all_y.at[a, pl.ds(0, ny - 1)]
        pltpu.make_async_copy(got, got, ar_recv.at[a, 1]).wait()
        total = jnp.sum(all_y[a], axis=0)
        return [jnp.sum(jnp.where(lane // 32 == i, total, 0.0), axis=1, keepdims=True) for i in range(3)]

    zero8 = jnp.zeros((8, CX), F32)
    main = pl.ds(8, CY)

    def tell(level, distance):
        for axis, n in enumerate((ny, nx)):
            if n // 2 > distance:
                for d in (-distance, distance):
                    pl.semaphore_signal(
                        known.at[axis, level], inc=1,
                        device_id=at(d, 0) if axis == 0 else at(0, d), device_id_type=MESH,
                    )

    def hear(level, distance):
        for axis, n in enumerate((ny, nx)):
            if n // 2 > distance:
                pl.semaphore_wait(known.at[axis, level], 2)

    def keep_tv(p, slope):
        tv[p] = slope

    def advance(step):
        def body(p, c):
            u_ext[p] = u_ext[p] - step * g_ext[p]
            return c

        planes(body, 0)
        ux[...] = ux[...] - step * gx_halo[...]
        own_edge[0] = own_edge[0] - step * own_edge[1]

    def read_main(ext):
        return lambda p, start: ext[p, pl.ds(8 + start, 8), :]

    def read_field(field):
        return lambda p, start: field[p, pl.ds(start, 8), :]

    def packed_main(ext):
        return pack_columns(lambda p: ext[p, main, :])

    def add_main(p, extra):
        g_ext[p, main, :] = g_ext[p, main, :] + extra

    def add_grad(p, extra):
        grad[p] = grad[p] + extra

    def add_resid(p, extra):
        resid[p] = resid[p] + extra

    def keep_grad(p, t, value):
        grad[p, pl.ds(t * 8, 8), :] = value

    def keep_spread(p, value):
        spread[p] = value

    def gradient_inside():
        def body(p, c):
            g_ext[p, main, :] = spread[p] + WEIGHT_TV * tv[p] + DAMPING * u_ext[p, main, :]
            return c

        planes(body, 0)

    def send_gradient(r, edge):
        rows, edge = fixed_edges(read_main(g_ext), edge)
        own_edge[1] = edge
        return halo_send(r, rows, edge)

    def spread_and_slope(field):
        spread_inside(field, keep_spread)
        variation(u_ext, ux, own_edge[0], keep_tv)

    def sums_of_gradient():
        def body(p, c):
            g = g_ext[p, main, :]
            h = grad[p]
            return c[0] + rows8(g * g), c[1] + rows8(h * h), c[2] + rows8(g * tv[p])

        return planes(body, (zero8, zero8, zero8))

    waiting = []
    clear_border(u_ext)
    edge = packed_main(u_ext)
    own_edge[0] = edge
    rows = edge_rows(read_main(u_ext))
    pl.semaphore_wait(barrier, len(SIDES))
    made = halo_send(0, rows, edge)
    waiting += made
    prepare()

    def keep_residual(p, t, value):
        resid[p, pl.ds(t * 8, 8), :] = value - u_ext[p, pl.ds(8 + t * 8, 8), :]

    blur_inside(u_ext, keep_residual)
    edge = pack_columns(lambda p: resid[p])
    halo_fix(0, made, u_ext, ux)
    rows, edge = fixed_edges(read_field(resid), edge)
    made = spill_send(1, rows, edge)
    waiting += made
    tell(0, 2)
    with_fix(add_resid)
    spread_and_slope(resid)
    gradient_inside()
    edge = packed_main(g_ext)
    spill_fix(1, made)
    made = send_gradient(2, edge)
    waiting += made
    hear(0, 2)
    tell(1, 4)
    with_fix(add_main)
    clear_border(g_ext)
    blur_inside(g_ext, keep_grad)
    halo_fix(2, made, g_ext, gx_halo)
    hear(1, 4)
    tell(2, 8)
    with_fix(add_grad)

    advance(START_STEP)
    gg, hh, gt = sums_of_gradient()
    gt = variation_dot(u_ext, ux, g_ext, gx_halo) - gt
    hear(2, 8)
    reduce_start(0, (gg, hh, gt))

    def next_residual(p, c):
        resid[p] = resid[p] - START_STEP * grad[p]
        return c

    planes(next_residual, 0)
    made = spill_send(3, edge_rows(read_field(resid)), pack_columns(lambda p: resid[p]))
    waiting += made
    spread_and_slope(resid)
    gradient_inside()
    edge = packed_main(g_ext)
    spill_fix(3, made)
    made = send_gradient(4, edge)
    waiting += made
    reduce_middle(0)

    def keep_pulled(p, extra):
        add_main(p, extra)
        resid[p] = spread[p] + extra

    with_fix(keep_pulled)
    clear_border(g_ext)
    blur_inside(g_ext, keep_grad)
    halo_fix(4, made, g_ext, gx_halo)
    with_fix(add_grad)
    gg, hh, gt = sums_of_gradient()
    g2, h2, t2 = reduce_end(0)
    change_sq = START_STEP * START_STEP * g2
    change_growth = START_STEP * START_STEP * (h2 + DAMPING * g2) - START_STEP * WEIGHT_TV * t2
    step = change_sq / change_growth

    advance(step)
    gt = variation_dot(u_ext, ux, g_ext, gx_halo) - gt
    reduce_start(1, (gg, hh, gt))

    made = spill_send(5, edge_rows(read_field(grad)), pack_columns(lambda p: grad[p]))
    waiting += made
    spread_and_slope(grad)
    spill_fix(5, made)
    reduce_middle(1)

    def last(p, extra):
        pulled = resid[p] - step * (spread[p] + extra)
        g_ext[p, main, :] = pulled + WEIGHT_TV * tv[p] + DAMPING * u_ext[p, main, :]

    with_fix(last)
    g2, h2, t2 = reduce_end(1)
    change_sq = step * step * g2
    change_growth = step * step * (h2 + DAMPING * g2) - step * WEIGHT_TV * t2
    step = change_sq / change_growth

    def finish(p, c):
        out_ref[p] = u_ext[p, main, :] - step * g_ext[p, main, :]
        return c

    planes(finish, 0)

    for c in waiting:
        c.wait_send()
    for a in range(2):
        got = all_x.at[a, pl.ds(0, nx - 1)]
        pltpu.make_async_copy(got, got, ar_send.at[a, 0]).wait()
        got = all_y.at[a, pl.ds(0, ny - 1)]
        pltpu.make_async_copy(got, got, ar_send.at[a, 1]).wait()


def per_device(ny, nx, observed, profiles, tile_index):
    field = pltpu.VMEM((Z, CY, CX), F32)
    extended = pltpu.VMEM((Z, EXT, CX), F32)
    matrix = pltpu.VMEM((2 * CX, 2 * CX), BF16)
    rounds = 6
    scratch = [
        extended, extended, field, field, field,
        pltpu.VMEM((Z, CY + 32, CX), F32), field,
        pltpu.VMEM((Z * CY, CX), F32), pltpu.VMEM((40, CX), F32),
        matrix, matrix, matrix, matrix,
        pltpu.VMEM((Z, 16, CX), F32), pltpu.VMEM((Z * 8, CX), F32), pltpu.VMEM((CY, CX), F32),
        pltpu.VMEM((EXT, CX), F32), pltpu.VMEM((EXT, CX), F32),
        pltpu.VMEM((2, CY, CX), F32), pltpu.VMEM((CY + 32, CX), F32),
        pltpu.VMEM((rounds, 2, 8, 8, CX), F32), pltpu.VMEM((rounds, 2, 8, 8, CX), F32),
        pltpu.VMEM((rounds, EXT, CX), F32), pltpu.VMEM((rounds, 2, EXT, CX), F32),
        pltpu.VMEM((2, 1, CX), F32), pltpu.VMEM((2, nx, 1, CX), F32),
        pltpu.VMEM((2, 1, CX), F32), pltpu.VMEM((2, ny, 1, CX), F32),
        pltpu.SemaphoreType.DMA,
        pltpu.SemaphoreType.DMA((rounds, 8)), pltpu.SemaphoreType.DMA((rounds, 8)),
        pltpu.SemaphoreType.DMA((2, 2)), pltpu.SemaphoreType.DMA((2, 2)),
        pltpu.SemaphoreType.REGULAR((2, 3)),
    ]
    return pl.pallas_call(
        functools.partial(kernel, ny, nx),
        out_shape=jax.ShapeDtypeStruct((Z, CY, CX), F32),
        in_specs=[
            pl.BlockSpec(memory_space=pl.ANY),
            pl.BlockSpec(memory_space=pltpu.SMEM),
            pl.BlockSpec(memory_space=pltpu.SMEM),
        ],
        out_specs=pl.BlockSpec(memory_space=pltpu.VMEM),
        scratch_shapes=scratch,
        compiler_params=pltpu.CompilerParams(collective_id=0, has_side_effects=True),
    )(observed, jnp.transpose(profiles, (2, 1, 0)), tile_index)


def solution(mesh):
    ny, nx = mesh.shape["gy"], mesh.shape["gx"]
    return jax.shard_map(
        functools.partial(per_device, ny, nx), mesh=mesh,
        in_specs=(P(None, "gy", "gx"), P(), P()),
        out_specs=P(None, "gy", "gx"), check_vma=False,
    )
```

```python
import functools

import jax
import jax.numpy as jnp
from jax import lax
from jax.experimental import pallas as pl
from jax.experimental.pallas import tpu as pltpu
from jax.sharding import PartitionSpec as P

WEIGHT_TV = 0.02
SMOOTHING = 0.1
DAMPING = 0.05
START_STEP = 0.5
RADIUS = 4
TAPS = 9
Z, CY, CX = 16, 32, 128
EXT = CY + 16
MESH = pl.DeviceIdType.MESH
F32 = jnp.float32
BF16 = jnp.bfloat16
SIDES = ((-1, 0), (1, 0), (0, -1), (0, 1), (-1, -1), (-1, 1), (1, -1), (1, 1))


def kernel(
    ny, nx,
    obs_hbm, prof, tiles, out_ref,
    u_ext, g_ext, grad, tv, resid, back, spread, blur_y, flux,
    fwd, bwd, side_fwd, side_bwd, twice, y_fix, x_fix,
    across_u, square, product, growth,
    ux, gx_halo, own_edge, edge_pad,
    send_y, recv_y, send_x, recv_x,
    part, all_x, part_y, all_y,
    load_sem, send_sem, recv_sem, ar_send, ar_recv, known,
):
    row = lax.axis_index("gy")
    col = lax.axis_index("gx")

    def at(dy, dx):
        return {
            "gy": lax.rem(row + dy + ny, ny),
            "gx": lax.rem(col + dx + nx, nx),
        }

    load = pltpu.make_async_copy(obs_hbm, u_ext.at[:, pl.ds(8, CY), :], load_sem)
    load.start()

    barrier = pltpu.get_barrier_semaphore()

    for dy, dx in SIDES:
        pl.semaphore_signal(barrier, inc=1, device_id=at(dy, dx), device_id_type=MESH)

    number = tiles[row, col]
    depth = [prof[a, 0, number] for a in range(TAPS)]
    along = [prof[a, 1, number] for a in range(TAPS)]
    across = [prof[a, 2, number] for a in range(TAPS)]

    lane = lax.broadcasted_iota(jnp.int32, (1, CX), 1)
    sub8 = lax.broadcasted_iota(jnp.int32, (8, CX), 0)
    low_half = sub8 < 4
    plane_of = lane // 8
    place = lane - plane_of * 8
    first_row, last_row = row == 0, row == ny - 1
    first_col, last_col = col == 0, col == nx - 1

    back[:, pl.ds(0, 16), :] = jnp.zeros((Z, 16, CX), F32)
    back[:, pl.ds(16 + CY, 16), :] = jnp.zeros((Z, 16, CX), F32)
    edge_pad[pl.ds(0, 16), :] = jnp.zeros((16, CX), F32)
    edge_pad[pl.ds(16 + CY, 16), :] = jnp.zeros((16, CX), F32)
    load.wait()

    def halves(value):
        high = value.astype(BF16)
        return high, (value - high.astype(F32)).astype(BF16)

    def prepare():
        mk = lax.broadcasted_iota(jnp.int32, (CX, CX), 0)
        mn = lax.broadcasted_iota(jnp.int32, (CX, CX), 1)

        def band(diff, taps, keep=None):
            total = jnp.zeros((CX, CX), F32)
            for c in range(TAPS):
                total = jnp.where(diff == c - RADIUS, taps[c], total)
            return total if keep is None else jnp.where(keep, total, 0.0)

        ahead = mn - mk
        planes_ahead = mn // 8 - mk // 8
        places_ahead = ahead - 8 * planes_ahead
        crossing = (mn // 4 + mk // 4) % 2 == 1
        for ref, sign in ((fwd, 1), (bwd, -1)):
            split_matrix(ref, band(sign * ahead, across))
        for ref, sign in ((side_fwd, 1), (side_bwd, -1)):
            split_matrix(
                ref, band(sign * planes_ahead, depth) * band(sign * places_ahead, across, crossing)
            )

    def split_matrix(ref, w):
        high, low = halves(w)
        ref[pl.ds(0, CX), pl.ds(0, CX)] = high
        ref[pl.ds(CX, CX), pl.ds(0, CX)] = high
        ref[pl.ds(0, CX), pl.ds(CX, CX)] = low
        ref[pl.ds(CX, CX), pl.ds(CX, CX)] = jnp.zeros((CX, CX), BF16)

    def times(value, ref):
        high, low = halves(value)
        both = jnp.dot(jnp.concatenate([high, low], axis=1), ref[...], preferred_element_type=F32)
        return both[:, 0:CX] + both[:, CX : 2 * CX]

    def planes(body, init, step=4):
        if step == Z:
            for p in range(Z):
                init = body(p, init)
            return init

        def some(i, carry):
            for k in range(step):
                carry = body(i * step + k, carry)
            return carry

        return lax.fori_loop(0, Z // step, some, init)

    def pack_columns(read):
        def body(p, total):
            turned = pltpu.roll(read(p), 8 * p + 4, 1)
            return jnp.where(plane_of == p, turned, total)

        return planes(body, jnp.zeros((CY, CX), F32), Z)

    def copies(r):
        made = []
        for k, (dy, dx) in enumerate(SIDES):
            if dx == 0:
                src = send_y.at[r, 0 if dy < 0 else 1]
                dst = recv_y.at[r, 1 if dy < 0 else 0]
            else:
                start, size = {-1: (0, 8), 0: (8, CY), 1: (8 + CY, 8)}[dy]
                land = {-1: 8 + CY, 0: 8, 1: 0}[dy]
                src = send_x.at[r, pl.ds(start, size), :]
                dst = recv_x.at[r, 1 if dx < 0 else 0, pl.ds(land, size), :]
            made.append(
                pltpu.make_async_remote_copy(
                    src_ref=src, dst_ref=dst,
                    send_sem=send_sem.at[r, k], recv_sem=recv_sem.at[r, k],
                    device_id=at(dy, dx), device_id_type=MESH,
                )
            )
        return made

    def send_columns(r):
        made = copies(r)
        for k in (4, 5, 6, 7, 2, 3):
            made[k].start()
        return made

    def send_rows(made):
        for k in (0, 1):
            made[k].start()
        return made

    def wait_rows(made):
        made[0].wait_recv()
        made[1].wait_recv()

    def wait_columns(made):
        for k in (2, 3, 4, 5, 6, 7):
            made[k].wait_recv()

    border = (lane < 4) | (lane >= CX - 4)

    def mixing(taps):
        limits = {1: (sub8 <= 0, 5), 2: (sub8 <= 1, 6), 3: (sub8 <= 2, 7), 5: (sub8 >= 5, 1), 6: (sub8 >= 6, 2), 7: (sub8 >= 7, 3)}
        weights = {s: jnp.where(mask, taps[b], 0.0) for s, (mask, b) in limits.items()}
        weights[4] = jnp.where(low_half, taps[8], taps[0])
        return weights

    def put_rows(rows, first, second):
        for q in range(8):
            a, b = rows[q], pltpu.roll(rows[q + 8], 4, 0)
            first[q] = jnp.where(low_half, a, b)
            second[q] = jnp.where(low_half, b, a)

    def get_rows(first, second, no_first, no_second):
        near, far = [], []
        for q in range(8):
            a = jnp.where(no_first, 0.0, first[q])
            b = jnp.where(no_second, 0.0, second[q])
            near.append(jnp.where(low_half, a, b))
            far.append(pltpu.roll(jnp.where(low_half, b, a), 4, 0))
        return near + far

    def cross(rows, taps, transposed, ref):
        for p in range(Z):
            twice[p, pl.ds(0, 8), :] = rows[p]
            twice[p, pl.ds(8, 8), :] = rows[p]
        weights = mixing(taps)
        mixed = []
        for p in range(Z):
            total = weights[4] * twice[p, pl.ds(4, 8), :]
            for s in (1, 2, 3, 5, 6, 7):
                total = total + weights[s] * twice[p, pl.ds(8 - s, 8), :]
            mixed.append(total)
        return times(jnp.concatenate(depth_sum(mixed, transposed), axis=0), ref)

    def edge_rows(read):
        return [jnp.where(low_half, read(p, 0), read(p, CY - 8)) for p in range(Z)]

    def halo_send(r, rows, edge):
        send_x[r, pl.ds(8, CY), :] = edge
        send_x[r, pl.ds(0, 8), :] = edge[0:8]
        send_x[r, pl.ds(8 + CY, 8), :] = edge[CY - 8 : CY]
        made = send_columns(r)
        put_rows(rows(), send_y.at[r, 0], send_y.at[r, 1])
        return send_rows(made)

    def halo_fix(r, made, ext, halo):
        wait_rows(made)
        rows = get_rows(recv_y.at[r, 1], recv_y.at[r, 0], last_row, first_row)
        for p in range(Z):
            ext[p, pl.ds(0, 8), :] = rows[p]
            ext[p, pl.ds(8 + CY, 8), :] = rows[p]
        y_fix[...] = cross(rows, along, False, fwd)
        wait_columns(made)
        halo[...] = sides(r, place < 4)
        edge = along[0] * halo[pl.ds(8 + RADIUS, CY), :]
        for b in range(1, TAPS):
            edge = edge + along[b] * halo[pl.ds(8 + RADIUS - b, CY), :]
        x_fix[...] = times(edge, side_fwd)

    def spill_send(r, rows, edge):
        edge_pad[pl.ds(16, CY), :] = times(edge, side_bwd)
        total = along[0] * edge_pad[pl.ds(4, EXT), :]
        for b in range(1, TAPS):
            total = total + along[b] * edge_pad[pl.ds(4 + b, EXT), :]
        send_x[r] = total
        made = send_columns(r)
        spilled = cross(rows(), along[::-1], True, bwd)
        put_rows([spilled[8 * p : 8 * p + 8] for p in range(Z)], send_y.at[r, 1], send_y.at[r, 0])
        return send_rows(made)

    def spill_fix(r, made):
        wait_rows(made)
        rows = get_rows(recv_y.at[r, 0], recv_y.at[r, 1], first_row, last_row)
        y_fix[...] = jnp.concatenate(rows, axis=0)
        wait_columns(made)
        both = sides(r, place >= 4)
        x_fix[pl.ds(0, 8), :] = both[8:16] + both[0:8]
        x_fix[pl.ds(8, 16), :] = both[16:CY]
        x_fix[pl.ds(24, 8), :] = both[CY : CY + 8] + both[CY + 8 : CY + 16]

    def packed_rows_fix():
        packed = jnp.zeros((8, CX), F32)
        for p in range(Z):
            packed = jnp.where(plane_of == p, pltpu.roll(y_fix[pl.ds(8 * p, 8), :], 8 * p + 4, 1), packed)
        return packed

    def fixed_columns(edge):
        packed = packed_rows_fix()
        edge = edge + x_fix[...]
        top = edge[0:8] + jnp.where(low_half, packed, 0.0)
        low = edge[CY - 8 : CY] + jnp.where(low_half, 0.0, packed)
        return jnp.concatenate([top, edge[8 : CY - 8], low], axis=0)

    def fixed_rows(read):
        ends = jnp.where(low_half, x_fix[pl.ds(0, 8), :], x_fix[pl.ds(CY - 8, 8), :])
        rows = edge_rows(read)
        for p in range(Z):
            extra = jnp.where(border, pltpu.roll(ends, 124 - 8 * p, 1), 0.0)
            rows[p] = rows[p] + y_fix[pl.ds(8 * p, 8), :] + extra
        return rows

    def with_fix(add):
        extra = x_fix[...]
        for p in range(Z):
            e = jnp.where(border, pltpu.roll(extra, 124 - 8 * p, 1), 0.0)
            y = y_fix[pl.ds(8 * p, 8), :]
            top = e[0:8] + jnp.where(low_half, y, 0.0)
            low = e[CY - 8 : CY] + jnp.where(low_half, 0.0, y)
            add(p, jnp.concatenate([top, e[8 : CY - 8], low], axis=0))

    def sides(r, from_left):
        left = jnp.where(first_col, 0.0, recv_x[r, 0])
        right = jnp.where(last_col, 0.0, recv_x[r, 1])
        both = jnp.where(from_left, left, right)
        at_row = lax.broadcasted_iota(jnp.int32, (EXT, CX), 0)
        both = jnp.where(first_row & (at_row < 8), 0.0, both)
        return jnp.where(last_row & (at_row >= 8 + CY), 0.0, both)

    def depth_sum(value, transposed):
        out = []
        for p in range(Z):
            total = None
            for a in range(TAPS):
                source = p - RADIUS + a if transposed else p + RADIUS - a
                if 0 <= source < Z:
                    term = depth[a] * value[source]
                    total = term if total is None else total + term
            out.append(total)
        return out

    def clear_border(ext):
        for p in range(Z):
            ext[p, pl.ds(0, 8), :] = jnp.zeros((8, CX), F32)
            ext[p, pl.ds(8 + CY, 8), :] = jnp.zeros((8, CX), F32)

    def blur_inside(ext, write):
        for group in range(4):
            rows = []
            for p in range(4 * group, 4 * group + 4):
                total = along[0] * ext[p, pl.ds(8 + RADIUS, CY), :]
                for b in range(1, TAPS):
                    total = total + along[b] * ext[p, pl.ds(8 + RADIUS - b, CY), :]
                rows.append(total)
            blur_y[pl.ds(group * 128, 128), :] = times(jnp.concatenate(rows, axis=0), fwd)
        for t in range(CY // 8):
            value = [blur_y[pl.ds(p * CY + t * 8, 8), :] for p in range(Z)]
            for p, total in enumerate(depth_sum(value, False)):
                write(p, t, total)

    def spread_inside(field, write):
        for t in range(CY // 8):
            value = [field[p, pl.ds(t * 8, 8), :] for p in range(Z)]
            out = times(jnp.concatenate(depth_sum(value, True), axis=0), bwd)
            for p in range(Z):
                back[p, pl.ds(16 + t * 8, 8), :] = out[8 * p : 8 * p + 8]

        for p in range(Z):
            total = along[0] * back[p, pl.ds(12, CY), :]
            for b in range(1, TAPS):
                total = total + along[b] * back[p, pl.ds(12 + b, CY), :]
            write(p, total)

    zero8 = jnp.zeros((8, CX), F32)
    main = pl.ds(8, CY)
    rows40 = lax.broadcasted_iota(jnp.int32, (40, CX), 0)
    rows32 = lax.broadcasted_iota(jnp.int32, (CY, CX), 0)
    no_row_diff = last_row & (rows40 == 39)
    no_row_flux = first_row & (rows40 == 7)
    no_col_diff = last_col & (lane == CX - 1)

    def inverse_size(dx, dy, dz):
        return lax.rsqrt(dx * dx + dy * dy + dz * dz + SMOOTHING * SMOOTHING)

    def variation(ext, halo, edges, write):
        here = halo[pl.ds(8, CY), :]
        dx = pltpu.roll(edges, CX - 1, 1) - here
        dy = halo[pl.ds(9, CY), :] - here
        dy = jnp.where(last_row & (rows32 == CY - 1), 0.0, dy)
        dz = jnp.where(plane_of == Z - 1, 0.0, pltpu.roll(here, CX - 8, 1) - here)
        side = jnp.where(first_col, 0.0, dx * inverse_size(dx, dy, dz))
        around = halo[pl.ds(0, 40), :]

        def body(p, before):
            u = ext[p, pl.ds(0, 40), :]
            dy = jnp.where(no_row_diff, 0.0, ext[p, pl.ds(1, 40), :] - u)
            beyond = pltpu.roll(around, 124 - 8 * p, 1)
            dx = pltpu.roll(jnp.where(lane == 0, beyond, u), CX - 1, 1) - u
            dx = jnp.where(no_col_diff, 0.0, dx)
            after = ext[min(p + 1, Z - 1) if isinstance(p, int) else jnp.minimum(p + 1, Z - 1), pl.ds(0, 40), :]
            dz = after - u
            inverse = inverse_size(dx, dy, dz)
            fy = jnp.where(no_row_flux, 0.0, dy * inverse)
            flux[...] = fy
            fx = (dx * inverse)[8:40]
            fz = (dz * inverse)[8:40]
            fx_side = pltpu.roll(side, 124 - 8 * p, 1)
            fx_before = pltpu.roll(jnp.where(lane == CX - 1, fx_side, fx), 1, 1)
            slope = (before - fz) + (flux[pl.ds(7, CY), :] - fy[8:40]) + (fx_before - fx)
            write(p, slope)
            return fz

        planes(body, jnp.zeros((CY, CX), F32), 4)

    def rows8(value):
        return value[0:8] + value[8:16] + value[16:24] + value[24:32]

    final_lane = lane == CX - 1
    next_lane = final_lane & jnp.logical_not(last_col)
    next_row = (sub8 == 7) & jnp.logical_not(last_row)

    def tension_inside():
        around = ux[pl.ds(8, CY), :]

        def body(p, total):
            u, g = u_ext[p, main, :], g_ext[p, main, :]
            after = min(p + 1, Z - 1) if isinstance(p, int) else jnp.minimum(p + 1, Z - 1)
            dz = u_ext[after, main, :] - u
            ez = g_ext[after, main, :] - g
            dy = jnp.where(last_row & (rows32 == CY - 1), 0.0, u_ext[p, pl.ds(9, CY), :] - u)
            ey = jnp.where(rows32 == CY - 1, 0.0, g_ext[p, pl.ds(9, CY), :] - g)
            beyond = pltpu.roll(around, 124 - 8 * p, 1)
            dx = pltpu.roll(jnp.where(lane == 0, beyond, u), CX - 1, 1) - u
            dx = jnp.where(no_col_diff, 0.0, dx)
            ex = jnp.where(final_lane, 0.0, pltpu.roll(g, CX - 1, 1) - g)
            across_u[p] = dx
            square[p] = dx * dx + dy * dy + dz * dz + SMOOTHING * SMOOTHING
            product[p] = dx * ex + dy * ey + dz * ez
            growth[p] = ex * ex + ey * ey + ez * ez
            return total[0] + rows8(g * g), total[1] + rows8(g * tv[p])

        return planes(body, (zero8, zero8))

    def tension_border():
        around = gx_halo[pl.ds(8, CY), :]
        for p in range(Z):
            ex = jnp.where(next_lane, pltpu.roll(around, 123 - 8 * p, 1) - g_ext[p, main, :], 0.0)
            product[p] = product[p] + across_u[p] * ex
            growth[p] = growth[p] + ex * ex
            bottom = pl.ds(CY - 8, 8)
            ey = jnp.where(next_row, g_ext[p, pl.ds(CY + 1, 8), :] - g_ext[p, pl.ds(CY, 8), :], 0.0)
            dy = u_ext[p, pl.ds(CY + 1, 8), :] - u_ext[p, pl.ds(CY, 8), :]
            product[p, bottom, :] = product[p, bottom, :] + dy * ey
            growth[p, bottom, :] = growth[p, bottom, :] + ey * ey

    def tension_sum(step):
        total = zero8
        for p in range(Z):
            part_ = product[p] - step * growth[p]
            size = square[p] - step * (product[p] + part_)
            size = jnp.maximum(size, SMOOTHING * SMOOTHING)
            total = total + rows8(part_ * lax.rsqrt(size))
        return total

    def fold(values):
        total = jnp.zeros((1, CX), F32)
        for i, value in enumerate(values):
            v = jnp.sum(value, axis=0, keepdims=True)
            v = v + pltpu.roll(v, 64, 1)
            v = v + pltpu.roll(v, 32, 1)
            total = jnp.where(lane // 32 == i, v, total)
        return total

    def far_first_x():
        if nx != 32:
            return [lax.rem(col + i, nx) for i in range(1, nx)]
        x, y, core = col // 8, lax.rem(col // 2, 4), lax.rem(col, 2)
        xs = [lax.rem(x + i, 4) * 8 for i in range(4)]
        ys = [lax.rem(y + i, 4) * 2 for i in range(4)]
        cores = [core, 1 - core]
        ring = (0, 1, 2, 1)
        moves = [(i, j, k) for i in range(4) for j in range(4) for k in range(2)][1:]
        moves.sort(key=lambda m: -(ring[m[0]] + ring[m[1]] + 0.3 * m[2]))
        return [xs[i] + ys[j] + cores[k] for i, j, k in moves]

    def reduce_start(a, values):
        mine = fold(values)
        part[a] = mine
        all_x[a, pl.ds(col, 1)] = mine.reshape(1, 1, CX)

        for peer in far_first_x():
            pltpu.make_async_remote_copy(
                src_ref=part.at[a], dst_ref=all_x.at[a, col],
                send_sem=ar_send.at[a, 0], recv_sem=ar_recv.at[a, 0],
                device_id={"gy": row, "gx": peer}, device_id_type=MESH,
            ).start()

    def reduce_middle(a):
        got = all_x.at[a, pl.ds(0, nx - 1)]
        pltpu.make_async_copy(got, got, ar_recv.at[a, 0]).wait()
        mine = jnp.sum(all_x[a], axis=0)
        part_y[a] = mine
        all_y[a, pl.ds(row, 1)] = mine.reshape(1, 1, CX)

        for i in sorted(range(1, ny), key=lambda i: -min(i, ny - i)):
            pltpu.make_async_remote_copy(
                src_ref=part_y.at[a], dst_ref=all_y.at[a, row],
                send_sem=ar_send.at[a, 1], recv_sem=ar_recv.at[a, 1],
                device_id=at(i, 0), device_id_type=MESH,
            ).start()

    def reduce_end(a):
        got = all_y.at[a, pl.ds(0, ny - 1)]
        pltpu.make_async_copy(got, got, ar_recv.at[a, 1]).wait()
        total = jnp.sum(all_y[a], axis=0)
        return [jnp.sum(jnp.where(lane // 32 == i, total, 0.0), axis=1, keepdims=True) for i in range(3)]

    def tell(level, distance):
        for axis, n in enumerate((ny, nx)):
            if n // 2 > distance:
                for d in (-distance, distance):
                    pl.semaphore_signal(
                        known.at[axis, level], inc=1,
                        device_id=at(d, 0) if axis == 0 else at(0, d), device_id_type=MESH,
                    )

    def hear(level, distance):
        for axis, n in enumerate((ny, nx)):
            if n // 2 > distance:
                pl.semaphore_wait(known.at[axis, level], 2)

    def keep_tv(p, slope):
        tv[p] = slope

    def advance(step):
        def body(p, c):
            u_ext[p] = u_ext[p] - step * g_ext[p]
            return c

        planes(body, 0)
        ux[...] = ux[...] - step * gx_halo[...]
        own_edge[0] = own_edge[0] - step * own_edge[1]

    def read_main(ext):
        return lambda p, start: ext[p, pl.ds(8 + start, 8), :]

    def read_field(field):
        return lambda p, start: field[p, pl.ds(start, 8), :]

    def packed_main(ext):
        return pack_columns(lambda p: ext[p, main, :])

    def add_main(p, extra):
        g_ext[p, main, :] = g_ext[p, main, :] + extra

    def finish_blur():
        sums = []

        def add(p, extra):
            h = grad[p] + extra
            grad[p] = h
            sums.append(rows8(h * h))

        with_fix(add)
        while len(sums) > 1:
            sums = [x + y for x, y in zip(sums[::2], sums[1::2])]
        return sums[0]

    def add_resid(p, extra):
        resid[p] = resid[p] + extra

    def keep_grad(p, t, value):
        grad[p, pl.ds(t * 8, 8), :] = value

    def keep_spread(p, value):
        spread[p] = value

    def gradient_inside():
        def body(p, c):
            g_ext[p, main, :] = spread[p] + WEIGHT_TV * tv[p] + DAMPING * u_ext[p, main, :]
            return c

        planes(body, 0)

    def send_gradient(r, edge):
        edge = fixed_columns(edge)
        own_edge[1] = edge
        return halo_send(r, lambda: fixed_rows(read_main(g_ext)), edge)

    def spread_and_slope(field):
        spread_inside(field, keep_spread)
        variation(u_ext, ux, own_edge[0], keep_tv)

    waiting = []
    clear_border(u_ext)
    edge = packed_main(u_ext)
    own_edge[0] = edge
    pl.semaphore_wait(barrier, len(SIDES))
    made = halo_send(0, lambda: edge_rows(read_main(u_ext)), edge)
    waiting += made
    prepare()

    def keep_residual(p, t, value):
        resid[p, pl.ds(t * 8, 8), :] = value - u_ext[p, pl.ds(8 + t * 8, 8), :]

    blur_inside(u_ext, keep_residual)
    edge = pack_columns(lambda p: resid[p])
    halo_fix(0, made, u_ext, ux)
    made = spill_send(1, lambda: fixed_rows(read_field(resid)), fixed_columns(edge))
    waiting += made
    tell(0, 2)
    with_fix(add_resid)
    spread_and_slope(resid)
    gradient_inside()
    edge = packed_main(g_ext)
    spill_fix(1, made)
    made = send_gradient(2, edge)
    waiting += made
    hear(0, 2)
    tell(1, 4)
    with_fix(add_main)
    clear_border(g_ext)
    blur_inside(g_ext, keep_grad)
    gg, gt = tension_inside()
    halo_fix(2, made, g_ext, gx_halo)
    hear(1, 4)
    tell(2, 8)
    hh = finish_blur()
    tension_border()
    gt = tension_sum(START_STEP) - gt
    hear(2, 8)
    reduce_start(0, (gg, hh, gt))

    def next_residual(p, c):
        resid[p] = resid[p] - START_STEP * grad[p]
        return c

    planes(next_residual, 0)
    made = spill_send(3, lambda: edge_rows(read_field(resid)), pack_columns(lambda p: resid[p]))
    waiting += made
    advance(START_STEP)
    spread_and_slope(resid)
    gradient_inside()
    edge = packed_main(g_ext)
    spill_fix(3, made)
    made = send_gradient(4, edge)
    waiting += made
    reduce_middle(0)

    def keep_pulled(p, extra):
        add_main(p, extra)
        resid[p] = spread[p] + extra

    with_fix(keep_pulled)
    clear_border(g_ext)
    blur_inside(g_ext, keep_grad)
    gg, gt = tension_inside()
    halo_fix(4, made, g_ext, gx_halo)
    hh = finish_blur()
    tension_border()
    g2, h2, t2 = reduce_end(0)
    change_sq = START_STEP * START_STEP * g2
    change_growth = START_STEP * START_STEP * (h2 + DAMPING * g2) - START_STEP * WEIGHT_TV * t2
    step = change_sq / change_growth

    gt = tension_sum(step) - gt
    reduce_start(1, (gg, hh, gt))

    made = spill_send(5, lambda: edge_rows(read_field(grad)), pack_columns(lambda p: grad[p]))
    waiting += made
    advance(step)
    spread_and_slope(grad)
    spill_fix(5, made)
    reduce_middle(1)

    def last(p, extra):
        pulled = resid[p] - step * (spread[p] + extra)
        g_ext[p, main, :] = pulled + WEIGHT_TV * tv[p] + DAMPING * u_ext[p, main, :]

    with_fix(last)
    g2, h2, t2 = reduce_end(1)
    change_sq = step * step * g2
    change_growth = step * step * (h2 + DAMPING * g2) - step * WEIGHT_TV * t2
    step = change_sq / change_growth

    def finish(p, c):
        out_ref[p] = u_ext[p, main, :] - step * g_ext[p, main, :]
        return c

    planes(finish, 0)

    for c in waiting:
        c.wait_send()
    for a in range(2):
        got = all_x.at[a, pl.ds(0, nx - 1)]
        pltpu.make_async_copy(got, got, ar_send.at[a, 0]).wait()
        got = all_y.at[a, pl.ds(0, ny - 1)]
        pltpu.make_async_copy(got, got, ar_send.at[a, 1]).wait()


def per_device(ny, nx, observed, profiles, tile_index):
    field = pltpu.VMEM((Z, CY, CX), F32)
    extended = pltpu.VMEM((Z, EXT, CX), F32)
    matrix = pltpu.VMEM((2 * CX, 2 * CX), BF16)
    rounds = 6
    scratch = [
        extended, extended, field, field, field,
        pltpu.VMEM((Z, CY + 32, CX), F32), field,
        pltpu.VMEM((Z * CY, CX), F32), pltpu.VMEM((40, CX), F32),
        matrix, matrix, matrix, matrix,
        pltpu.VMEM((Z, 16, CX), F32), pltpu.VMEM((Z * 8, CX), F32), pltpu.VMEM((CY, CX), F32),
        field, field, field, field,
        pltpu.VMEM((EXT, CX), F32), pltpu.VMEM((EXT, CX), F32),
        pltpu.VMEM((2, CY, CX), F32), pltpu.VMEM((CY + 32, CX), F32),
        pltpu.VMEM((rounds, 2, 8, 8, CX), F32), pltpu.VMEM((rounds, 2, 8, 8, CX), F32),
        pltpu.VMEM((rounds, EXT, CX), F32), pltpu.VMEM((rounds, 2, EXT, CX), F32),
        pltpu.VMEM((2, 1, CX), F32), pltpu.VMEM((2, nx, 1, CX), F32),
        pltpu.VMEM((2, 1, CX), F32), pltpu.VMEM((2, ny, 1, CX), F32),
        pltpu.SemaphoreType.DMA,
        pltpu.SemaphoreType.DMA((rounds, 8)), pltpu.SemaphoreType.DMA((rounds, 8)),
        pltpu.SemaphoreType.DMA((2, 2)), pltpu.SemaphoreType.DMA((2, 2)),
        pltpu.SemaphoreType.REGULAR((2, 3)),
    ]
    return pl.pallas_call(
        functools.partial(kernel, ny, nx),
        out_shape=jax.ShapeDtypeStruct((Z, CY, CX), F32),
        in_specs=[
            pl.BlockSpec(memory_space=pl.ANY),
            pl.BlockSpec(memory_space=pltpu.SMEM),
            pl.BlockSpec(memory_space=pltpu.SMEM),
        ],
        out_specs=pl.BlockSpec(memory_space=pltpu.VMEM),
        scratch_shapes=scratch,
        compiler_params=pltpu.CompilerParams(collective_id=0, has_side_effects=True),
    )(observed, jnp.transpose(profiles, (2, 1, 0)), tile_index)


def solution(mesh):
    ny, nx = mesh.shape["gy"], mesh.shape["gx"]
    return jax.shard_map(
        functools.partial(per_device, ny, nx), mesh=mesh,
        in_specs=(P(None, "gy", "gx"), P(), P()),
        out_specs=P(None, "gy", "gx"), check_vma=False,
    )
```

```python
import functools

import jax
import jax.numpy as jnp
from jax import lax
from jax.experimental import pallas as pl
from jax.experimental.pallas import tpu as pltpu
from jax.sharding import PartitionSpec as P

WEIGHT_TV = 0.02
SMOOTHING = 0.1
DAMPING = 0.05
START_STEP = 0.5
RADIUS = 4
TAPS = 9
Z, CY, CX = 16, 32, 128
EXT = CY + 16
MESH = pl.DeviceIdType.MESH
F32 = jnp.float32
BF16 = jnp.bfloat16
SIDES = ((-1, 0), (1, 0), (0, -1), (0, 1), (-1, -1), (-1, 1), (1, -1), (1, 1))


def kernel(
    ny, nx,
    obs_hbm, prof_hbm, tiles_hbm, u_out, g_out, step_out,
    prof, tiles,
    u_ext, g_ext, grad, tv, resid, back, spread, blur_y, flux,
    fwd, bwd, side_fwd, side_bwd, twice, y_fix, x_fix,
    across_u, square, product, growth,
    ux, gx_halo, own_edge, edge_pad,
    send_y, recv_y, send_x, recv_x,
    part, all_x, part_y, all_y,
    load_sem, table_sem, store_sem, send_sem, recv_sem, ar_send, ar_recv, known,
):
    row = lax.axis_index("gy")
    col = lax.axis_index("gx")

    def at(dy, dx):
        return {
            "gy": lax.rem(row + dy + ny, ny),
            "gx": lax.rem(col + dx + nx, nx),
        }

    load = pltpu.make_async_copy(obs_hbm, u_ext.at[:, pl.ds(8, CY), :], load_sem)
    load.start()
    table_loads = (
        pltpu.make_async_copy(prof_hbm, prof, table_sem.at[0]),
        pltpu.make_async_copy(tiles_hbm, tiles, table_sem.at[1]),
    )
    table_loads[0].start()
    table_loads[1].start()

    barrier = pltpu.get_barrier_semaphore()

    for dy, dx in SIDES:
        pl.semaphore_signal(barrier, inc=1, device_id=at(dy, dx), device_id_type=MESH)

    lane = lax.broadcasted_iota(jnp.int32, (1, CX), 1)
    sub8 = lax.broadcasted_iota(jnp.int32, (8, CX), 0)
    low_half = sub8 < 4
    plane_of = lane // 8
    place = lane - plane_of * 8
    first_row, last_row = row == 0, row == ny - 1
    first_col, last_col = col == 0, col == nx - 1

    back[:, pl.ds(0, 16), :] = jnp.zeros((Z, 16, CX), F32)
    back[:, pl.ds(16 + CY, 16), :] = jnp.zeros((Z, 16, CX), F32)
    edge_pad[pl.ds(0, 16), :] = jnp.zeros((16, CX), F32)
    edge_pad[pl.ds(16 + CY, 16), :] = jnp.zeros((16, CX), F32)
    load.wait()

    def halves(value):
        high = value.astype(BF16)
        return high, (value - high.astype(F32)).astype(BF16)

    def prepare():
        mk = lax.broadcasted_iota(jnp.int32, (CX, CX), 0)
        mn = lax.broadcasted_iota(jnp.int32, (CX, CX), 1)

        def band(diff, taps, keep=None):
            total = jnp.zeros((CX, CX), F32)
            for c in range(TAPS):
                total = jnp.where(diff == c - RADIUS, taps[c], total)
            return total if keep is None else jnp.where(keep, total, 0.0)

        ahead = mn - mk
        planes_ahead = mn // 8 - mk // 8
        places_ahead = ahead - 8 * planes_ahead
        crossing = (mn // 4 + mk // 4) % 2 == 1
        for ref, sign in ((fwd, 1), (bwd, -1)):
            split_matrix(ref, band(sign * ahead, across))
        for ref, sign in ((side_fwd, 1), (side_bwd, -1)):
            split_matrix(
                ref, band(sign * planes_ahead, depth) * band(sign * places_ahead, across, crossing)
            )

    def split_matrix(ref, w):
        high, low = halves(w)
        ref[pl.ds(0, CX), pl.ds(0, CX)] = high
        ref[pl.ds(CX, CX), pl.ds(0, CX)] = high
        ref[pl.ds(0, CX), pl.ds(CX, CX)] = low
        ref[pl.ds(CX, CX), pl.ds(CX, CX)] = jnp.zeros((CX, CX), BF16)

    def times(value, ref):
        high, low = halves(value)
        both = jnp.dot(jnp.concatenate([high, low], axis=1), ref[...], preferred_element_type=F32)
        return both[:, 0:CX] + both[:, CX : 2 * CX]

    def planes(body, init, step=4):
        if step == Z:
            for p in range(Z):
                init = body(p, init)
            return init

        def some(i, carry):
            for k in range(step):
                carry = body(i * step + k, carry)
            return carry

        return lax.fori_loop(0, Z // step, some, init)

    def pack_columns(read):
        def body(p, total):
            turned = pltpu.roll(read(p), 8 * p + 4, 1)
            return jnp.where(plane_of == p, turned, total)

        return planes(body, jnp.zeros((CY, CX), F32), Z)

    def copies(r):
        made = []
        for k, (dy, dx) in enumerate(SIDES):
            if dx == 0:
                src = send_y.at[r, 0 if dy < 0 else 1]
                dst = recv_y.at[r, 1 if dy < 0 else 0]
            else:
                start, size = {-1: (0, 8), 0: (8, CY), 1: (8 + CY, 8)}[dy]
                land = {-1: 8 + CY, 0: 8, 1: 0}[dy]
                src = send_x.at[r, pl.ds(start, size), :]
                dst = recv_x.at[r, 1 if dx < 0 else 0, pl.ds(land, size), :]
            made.append(
                pltpu.make_async_remote_copy(
                    src_ref=src, dst_ref=dst,
                    send_sem=send_sem.at[r, k], recv_sem=recv_sem.at[r, k],
                    device_id=at(dy, dx), device_id_type=MESH,
                )
            )
        return made

    def send_columns(r):
        made = copies(r)
        for k in (4, 5, 6, 7, 2, 3):
            made[k].start()
        return made

    def send_rows(made):
        for k in (0, 1):
            made[k].start()
        return made

    def wait_rows(made):
        made[0].wait_recv()
        made[1].wait_recv()

    def wait_columns(made):
        for k in (2, 3, 4, 5, 6, 7):
            made[k].wait_recv()

    border = (lane < 4) | (lane >= CX - 4)

    def mixing(taps):
        limits = {1: (sub8 <= 0, 5), 2: (sub8 <= 1, 6), 3: (sub8 <= 2, 7), 5: (sub8 >= 5, 1), 6: (sub8 >= 6, 2), 7: (sub8 >= 7, 3)}
        weights = {s: jnp.where(mask, taps[b], 0.0) for s, (mask, b) in limits.items()}
        weights[4] = jnp.where(low_half, taps[8], taps[0])
        return weights

    def put_rows(rows, first, second):
        for q in range(8):
            a, b = rows[q], pltpu.roll(rows[q + 8], 4, 0)
            first[q] = jnp.where(low_half, a, b)
            second[q] = jnp.where(low_half, b, a)

    def get_rows(first, second, no_first, no_second):
        near, far = [], []
        for q in range(8):
            a = jnp.where(no_first, 0.0, first[q])
            b = jnp.where(no_second, 0.0, second[q])
            near.append(jnp.where(low_half, a, b))
            far.append(pltpu.roll(jnp.where(low_half, b, a), 4, 0))
        return near + far

    def cross(rows, taps, transposed, ref):
        for p in range(Z):
            twice[p, pl.ds(0, 8), :] = rows[p]
            twice[p, pl.ds(8, 8), :] = rows[p]
        weights = mixing(taps)
        mixed = []
        for p in range(Z):
            total = weights[4] * twice[p, pl.ds(4, 8), :]
            for s in (1, 2, 3, 5, 6, 7):
                total = total + weights[s] * twice[p, pl.ds(8 - s, 8), :]
            mixed.append(total)
        return times(jnp.concatenate(depth_sum(mixed, transposed), axis=0), ref)

    def edge_rows(read):
        return [jnp.where(low_half, read(p, 0), read(p, CY - 8)) for p in range(Z)]

    def halo_send(r, rows, edge):
        send_x[r, pl.ds(8, CY), :] = edge
        send_x[r, pl.ds(0, 8), :] = edge[0:8]
        send_x[r, pl.ds(8 + CY, 8), :] = edge[CY - 8 : CY]
        made = send_columns(r)
        put_rows(rows(), send_y.at[r, 0], send_y.at[r, 1])
        return send_rows(made)

    def halo_fix(r, made, ext, halo, between=None):
        wait_rows(made)
        rows = get_rows(recv_y.at[r, 1], recv_y.at[r, 0], last_row, first_row)
        for p in range(Z):
            ext[p, pl.ds(0, 8), :] = rows[p]
            ext[p, pl.ds(8 + CY, 8), :] = rows[p]
        y_fix[...] = cross(rows, along, False, fwd)
        if between is not None:
            made[2].wait_recv()
            made[3].wait_recv()
            halo[pl.ds(8, CY), :] = sides(r, place < 4, 8, CY)
            between()
            for k in (4, 5, 6, 7):
                made[k].wait_recv()
        else:
            wait_columns(made)
        halo[...] = sides(r, place < 4)
        edge = along[0] * halo[pl.ds(8 + RADIUS, CY), :]
        for b in range(1, TAPS):
            edge = edge + along[b] * halo[pl.ds(8 + RADIUS - b, CY), :]
        x_fix[...] = times(edge, side_fwd)

    def spill_send(r, rows, edge):
        edge_pad[pl.ds(16, CY), :] = times(edge, side_bwd)
        total = along[0] * edge_pad[pl.ds(4, EXT), :]
        for b in range(1, TAPS):
            total = total + along[b] * edge_pad[pl.ds(4 + b, EXT), :]
        send_x[r] = total
        made = send_columns(r)
        spilled = cross(rows(), along[::-1], True, bwd)
        put_rows([spilled[8 * p : 8 * p + 8] for p in range(Z)], send_y.at[r, 1], send_y.at[r, 0])
        return send_rows(made)

    def spill_fix(r, made):
        wait_rows(made)
        rows = get_rows(recv_y.at[r, 0], recv_y.at[r, 1], first_row, last_row)
        y_fix[...] = jnp.concatenate(rows, axis=0)
        wait_columns(made)
        both = sides(r, place >= 4)
        x_fix[pl.ds(0, 8), :] = both[8:16] + both[0:8]
        x_fix[pl.ds(8, 16), :] = both[16:CY]
        x_fix[pl.ds(24, 8), :] = both[CY : CY + 8] + both[CY + 8 : CY + 16]

    def packed_rows_fix():
        packed = jnp.zeros((8, CX), F32)
        for p in range(Z):
            packed = jnp.where(plane_of == p, pltpu.roll(y_fix[pl.ds(8 * p, 8), :], 8 * p + 4, 1), packed)
        return packed

    def fixed_columns(edge):
        packed = packed_rows_fix()
        edge = edge + x_fix[...]
        top = edge[0:8] + jnp.where(low_half, packed, 0.0)
        low = edge[CY - 8 : CY] + jnp.where(low_half, 0.0, packed)
        return jnp.concatenate([top, edge[8 : CY - 8], low], axis=0)

    def fixed_rows(read):
        ends = jnp.where(low_half, x_fix[pl.ds(0, 8), :], x_fix[pl.ds(CY - 8, 8), :])
        rows = edge_rows(read)
        for p in range(Z):
            extra = jnp.where(border, pltpu.roll(ends, 124 - 8 * p, 1), 0.0)
            rows[p] = rows[p] + y_fix[pl.ds(8 * p, 8), :] + extra
        return rows

    def with_fix(add):
        extra = x_fix[...]
        for p in range(Z):
            e = jnp.where(border, pltpu.roll(extra, 124 - 8 * p, 1), 0.0)
            y = y_fix[pl.ds(8 * p, 8), :]
            top = e[0:8] + jnp.where(low_half, y, 0.0)
            low = e[CY - 8 : CY] + jnp.where(low_half, 0.0, y)
            add(p, jnp.concatenate([top, e[8 : CY - 8], low], axis=0))

    def sides(r, from_left, start=0, size=EXT):
        left = jnp.where(first_col, 0.0, recv_x[r, 0, pl.ds(start, size), :])
        right = jnp.where(last_col, 0.0, recv_x[r, 1, pl.ds(start, size), :])
        both = jnp.where(from_left, left, right)
        if size < EXT:
            return both
        at_row = lax.broadcasted_iota(jnp.int32, (EXT, CX), 0)
        both = jnp.where(first_row & (at_row < 8), 0.0, both)
        return jnp.where(last_row & (at_row >= 8 + CY), 0.0, both)

    def depth_sum(value, transposed):
        out = []
        for p in range(Z):
            total = None
            for a in range(TAPS):
                source = p - RADIUS + a if transposed else p + RADIUS - a
                if 0 <= source < Z:
                    term = depth[a] * value[source]
                    total = term if total is None else total + term
            out.append(total)
        return out

    def clear_border(ext):
        for p in range(Z):
            ext[p, pl.ds(0, 8), :] = jnp.zeros((8, CX), F32)
            ext[p, pl.ds(8 + CY, 8), :] = jnp.zeros((8, CX), F32)

    def blur_inside(ext, write):
        for group in range(4):
            rows = []
            for p in range(4 * group, 4 * group + 4):
                total = along[0] * ext[p, pl.ds(8 + RADIUS, CY), :]
                for b in range(1, TAPS):
                    total = total + along[b] * ext[p, pl.ds(8 + RADIUS - b, CY), :]
                rows.append(total)
            blur_y[pl.ds(group * 128, 128), :] = times(jnp.concatenate(rows, axis=0), fwd)
        for t in range(CY // 8):
            value = [blur_y[pl.ds(p * CY + t * 8, 8), :] for p in range(Z)]
            for p, total in enumerate(depth_sum(value, False)):
                write(p, t, total)

    def spread_inside(field, write):
        for t in range(CY // 8):
            value = [field[p, pl.ds(t * 8, 8), :] for p in range(Z)]
            out = times(jnp.concatenate(depth_sum(value, True), axis=0), bwd)
            for p in range(Z):
                back[p, pl.ds(16 + t * 8, 8), :] = out[8 * p : 8 * p + 8]

        for p in range(Z):
            total = along[0] * back[p, pl.ds(12, CY), :]
            for b in range(1, TAPS):
                total = total + along[b] * back[p, pl.ds(12 + b, CY), :]
            write(p, total)

    zero8 = jnp.zeros((8, CX), F32)
    main = pl.ds(8, CY)
    rows40 = lax.broadcasted_iota(jnp.int32, (40, CX), 0)
    rows32 = lax.broadcasted_iota(jnp.int32, (CY, CX), 0)
    no_row_diff = last_row & (rows40 == 39)
    no_row_flux = first_row & (rows40 == 7)
    no_col_diff = last_col & (lane == CX - 1)

    def inverse_size(dx, dy, dz):
        return lax.rsqrt(dx * dx + dy * dy + dz * dz + SMOOTHING * SMOOTHING)

    def variation(ext, halo, edges, write):
        here = halo[pl.ds(8, CY), :]
        dx = pltpu.roll(edges, CX - 1, 1) - here
        dy = halo[pl.ds(9, CY), :] - here
        dy = jnp.where(last_row & (rows32 == CY - 1), 0.0, dy)
        dz = jnp.where(plane_of == Z - 1, 0.0, pltpu.roll(here, CX - 8, 1) - here)
        side = jnp.where(first_col, 0.0, dx * inverse_size(dx, dy, dz))
        around = halo[pl.ds(0, 40), :]

        def body(p, before):
            u = ext[p, pl.ds(0, 40), :]
            dy = jnp.where(no_row_diff, 0.0, ext[p, pl.ds(1, 40), :] - u)
            beyond = pltpu.roll(around, 124 - 8 * p, 1)
            dx = pltpu.roll(jnp.where(lane == 0, beyond, u), CX - 1, 1) - u
            dx = jnp.where(no_col_diff, 0.0, dx)
            after = ext[min(p + 1, Z - 1) if isinstance(p, int) else jnp.minimum(p + 1, Z - 1), pl.ds(0, 40), :]
            dz = after - u
            inverse = inverse_size(dx, dy, dz)
            fy = jnp.where(no_row_flux, 0.0, dy * inverse)
            flux[...] = fy
            fx = (dx * inverse)[8:40]
            fz = (dz * inverse)[8:40]
            fx_side = pltpu.roll(side, 124 - 8 * p, 1)
            fx_before = pltpu.roll(jnp.where(lane == CX - 1, fx_side, fx), 1, 1)
            slope = (before - fz) + (flux[pl.ds(7, CY), :] - fy[8:40]) + (fx_before - fx)
            write(p, slope)
            return fz

        planes(body, jnp.zeros((CY, CX), F32), 4)

    def rows8(value):
        return value[0:8] + value[8:16] + value[16:24] + value[24:32]

    final_lane = lane == CX - 1
    next_lane = final_lane & jnp.logical_not(last_col)
    next_row = (sub8 == 7) & jnp.logical_not(last_row)

    def tension_inside():
        around = ux[pl.ds(8, CY), :]

        def body(p, total):
            u, g = u_ext[p, main, :], g_ext[p, main, :]
            after = min(p + 1, Z - 1) if isinstance(p, int) else jnp.minimum(p + 1, Z - 1)
            dz = u_ext[after, main, :] - u
            ez = g_ext[after, main, :] - g
            dy = jnp.where(last_row & (rows32 == CY - 1), 0.0, u_ext[p, pl.ds(9, CY), :] - u)
            ey = jnp.where(rows32 == CY - 1, 0.0, g_ext[p, pl.ds(9, CY), :] - g)
            beyond = pltpu.roll(around, 124 - 8 * p, 1)
            dx = pltpu.roll(jnp.where(lane == 0, beyond, u), CX - 1, 1) - u
            dx = jnp.where(no_col_diff, 0.0, dx)
            ex = jnp.where(final_lane, 0.0, pltpu.roll(g, CX - 1, 1) - g)
            across_u[p] = dx
            square[p] = dx * dx + dy * dy + dz * dz + SMOOTHING * SMOOTHING
            product[p] = dx * ex + dy * ey + dz * ez
            growth[p] = ex * ex + ey * ey + ez * ez
            return total[0] + rows8(g * g), total[1] + rows8(g * tv[p])

        return planes(body, (zero8, zero8))

    def tension_border():
        around = gx_halo[pl.ds(8, CY), :]
        for p in range(Z):
            ex = jnp.where(next_lane, pltpu.roll(around, 123 - 8 * p, 1) - g_ext[p, main, :], 0.0)
            product[p] = product[p] + across_u[p] * ex
            growth[p] = growth[p] + ex * ex
            bottom = pl.ds(CY - 8, 8)
            ey = jnp.where(next_row, g_ext[p, pl.ds(CY + 1, 8), :] - g_ext[p, pl.ds(CY, 8), :], 0.0)
            dy = u_ext[p, pl.ds(CY + 1, 8), :] - u_ext[p, pl.ds(CY, 8), :]
            product[p, bottom, :] = product[p, bottom, :] + dy * ey
            growth[p, bottom, :] = growth[p, bottom, :] + ey * ey

    def tension_sum(step):
        total = zero8
        for p in range(Z):
            part_ = product[p] - step * growth[p]
            size = square[p] - step * (product[p] + part_)
            size = jnp.maximum(size, SMOOTHING * SMOOTHING)
            total = total + rows8(part_ * lax.rsqrt(size))
        return total

    def fold(values):
        total = jnp.zeros((1, CX), F32)
        for i, value in enumerate(values):
            v = jnp.sum(value, axis=0, keepdims=True)
            v = v + pltpu.roll(v, 64, 1)
            v = v + pltpu.roll(v, 32, 1)
            total = jnp.where(lane // 32 == i, v, total)
        return total

    def far_first_x():
        if nx != 32:
            return [lax.rem(col + i, nx) for i in range(1, nx)]
        x, y, core = col // 8, lax.rem(col // 2, 4), lax.rem(col, 2)
        xs = [lax.rem(x + i, 4) * 8 for i in range(4)]
        ys = [lax.rem(y + i, 4) * 2 for i in range(4)]
        cores = [core, 1 - core]
        ring = (0, 1, 2, 1)
        moves = [(i, j, k) for i in range(4) for j in range(4) for k in range(2)][1:]
        moves.sort(key=lambda m: -(ring[m[0]] + ring[m[1]] + 0.3 * m[2]))
        return [xs[i] + ys[j] + cores[k] for i, j, k in moves]

    def reduce_start(a, values):
        mine = fold(values)
        part[a] = mine
        all_x[a, pl.ds(col, 1)] = mine.reshape(1, 1, CX)

        for peer in far_first_x():
            pltpu.make_async_remote_copy(
                src_ref=part.at[a], dst_ref=all_x.at[a, col],
                send_sem=ar_send.at[a, 0], recv_sem=ar_recv.at[a, 0],
                device_id={"gy": row, "gx": peer}, device_id_type=MESH,
            ).start()

    def reduce_middle(a):
        got = all_x.at[a, pl.ds(0, nx - 1)]
        pltpu.make_async_copy(got, got, ar_recv.at[a, 0]).wait()
        mine = jnp.sum(all_x[a], axis=0)
        part_y[a] = mine
        all_y[a, pl.ds(row, 1)] = mine.reshape(1, 1, CX)

        for i in sorted(range(1, ny), key=lambda i: -min(i, ny - i)):
            pltpu.make_async_remote_copy(
                src_ref=part_y.at[a], dst_ref=all_y.at[a, row],
                send_sem=ar_send.at[a, 1], recv_sem=ar_recv.at[a, 1],
                device_id=at(i, 0), device_id_type=MESH,
            ).start()

    def reduce_end(a):
        got = all_y.at[a, pl.ds(0, ny - 1)]
        pltpu.make_async_copy(got, got, ar_recv.at[a, 1]).wait()
        total = jnp.sum(all_y[a], axis=0)
        return [jnp.sum(jnp.where(lane // 32 == i, total, 0.0), axis=1, keepdims=True) for i in range(3)]

    def tell(level, distance):
        for axis, n in enumerate((ny, nx)):
            if n // 2 > distance:
                for d in (-distance, distance):
                    pl.semaphore_signal(
                        known.at[axis, level], inc=1,
                        device_id=at(d, 0) if axis == 0 else at(0, d), device_id_type=MESH,
                    )

    def hear(level, distance):
        for axis, n in enumerate((ny, nx)):
            if n // 2 > distance:
                pl.semaphore_wait(known.at[axis, level], 2)

    def keep_tv(p, slope):
        tv[p] = slope

    def advance(step):
        def body(p, c):
            u_ext[p] = u_ext[p] - step * g_ext[p]
            return c

        planes(body, 0)
        ux[...] = ux[...] - step * gx_halo[...]
        own_edge[0] = own_edge[0] - step * own_edge[1]

    def read_main(ext):
        return lambda p, start: ext[p, pl.ds(8 + start, 8), :]

    def read_field(field):
        return lambda p, start: field[p, pl.ds(start, 8), :]

    def packed_main(ext):
        return pack_columns(lambda p: ext[p, main, :])

    def add_main(p, extra):
        g_ext[p, main, :] = g_ext[p, main, :] + extra

    def finish_blur():
        sums = []

        def add(p, extra):
            h = grad[p] + extra
            grad[p] = h
            sums.append(rows8(h * h))

        with_fix(add)
        while len(sums) > 1:
            sums = [x + y for x, y in zip(sums[::2], sums[1::2])]
        return sums[0]

    def add_resid(p, extra):
        resid[p] = resid[p] + extra

    def keep_grad(p, t, value):
        grad[p, pl.ds(t * 8, 8), :] = value

    def keep_spread(p, value):
        spread[p] = value

    def gradient_inside():
        def body(p, c):
            g_ext[p, main, :] = spread[p] + WEIGHT_TV * tv[p] + DAMPING * u_ext[p, main, :]
            return c

        planes(body, 0)

    def send_gradient(r, edge):
        edge = fixed_columns(edge)
        own_edge[1] = edge
        return halo_send(r, lambda: fixed_rows(read_main(g_ext)), edge)

    def spread_and_slope(field):
        spread_inside(field, keep_spread)
        variation(u_ext, ux, own_edge[0], keep_tv)

    waiting = []
    clear_border(u_ext)
    edge = packed_main(u_ext)
    own_edge[0] = edge
    pl.semaphore_wait(barrier, len(SIDES))
    made = halo_send(0, lambda: edge_rows(read_main(u_ext)), edge)
    waiting += made
    table_loads[0].wait()
    table_loads[1].wait()
    number = tiles[row, col]
    depth = [prof[a, 0, number] for a in range(TAPS)]
    along = [prof[a, 1, number] for a in range(TAPS)]
    across = [prof[a, 2, number] for a in range(TAPS)]
    prepare()

    def keep_residual(p, t, value):
        resid[p, pl.ds(t * 8, 8), :] = value - u_ext[p, pl.ds(8 + t * 8, 8), :]

    blur_inside(u_ext, keep_residual)
    edge = pack_columns(lambda p: resid[p])
    halo_fix(0, made, u_ext, ux)
    made = spill_send(1, lambda: fixed_rows(read_field(resid)), fixed_columns(edge))
    waiting += made
    tell(0, 2)
    with_fix(add_resid)
    spread_and_slope(resid)
    gradient_inside()
    edge = packed_main(g_ext)
    spill_fix(1, made)
    made = send_gradient(2, edge)
    waiting += made
    hear(0, 2)
    tell(1, 4)
    with_fix(add_main)
    clear_border(g_ext)
    blur_inside(g_ext, keep_grad)
    gg, gt = tension_inside()
    sums = []

    def tension():
        tension_border()
        sums.append(tension_sum(START_STEP))

    halo_fix(2, made, g_ext, gx_halo, tension)
    hear(1, 4)
    tell(2, 8)
    hh = finish_blur()
    gt = sums[0] - gt
    hear(2, 8)
    reduce_start(0, (gg, hh, gt))

    def next_residual(p, c):
        resid[p] = resid[p] - START_STEP * grad[p]
        return c

    planes(next_residual, 0)
    made = spill_send(3, lambda: edge_rows(read_field(resid)), pack_columns(lambda p: resid[p]))
    waiting += made
    advance(START_STEP)
    spread_and_slope(resid)
    gradient_inside()
    edge = packed_main(g_ext)
    spill_fix(3, made)
    made = send_gradient(4, edge)
    waiting += made
    reduce_middle(0)

    def keep_pulled(p, extra):
        add_main(p, extra)
        resid[p] = spread[p] + extra

    with_fix(keep_pulled)
    clear_border(g_ext)
    blur_inside(g_ext, keep_grad)
    gg, gt = tension_inside()
    halo_fix(4, made, g_ext, gx_halo, tension_border)
    hh = finish_blur()
    g2, h2, t2 = reduce_end(0)
    change_sq = START_STEP * START_STEP * g2
    change_growth = START_STEP * START_STEP * (h2 + DAMPING * g2) - START_STEP * WEIGHT_TV * t2
    step = change_sq / change_growth

    gt = tension_sum(step) - gt
    reduce_start(1, (gg, hh, gt))

    made = spill_send(5, lambda: edge_rows(read_field(grad)), pack_columns(lambda p: grad[p]))
    waiting += made
    advance(step)
    u_store = pltpu.make_async_copy(u_ext.at[:, main, :], u_out, store_sem.at[0])
    u_store.start()
    spread_and_slope(grad)
    spill_fix(5, made)
    reduce_middle(1)

    def last(p, extra):
        pulled = resid[p] - step * (spread[p] + extra)
        g_ext[p, main, :] = pulled + WEIGHT_TV * tv[p] + DAMPING * u_ext[p, main, :]

    with_fix(last)
    g_store = pltpu.make_async_copy(g_ext.at[:, main, :], g_out, store_sem.at[1])
    g_store.start()
    for c in waiting:
        c.wait_send()
    for a in range(2):
        got = all_x.at[a, pl.ds(0, nx - 1)]
        pltpu.make_async_copy(got, got, ar_send.at[a, 0]).wait()
        got = all_y.at[a, pl.ds(0, ny - 1)]
        pltpu.make_async_copy(got, got, ar_send.at[a, 1]).wait()
    u_store.wait()
    g_store.wait()
    g2, h2, t2 = reduce_end(1)
    change_sq = step * step * g2
    change_growth = step * step * (h2 + DAMPING * g2) - step * WEIGHT_TV * t2
    step_out[...] = jnp.broadcast_to(change_sq / change_growth, (1, CX))


def per_device(ny, nx, observed, profiles, tile_index):
    field = pltpu.VMEM((Z, CY, CX), F32)
    extended = pltpu.VMEM((Z, EXT, CX), F32)
    matrix = pltpu.VMEM((2 * CX, 2 * CX), BF16)
    rounds = 6
    scratch = [
        pltpu.SMEM((TAPS, 3, profiles.shape[0]), F32), pltpu.SMEM((ny, nx), jnp.int32),
        extended, extended, field, field, field,
        pltpu.VMEM((Z, CY + 32, CX), F32), field,
        pltpu.VMEM((Z * CY, CX), F32), pltpu.VMEM((40, CX), F32),
        matrix, matrix, matrix, matrix,
        pltpu.VMEM((Z, 16, CX), F32), pltpu.VMEM((Z * 8, CX), F32), pltpu.VMEM((CY, CX), F32),
        field, field, field, field,
        pltpu.VMEM((EXT, CX), F32), pltpu.VMEM((EXT, CX), F32),
        pltpu.VMEM((2, CY, CX), F32), pltpu.VMEM((CY + 32, CX), F32),
        pltpu.VMEM((rounds, 2, 8, 8, CX), F32), pltpu.VMEM((rounds, 2, 8, 8, CX), F32),
        pltpu.VMEM((rounds, EXT, CX), F32), pltpu.VMEM((rounds, 2, EXT, CX), F32),
        pltpu.VMEM((2, 1, CX), F32), pltpu.VMEM((2, nx, 1, CX), F32),
        pltpu.VMEM((2, 1, CX), F32), pltpu.VMEM((2, ny, 1, CX), F32),
        pltpu.SemaphoreType.DMA, pltpu.SemaphoreType.DMA((2,)), pltpu.SemaphoreType.DMA((2,)),
        pltpu.SemaphoreType.DMA((rounds, 8)), pltpu.SemaphoreType.DMA((rounds, 8)),
        pltpu.SemaphoreType.DMA((2, 2)), pltpu.SemaphoreType.DMA((2, 2)),
        pltpu.SemaphoreType.REGULAR((2, 3)),
    ]
    whole = jax.ShapeDtypeStruct((Z, CY, CX), F32)
    estimate, gradient, step = pl.pallas_call(
        functools.partial(kernel, ny, nx),
        out_shape=(whole, whole, jax.ShapeDtypeStruct((1, CX), F32)),
        in_specs=[
            pl.BlockSpec(memory_space=pl.ANY),
            pl.BlockSpec(memory_space=pl.ANY),
            pl.BlockSpec(memory_space=pl.ANY),
        ],
        out_specs=(
            pl.BlockSpec(memory_space=pl.ANY),
            pl.BlockSpec(memory_space=pl.ANY),
            pl.BlockSpec(memory_space=pltpu.VMEM),
        ),
        scratch_shapes=scratch,
        compiler_params=pltpu.CompilerParams(collective_id=0, has_side_effects=True),
    )(observed, jnp.transpose(profiles, (2, 1, 0)), tile_index)
    return estimate - step[0] * gradient


def solution(mesh):
    ny, nx = mesh.shape["gy"], mesh.shape["gx"]
    return jax.shard_map(
        functools.partial(per_device, ny, nx), mesh=mesh,
        in_specs=(P(None, "gy", "gx"), P(), P()),
        out_specs=P(None, "gy", "gx"), check_vma=False,
    )
```

```python
import functools

import jax
import jax.numpy as jnp
from jax import lax
from jax.experimental import pallas as pl
from jax.experimental.pallas import tpu as pltpu
from jax.sharding import PartitionSpec as P

WEIGHT_TV = 0.02
SMOOTHING = 0.1
DAMPING = 0.05
START_STEP = 0.5
RADIUS = 4
TAPS = 9
Z, CY, CX = 16, 32, 128
EXT = CY + 16
MESH = pl.DeviceIdType.MESH
F32 = jnp.float32
BF16 = jnp.bfloat16
SIDES = ((-1, 0), (1, 0), (0, -1), (0, 1), (-1, -1), (-1, 1), (1, -1), (1, 1))


def kernel(
    ny, nx,
    obs_hbm, prof_hbm, tiles_hbm, u_out, g_out, step_out,
    prof, tiles,
    u_ext, g_ext, grad, tv, resid, back, spread, blur_y, flux,
    fwd, bwd, side_fwd, side_bwd, twice, y_fix, x_fix,
    across_u, square, product, growth,
    ux, gx_halo, own_edge, edge_pad,
    send_y, recv_y, send_x, recv_x,
    part, all_x, part_y, all_y,
    load_sem, table_sem, send_sem, recv_sem, ar_send, ar_recv, known,
):
    row = lax.axis_index("gy")
    col = lax.axis_index("gx")

    def at(dy, dx):
        return {
            "gy": lax.rem(row + dy + ny, ny),
            "gx": lax.rem(col + dx + nx, nx),
        }

    load = pltpu.make_async_copy(obs_hbm, u_ext.at[:, pl.ds(8, CY), :], load_sem)
    load.start()
    table_loads = (
        pltpu.make_async_copy(prof_hbm, prof, table_sem.at[0]),
        pltpu.make_async_copy(tiles_hbm, tiles, table_sem.at[1]),
    )
    table_loads[0].start()
    table_loads[1].start()

    barrier = pltpu.get_barrier_semaphore()

    for dy, dx in SIDES:
        pl.semaphore_signal(barrier, inc=1, device_id=at(dy, dx), device_id_type=MESH)

    lane = lax.broadcasted_iota(jnp.int32, (1, CX), 1)
    sub8 = lax.broadcasted_iota(jnp.int32, (8, CX), 0)
    low_half = sub8 < 4
    plane_of = lane // 8
    place = lane - plane_of * 8
    first_row, last_row = row == 0, row == ny - 1
    first_col, last_col = col == 0, col == nx - 1

    back[:, pl.ds(0, 16), :] = jnp.zeros((Z, 16, CX), F32)
    back[:, pl.ds(16 + CY, 16), :] = jnp.zeros((Z, 16, CX), F32)
    edge_pad[pl.ds(0, 16), :] = jnp.zeros((16, CX), F32)
    edge_pad[pl.ds(16 + CY, 16), :] = jnp.zeros((16, CX), F32)
    load.wait()

    def halves(value):
        high = value.astype(BF16)
        return high, (value - high.astype(F32)).astype(BF16)

    def prepare():
        mk = lax.broadcasted_iota(jnp.int32, (CX, CX), 0)
        mn = lax.broadcasted_iota(jnp.int32, (CX, CX), 1)

        def band(diff, taps, keep=None):
            total = jnp.zeros((CX, CX), F32)
            for c in range(TAPS):
                total = jnp.where(diff == c - RADIUS, taps[c], total)
            return total if keep is None else jnp.where(keep, total, 0.0)

        ahead = mn - mk
        planes_ahead = mn // 8 - mk // 8
        places_ahead = ahead - 8 * planes_ahead
        crossing = (mn // 4 + mk // 4) % 2 == 1
        for ref, sign in ((fwd, 1), (bwd, -1)):
            split_matrix(ref, band(sign * ahead, across))
        for ref, sign in ((side_fwd, 1), (side_bwd, -1)):
            split_matrix(
                ref, band(sign * planes_ahead, depth) * band(sign * places_ahead, across, crossing)
            )

    def split_matrix(ref, w):
        high, low = halves(w)
        ref[pl.ds(0, CX), pl.ds(0, CX)] = high
        ref[pl.ds(CX, CX), pl.ds(0, CX)] = high
        ref[pl.ds(0, CX), pl.ds(CX, CX)] = low
        ref[pl.ds(CX, CX), pl.ds(CX, CX)] = jnp.zeros((CX, CX), BF16)

    def times(value, ref):
        high, low = halves(value)
        both = jnp.dot(jnp.concatenate([high, low], axis=1), ref[...], preferred_element_type=F32)
        return both[:, 0:CX] + both[:, CX : 2 * CX]

    def planes(body, init, step=4):
        if step == Z:
            for p in range(Z):
                init = body(p, init)
            return init

        def some(i, carry):
            for k in range(step):
                carry = body(i * step + k, carry)
            return carry

        return lax.fori_loop(0, Z // step, some, init)

    def pack_columns(read):
        def body(p, total):
            turned = pltpu.roll(read(p), 8 * p + 4, 1)
            return jnp.where(plane_of == p, turned, total)

        return planes(body, jnp.zeros((CY, CX), F32), Z)

    def copies(r):
        made = []
        for k, (dy, dx) in enumerate(SIDES):
            if dx == 0:
                src = send_y.at[r, 0 if dy < 0 else 1]
                dst = recv_y.at[r, 1 if dy < 0 else 0]
            else:
                start, size = {-1: (0, 8), 0: (8, CY), 1: (8 + CY, 8)}[dy]
                land = {-1: 8 + CY, 0: 8, 1: 0}[dy]
                src = send_x.at[r, pl.ds(start, size), :]
                dst = recv_x.at[r, 1 if dx < 0 else 0, pl.ds(land, size), :]
            made.append(
                pltpu.make_async_remote_copy(
                    src_ref=src, dst_ref=dst,
                    send_sem=send_sem.at[r, k], recv_sem=recv_sem.at[r, k],
                    device_id=at(dy, dx), device_id_type=MESH,
                )
            )
        return made

    def send_columns(r):
        made = copies(r)
        for k in (4, 5, 6, 7, 2, 3):
            made[k].start()
        return made

    def send_rows(made):
        for k in (0, 1):
            made[k].start()
        return made

    def wait_rows(made):
        made[0].wait_recv()
        made[1].wait_recv()

    def wait_columns(made):
        for k in (2, 3, 4, 5, 6, 7):
            made[k].wait_recv()

    border = (lane < 4) | (lane >= CX - 4)

    def mixing(taps):
        limits = {1: (sub8 <= 0, 5), 2: (sub8 <= 1, 6), 3: (sub8 <= 2, 7), 5: (sub8 >= 5, 1), 6: (sub8 >= 6, 2), 7: (sub8 >= 7, 3)}
        weights = {s: jnp.where(mask, taps[b], 0.0) for s, (mask, b) in limits.items()}
        weights[4] = jnp.where(low_half, taps[8], taps[0])
        return weights

    def put_rows(rows, first, second):
        for q in range(8):
            a, b = rows[q], pltpu.roll(rows[q + 8], 4, 0)
            first[q] = jnp.where(low_half, a, b)
            second[q] = jnp.where(low_half, b, a)

    def get_rows(first, second, no_first, no_second):
        near, far = [], []
        for q in range(8):
            a = jnp.where(no_first, 0.0, first[q])
            b = jnp.where(no_second, 0.0, second[q])
            near.append(jnp.where(low_half, a, b))
            far.append(pltpu.roll(jnp.where(low_half, b, a), 4, 0))
        return near + far

    def cross(rows, taps, transposed, ref):
        for p in range(Z):
            twice[p, pl.ds(0, 8), :] = rows[p]
            twice[p, pl.ds(8, 8), :] = rows[p]
        weights = mixing(taps)
        mixed = []
        for p in range(Z):
            total = weights[4] * twice[p, pl.ds(4, 8), :]
            for s in (1, 2, 3, 5, 6, 7):
                total = total + weights[s] * twice[p, pl.ds(8 - s, 8), :]
            mixed.append(total)
        return times(jnp.concatenate(depth_sum(mixed, transposed), axis=0), ref)

    def edge_rows(read):
        return [jnp.where(low_half, read(p, 0), read(p, CY - 8)) for p in range(Z)]

    def halo_send(r, rows, edge):
        send_x[r, pl.ds(8, CY), :] = edge
        send_x[r, pl.ds(0, 8), :] = edge[0:8]
        send_x[r, pl.ds(8 + CY, 8), :] = edge[CY - 8 : CY]
        made = send_columns(r)
        put_rows(rows(), send_y.at[r, 0], send_y.at[r, 1])
        return send_rows(made)

    def halo_fix(r, made, ext, halo, between=None):
        wait_rows(made)
        rows = get_rows(recv_y.at[r, 1], recv_y.at[r, 0], last_row, first_row)
        for p in range(Z):
            ext[p, pl.ds(0, 8), :] = rows[p]
            ext[p, pl.ds(8 + CY, 8), :] = rows[p]
        y_fix[...] = cross(rows, along, False, fwd)
        if between is not None:
            made[2].wait_recv()
            made[3].wait_recv()
            halo[pl.ds(8, CY), :] = sides(r, place < 4, 8, CY)
            between()
            for k in (4, 5, 6, 7):
                made[k].wait_recv()
        else:
            wait_columns(made)
        halo[...] = sides(r, place < 4)
        edge = along[0] * halo[pl.ds(8 + RADIUS, CY), :]
        for b in range(1, TAPS):
            edge = edge + along[b] * halo[pl.ds(8 + RADIUS - b, CY), :]
        x_fix[...] = times(edge, side_fwd)

    def spill_send(r, rows, edge):
        edge_pad[pl.ds(16, CY), :] = times(edge, side_bwd)
        total = along[0] * edge_pad[pl.ds(4, EXT), :]
        for b in range(1, TAPS):
            total = total + along[b] * edge_pad[pl.ds(4 + b, EXT), :]
        send_x[r] = total
        made = send_columns(r)
        spilled = cross(rows(), along[::-1], True, bwd)
        put_rows([spilled[8 * p : 8 * p + 8] for p in range(Z)], send_y.at[r, 1], send_y.at[r, 0])
        return send_rows(made)

    def spill_fix(r, made):
        wait_rows(made)
        rows = get_rows(recv_y.at[r, 0], recv_y.at[r, 1], first_row, last_row)
        y_fix[...] = jnp.concatenate(rows, axis=0)
        wait_columns(made)
        both = sides(r, place >= 4)
        x_fix[pl.ds(0, 8), :] = both[8:16] + both[0:8]
        x_fix[pl.ds(8, 16), :] = both[16:CY]
        x_fix[pl.ds(24, 8), :] = both[CY : CY + 8] + both[CY + 8 : CY + 16]

    def packed_rows_fix():
        packed = jnp.zeros((8, CX), F32)
        for p in range(Z):
            packed = jnp.where(plane_of == p, pltpu.roll(y_fix[pl.ds(8 * p, 8), :], 8 * p + 4, 1), packed)
        return packed

    def fixed_columns(edge):
        packed = packed_rows_fix()
        edge = edge + x_fix[...]
        top = edge[0:8] + jnp.where(low_half, packed, 0.0)
        low = edge[CY - 8 : CY] + jnp.where(low_half, 0.0, packed)
        return jnp.concatenate([top, edge[8 : CY - 8], low], axis=0)

    def fixed_rows(read):
        ends = jnp.where(low_half, x_fix[pl.ds(0, 8), :], x_fix[pl.ds(CY - 8, 8), :])
        rows = edge_rows(read)
        for p in range(Z):
            extra = jnp.where(border, pltpu.roll(ends, 124 - 8 * p, 1), 0.0)
            rows[p] = rows[p] + y_fix[pl.ds(8 * p, 8), :] + extra
        return rows

    def with_fix(add):
        extra = x_fix[...]
        for p in range(Z):
            e = jnp.where(border, pltpu.roll(extra, 124 - 8 * p, 1), 0.0)
            y = y_fix[pl.ds(8 * p, 8), :]
            top = e[0:8] + jnp.where(low_half, y, 0.0)
            low = e[CY - 8 : CY] + jnp.where(low_half, 0.0, y)
            add(p, jnp.concatenate([top, e[8 : CY - 8], low], axis=0))

    def sides(r, from_left, start=0, size=EXT):
        left = jnp.where(first_col, 0.0, recv_x[r, 0, pl.ds(start, size), :])
        right = jnp.where(last_col, 0.0, recv_x[r, 1, pl.ds(start, size), :])
        both = jnp.where(from_left, left, right)
        if size < EXT:
            return both
        at_row = lax.broadcasted_iota(jnp.int32, (EXT, CX), 0)
        both = jnp.where(first_row & (at_row < 8), 0.0, both)
        return jnp.where(last_row & (at_row >= 8 + CY), 0.0, both)

    def depth_sum(value, transposed):
        out = []
        for p in range(Z):
            total = None
            for a in range(TAPS):
                source = p - RADIUS + a if transposed else p + RADIUS - a
                if 0 <= source < Z:
                    term = depth[a] * value[source]
                    total = term if total is None else total + term
            out.append(total)
        return out

    def clear_border(ext):
        for p in range(Z):
            ext[p, pl.ds(0, 8), :] = jnp.zeros((8, CX), F32)
            ext[p, pl.ds(8 + CY, 8), :] = jnp.zeros((8, CX), F32)

    def blur_inside(ext, write):
        for group in range(4):
            rows = []
            for p in range(4 * group, 4 * group + 4):
                total = along[0] * ext[p, pl.ds(8 + RADIUS, CY), :]
                for b in range(1, TAPS):
                    total = total + along[b] * ext[p, pl.ds(8 + RADIUS - b, CY), :]
                rows.append(total)
            blur_y[pl.ds(group * 128, 128), :] = times(jnp.concatenate(rows, axis=0), fwd)
        for t in range(CY // 8):
            value = [blur_y[pl.ds(p * CY + t * 8, 8), :] for p in range(Z)]
            for p, total in enumerate(depth_sum(value, False)):
                write(p, t, total)

    def spread_inside(field, write):
        for t in range(CY // 8):
            value = [field[p, pl.ds(t * 8, 8), :] for p in range(Z)]
            out = times(jnp.concatenate(depth_sum(value, True), axis=0), bwd)
            for p in range(Z):
                back[p, pl.ds(16 + t * 8, 8), :] = out[8 * p : 8 * p + 8]

        for p in range(Z):
            total = along[0] * back[p, pl.ds(12, CY), :]
            for b in range(1, TAPS):
                total = total + along[b] * back[p, pl.ds(12 + b, CY), :]
            write(p, total)

    zero8 = jnp.zeros((8, CX), F32)
    main = pl.ds(8, CY)
    rows40 = lax.broadcasted_iota(jnp.int32, (40, CX), 0)
    rows32 = lax.broadcasted_iota(jnp.int32, (CY, CX), 0)
    no_row_diff = last_row & (rows40 == 39)
    no_row_flux = first_row & (rows40 == 7)
    no_col_diff = last_col & (lane == CX - 1)

    def inverse_size(dx, dy, dz):
        return lax.rsqrt(dx * dx + dy * dy + dz * dz + SMOOTHING * SMOOTHING)

    def variation(ext, halo, edges, write):
        here = halo[pl.ds(8, CY), :]
        dx = pltpu.roll(edges, CX - 1, 1) - here
        dy = halo[pl.ds(9, CY), :] - here
        dy = jnp.where(last_row & (rows32 == CY - 1), 0.0, dy)
        dz = jnp.where(plane_of == Z - 1, 0.0, pltpu.roll(here, CX - 8, 1) - here)
        side = jnp.where(first_col, 0.0, dx * inverse_size(dx, dy, dz))
        around = halo[pl.ds(0, 40), :]

        def body(p, before):
            u = ext[p, pl.ds(0, 40), :]
            dy = jnp.where(no_row_diff, 0.0, ext[p, pl.ds(1, 40), :] - u)
            beyond = pltpu.roll(around, 124 - 8 * p, 1)
            dx = pltpu.roll(jnp.where(lane == 0, beyond, u), CX - 1, 1) - u
            dx = jnp.where(no_col_diff, 0.0, dx)
            after = ext[min(p + 1, Z - 1) if isinstance(p, int) else jnp.minimum(p + 1, Z - 1), pl.ds(0, 40), :]
            dz = after - u
            inverse = inverse_size(dx, dy, dz)
            fy = jnp.where(no_row_flux, 0.0, dy * inverse)
            flux[...] = fy
            fx = (dx * inverse)[8:40]
            fz = (dz * inverse)[8:40]
            fx_side = pltpu.roll(side, 124 - 8 * p, 1)
            fx_before = pltpu.roll(jnp.where(lane == CX - 1, fx_side, fx), 1, 1)
            slope = (before - fz) + (flux[pl.ds(7, CY), :] - fy[8:40]) + (fx_before - fx)
            write(p, slope)
            return fz

        planes(body, jnp.zeros((CY, CX), F32), 4)

    def rows8(value):
        return value[0:8] + value[8:16] + value[16:24] + value[24:32]

    final_lane = lane == CX - 1
    next_lane = final_lane & jnp.logical_not(last_col)
    next_row = (sub8 == 7) & jnp.logical_not(last_row)

    def tension_inside():
        around = ux[pl.ds(8, CY), :]

        def body(p, total):
            u, g = u_ext[p, main, :], g_ext[p, main, :]
            after = min(p + 1, Z - 1) if isinstance(p, int) else jnp.minimum(p + 1, Z - 1)
            dz = u_ext[after, main, :] - u
            ez = g_ext[after, main, :] - g
            dy = jnp.where(last_row & (rows32 == CY - 1), 0.0, u_ext[p, pl.ds(9, CY), :] - u)
            ey = jnp.where(rows32 == CY - 1, 0.0, g_ext[p, pl.ds(9, CY), :] - g)
            beyond = pltpu.roll(around, 124 - 8 * p, 1)
            dx = pltpu.roll(jnp.where(lane == 0, beyond, u), CX - 1, 1) - u
            dx = jnp.where(no_col_diff, 0.0, dx)
            ex = jnp.where(final_lane, 0.0, pltpu.roll(g, CX - 1, 1) - g)
            across_u[p] = dx
            square[p] = dx * dx + dy * dy + dz * dz + SMOOTHING * SMOOTHING
            product[p] = dx * ex + dy * ey + dz * ez
            growth[p] = ex * ex + ey * ey + ez * ez
            return total[0] + rows8(g * g), total[1] + rows8(g * tv[p])

        return planes(body, (zero8, zero8))

    def tension_border():
        around = gx_halo[pl.ds(8, CY), :]
        for p in range(Z):
            ex = jnp.where(next_lane, pltpu.roll(around, 123 - 8 * p, 1) - g_ext[p, main, :], 0.0)
            product[p] = product[p] + across_u[p] * ex
            growth[p] = growth[p] + ex * ex
            bottom = pl.ds(CY - 8, 8)
            ey = jnp.where(next_row, g_ext[p, pl.ds(CY + 1, 8), :] - g_ext[p, pl.ds(CY, 8), :], 0.0)
            dy = u_ext[p, pl.ds(CY + 1, 8), :] - u_ext[p, pl.ds(CY, 8), :]
            product[p, bottom, :] = product[p, bottom, :] + dy * ey
            growth[p, bottom, :] = growth[p, bottom, :] + ey * ey

    def tension_sum(step):
        total = zero8
        for p in range(Z):
            part_ = product[p] - step * growth[p]
            size = square[p] - step * (product[p] + part_)
            size = jnp.maximum(size, SMOOTHING * SMOOTHING)
            total = total + rows8(part_ * lax.rsqrt(size))
        return total

    def fold(values):
        total = jnp.zeros((1, CX), F32)
        for i, value in enumerate(values):
            v = jnp.sum(value, axis=0, keepdims=True)
            v = v + pltpu.roll(v, 64, 1)
            v = v + pltpu.roll(v, 32, 1)
            total = jnp.where(lane // 32 == i, v, total)
        return total

    def far_first_x():
        if nx != 32:
            return [lax.rem(col + i, nx) for i in range(1, nx)]
        x, y, core = col // 8, lax.rem(col // 2, 4), lax.rem(col, 2)
        xs = [lax.rem(x + i, 4) * 8 for i in range(4)]
        ys = [lax.rem(y + i, 4) * 2 for i in range(4)]
        cores = [core, 1 - core]
        ring = (0, 1, 2, 1)
        moves = [(i, j, k) for i in range(4) for j in range(4) for k in range(2)][1:]
        moves.sort(key=lambda m: -(ring[m[0]] + ring[m[1]] + 0.3 * m[2]))
        return [xs[i] + ys[j] + cores[k] for i, j, k in moves]

    def reduce_start(a, values):
        mine = fold(values)
        part[a] = mine
        all_x[a, pl.ds(col, 1)] = mine.reshape(1, 1, CX)

        for peer in far_first_x():
            pltpu.make_async_remote_copy(
                src_ref=part.at[a], dst_ref=all_x.at[a, col],
                send_sem=ar_send.at[a, 0], recv_sem=ar_recv.at[a, 0],
                device_id={"gy": row, "gx": peer}, device_id_type=MESH,
            ).start()

    def reduce_middle(a):
        got = all_x.at[a, pl.ds(0, nx - 1)]
        pltpu.make_async_copy(got, got, ar_recv.at[a, 0]).wait()
        mine = jnp.sum(all_x[a], axis=0)
        part_y[a] = mine
        all_y[a, pl.ds(row, 1)] = mine.reshape(1, 1, CX)

        for i in sorted(range(1, ny), key=lambda i: -min(i, ny - i)):
            pltpu.make_async_remote_copy(
                src_ref=part_y.at[a], dst_ref=all_y.at[a, row],
                send_sem=ar_send.at[a, 1], recv_sem=ar_recv.at[a, 1],
                device_id=at(i, 0), device_id_type=MESH,
            ).start()

    def reduce_end(a):
        got = all_y.at[a, pl.ds(0, ny - 1)]
        pltpu.make_async_copy(got, got, ar_recv.at[a, 1]).wait()
        total = jnp.sum(all_y[a], axis=0)
        return [jnp.sum(jnp.where(lane // 32 == i, total, 0.0), axis=1, keepdims=True) for i in range(3)]

    def tell(level, distance):
        for axis, n in enumerate((ny, nx)):
            if n // 2 > distance:
                for d in (-distance, distance):
                    pl.semaphore_signal(
                        known.at[axis, level], inc=1,
                        device_id=at(d, 0) if axis == 0 else at(0, d), device_id_type=MESH,
                    )

    def hear(level, distance):
        for axis, n in enumerate((ny, nx)):
            if n // 2 > distance:
                pl.semaphore_wait(known.at[axis, level], 2)

    def keep_tv(p, slope):
        tv[p] = slope

    def advance(step):
        def body(p, c):
            u_ext[p] = u_ext[p] - step * g_ext[p]
            return c

        planes(body, 0)
        ux[...] = ux[...] - step * gx_halo[...]
        own_edge[0] = own_edge[0] - step * own_edge[1]

    def read_main(ext):
        return lambda p, start: ext[p, pl.ds(8 + start, 8), :]

    def read_field(field):
        return lambda p, start: field[p, pl.ds(start, 8), :]

    def packed_main(ext):
        return pack_columns(lambda p: ext[p, main, :])

    def add_main(p, extra):
        g_ext[p, main, :] = g_ext[p, main, :] + extra

    def finish_blur():
        sums = []

        def add(p, extra):
            h = grad[p] + extra
            grad[p] = h
            sums.append(rows8(h * h))

        with_fix(add)
        while len(sums) > 1:
            sums = [x + y for x, y in zip(sums[::2], sums[1::2])]
        return sums[0]

    def add_resid(p, extra):
        resid[p] = resid[p] + extra

    def keep_grad(p, t, value):
        grad[p, pl.ds(t * 8, 8), :] = value

    def keep_spread(p, value):
        spread[p] = value

    def gradient_inside():
        def body(p, c):
            g_ext[p, main, :] = spread[p] + WEIGHT_TV * tv[p] + DAMPING * u_ext[p, main, :]
            return c

        planes(body, 0)

    def send_gradient(r, edge):
        edge = fixed_columns(edge)
        own_edge[1] = edge
        return halo_send(r, lambda: fixed_rows(read_main(g_ext)), edge)

    def spread_and_slope(field):
        spread_inside(field, keep_spread)
        variation(u_ext, ux, own_edge[0], keep_tv)

    waiting = []
    clear_border(u_ext)
    edge = packed_main(u_ext)
    own_edge[0] = edge
    pl.semaphore_wait(barrier, len(SIDES))
    made = halo_send(0, lambda: edge_rows(read_main(u_ext)), edge)
    waiting += made
    table_loads[0].wait()
    table_loads[1].wait()
    number = tiles[row, col]
    depth = [prof[a, 0, number] for a in range(TAPS)]
    along = [prof[a, 1, number] for a in range(TAPS)]
    across = [prof[a, 2, number] for a in range(TAPS)]
    prepare()

    def keep_residual(p, t, value):
        resid[p, pl.ds(t * 8, 8), :] = value - u_ext[p, pl.ds(8 + t * 8, 8), :]

    blur_inside(u_ext, keep_residual)
    edge = pack_columns(lambda p: resid[p])
    halo_fix(0, made, u_ext, ux)
    made = spill_send(1, lambda: fixed_rows(read_field(resid)), fixed_columns(edge))
    waiting += made
    tell(0, 2)
    with_fix(add_resid)
    spread_and_slope(resid)
    gradient_inside()
    edge = packed_main(g_ext)
    spill_fix(1, made)
    made = send_gradient(2, edge)
    waiting += made
    hear(0, 2)
    tell(1, 4)
    with_fix(add_main)
    clear_border(g_ext)
    blur_inside(g_ext, keep_grad)
    gg, gt = tension_inside()
    sums = []

    def tension():
        tension_border()
        sums.append(tension_sum(START_STEP))

    halo_fix(2, made, g_ext, gx_halo, tension)
    hear(1, 4)
    tell(2, 8)
    hh = finish_blur()
    gt = sums[0] - gt
    hear(2, 8)
    reduce_start(0, (gg, hh, gt))

    def next_residual(p, c):
        resid[p] = resid[p] - START_STEP * grad[p]
        return c

    planes(next_residual, 0)
    made = spill_send(3, lambda: edge_rows(read_field(resid)), pack_columns(lambda p: resid[p]))
    waiting += made
    advance(START_STEP)
    spread_and_slope(resid)
    gradient_inside()
    edge = packed_main(g_ext)
    spill_fix(3, made)
    made = send_gradient(4, edge)
    waiting += made
    reduce_middle(0)

    def keep_pulled(p, extra):
        add_main(p, extra)
        resid[p] = spread[p] + extra

    with_fix(keep_pulled)
    clear_border(g_ext)
    blur_inside(g_ext, keep_grad)
    gg, gt = tension_inside()
    halo_fix(4, made, g_ext, gx_halo, tension_border)
    hh = finish_blur()
    g2, h2, t2 = reduce_end(0)
    change_sq = START_STEP * START_STEP * g2
    change_growth = START_STEP * START_STEP * (h2 + DAMPING * g2) - START_STEP * WEIGHT_TV * t2
    step = change_sq / change_growth

    gt = tension_sum(step) - gt
    reduce_start(1, (gg, hh, gt))

    made = spill_send(5, lambda: edge_rows(read_field(grad)), pack_columns(lambda p: grad[p]))
    waiting += made
    advance(step)
    spread_and_slope(grad)
    spill_fix(5, made)
    reduce_middle(1)

    def last(p, extra):
        pulled = resid[p] - step * (spread[p] + extra)
        u = u_ext[p, main, :]
        u_out[p] = u
        g_out[p] = pulled + WEIGHT_TV * tv[p] + DAMPING * u

    with_fix(last)
    for c in waiting:
        c.wait_send()
    for a in range(2):
        got = all_x.at[a, pl.ds(0, nx - 1)]
        pltpu.make_async_copy(got, got, ar_send.at[a, 0]).wait()
        got = all_y.at[a, pl.ds(0, ny - 1)]
        pltpu.make_async_copy(got, got, ar_send.at[a, 1]).wait()
    g2, h2, t2 = reduce_end(1)
    change_sq = step * step * g2
    change_growth = step * step * (h2 + DAMPING * g2) - step * WEIGHT_TV * t2
    step_out[...] = jnp.broadcast_to(change_sq / change_growth, (1, CX))


def per_device(ny, nx, observed, profiles, tile_index):
    field = pltpu.VMEM((Z, CY, CX), F32)
    extended = pltpu.VMEM((Z, EXT, CX), F32)
    matrix = pltpu.VMEM((2 * CX, 2 * CX), BF16)
    rounds = 6
    scratch = [
        pltpu.SMEM((TAPS, 3, profiles.shape[0]), F32), pltpu.SMEM((ny, nx), jnp.int32),
        extended, extended, field, field, field,
        pltpu.VMEM((Z, CY + 32, CX), F32), field,
        pltpu.VMEM((Z * CY, CX), F32), pltpu.VMEM((40, CX), F32),
        matrix, matrix, matrix, matrix,
        pltpu.VMEM((Z, 16, CX), F32), pltpu.VMEM((Z * 8, CX), F32), pltpu.VMEM((CY, CX), F32),
        field, field, field, field,
        pltpu.VMEM((EXT, CX), F32), pltpu.VMEM((EXT, CX), F32),
        pltpu.VMEM((2, CY, CX), F32), pltpu.VMEM((CY + 32, CX), F32),
        pltpu.VMEM((rounds, 2, 8, 8, CX), F32), pltpu.VMEM((rounds, 2, 8, 8, CX), F32),
        pltpu.VMEM((rounds, EXT, CX), F32), pltpu.VMEM((rounds, 2, EXT, CX), F32),
        pltpu.VMEM((2, 1, CX), F32), pltpu.VMEM((2, nx, 1, CX), F32),
        pltpu.VMEM((2, 1, CX), F32), pltpu.VMEM((2, ny, 1, CX), F32),
        pltpu.SemaphoreType.DMA, pltpu.SemaphoreType.DMA((2,)),
        pltpu.SemaphoreType.DMA((rounds, 8)), pltpu.SemaphoreType.DMA((rounds, 8)),
        pltpu.SemaphoreType.DMA((2, 2)), pltpu.SemaphoreType.DMA((2, 2)),
        pltpu.SemaphoreType.REGULAR((2, 3)),
    ]
    whole = pltpu.VMEM((Z, CY, CX), F32)
    estimate, gradient, step = pl.pallas_call(
        functools.partial(kernel, ny, nx),
        out_shape=(whole, whole, pltpu.VMEM((1, CX), F32)),
        in_specs=[pl.BlockSpec(memory_space=pltpu.HBM)] * 3,
        out_specs=(pl.BlockSpec(memory_space=pltpu.VMEM),) * 3,
        scratch_shapes=scratch,
        compiler_params=pltpu.CompilerParams(
            collective_id=0, has_side_effects=True
        ),
    )(observed, jnp.transpose(profiles, (2, 1, 0)), tile_index)
    return pl.pallas_call(
        last_update,
        out_shape=jax.ShapeDtypeStruct((Z, CY, CX), F32),
        in_specs=[pl.BlockSpec(memory_space=pltpu.VMEM)] * 3,
        out_specs=pl.BlockSpec(memory_space=pltpu.VMEM),
        compiler_params=pltpu.CompilerParams(vmem_limit_bytes=24 << 20),
    )(estimate, gradient, step)


def last_update(u, g, step, out_ref):
    t = step[...]
    for p in range(Z):
        out_ref[p] = u[p] - t * g[p]


def solution(mesh):
    ny, nx = mesh.shape["gy"], mesh.shape["gx"]
    return jax.shard_map(
        functools.partial(per_device, ny, nx), mesh=mesh,
        in_specs=(P(None, "gy", "gx"), P(), P()),
        out_specs=P(None, "gy", "gx"), check_vma=False,
    )
```

```python
import functools

import jax
import jax.numpy as jnp
from jax import lax
from jax.experimental import pallas as pl
from jax.experimental.pallas import tpu as pltpu
from jax.sharding import PartitionSpec as P

WEIGHT_TV = 0.02
SMOOTHING = 0.1
DAMPING = 0.05
START_STEP = 0.5
RADIUS = 4
TAPS = 9
Z, CY, CX = 16, 32, 128
EXT = CY + 16
MESH = pl.DeviceIdType.MESH
F32 = jnp.float32
BF16 = jnp.bfloat16
SIDES = ((-1, 0), (1, 0), (0, -1), (0, 1), (-1, -1), (-1, 1), (1, -1), (1, 1))


def kernel(
    ny, nx,
    obs_hbm, prof_hbm, tiles_hbm, u_out, g_out, step_out,
    prof, tiles,
    u_ext, g_ext, grad, tv, resid, back, spread, blur_y, flux,
    fwd, bwd, side_fwd, side_bwd, twice, y_fix, x_fix,
    across_u, square, product, growth,
    ux, gx_halo, own_edge, edge_pad,
    send_y, recv_y, send_x, recv_x,
    part, all_x, part_y, all_y,
    load_sem, table_sem, send_sem, recv_sem, ar_send, ar_recv, known,
):
    row = lax.axis_index("gy")
    col = lax.axis_index("gx")

    def at(dy, dx):
        return {
            "gy": lax.rem(row + dy + ny, ny),
            "gx": lax.rem(col + dx + nx, nx),
        }

    load = pltpu.make_async_copy(obs_hbm, u_ext.at[:, pl.ds(8, CY), :], load_sem)
    load.start()
    table_loads = (
        pltpu.make_async_copy(prof_hbm, prof, table_sem.at[0]),
        pltpu.make_async_copy(tiles_hbm, tiles, table_sem.at[1]),
    )
    table_loads[0].start()
    table_loads[1].start()

    barrier = pltpu.get_barrier_semaphore()

    for dy, dx in SIDES:
        pl.semaphore_signal(barrier, inc=1, device_id=at(dy, dx), device_id_type=MESH)

    lane = lax.broadcasted_iota(jnp.int32, (1, CX), 1)
    sub8 = lax.broadcasted_iota(jnp.int32, (8, CX), 0)
    low_half = sub8 < 4
    plane_of = lane // 8
    place = lane - plane_of * 8
    first_row, last_row = row == 0, row == ny - 1
    first_col, last_col = col == 0, col == nx - 1

    back[:, pl.ds(0, 16), :] = jnp.zeros((Z, 16, CX), F32)
    back[:, pl.ds(16 + CY, 16), :] = jnp.zeros((Z, 16, CX), F32)
    edge_pad[pl.ds(0, 16), :] = jnp.zeros((16, CX), F32)
    edge_pad[pl.ds(16 + CY, 16), :] = jnp.zeros((16, CX), F32)
    load.wait()

    def halves(value):
        high = value.astype(BF16)
        return high, (value - high.astype(F32)).astype(BF16)

    def prepare():
        mk = lax.broadcasted_iota(jnp.int32, (CX, CX), 0)
        mn = lax.broadcasted_iota(jnp.int32, (CX, CX), 1)

        def band(diff, taps, keep=None):
            total = jnp.zeros((CX, CX), F32)
            for c in range(TAPS):
                total = jnp.where(diff == c - RADIUS, taps[c], total)
            return total if keep is None else jnp.where(keep, total, 0.0)

        ahead = mn - mk
        planes_ahead = mn // 8 - mk // 8
        places_ahead = ahead - 8 * planes_ahead
        crossing = (mn // 4 + mk // 4) % 2 == 1
        for ref, sign in ((fwd, 1), (bwd, -1)):
            split_matrix(ref, band(sign * ahead, across))
        for ref, sign in ((side_fwd, 1), (side_bwd, -1)):
            split_matrix(
                ref, band(sign * planes_ahead, depth) * band(sign * places_ahead, across, crossing)
            )

    def split_matrix(ref, w):
        high, low = halves(w)
        ref[pl.ds(0, CX), pl.ds(0, CX)] = high
        ref[pl.ds(CX, CX), pl.ds(0, CX)] = high
        ref[pl.ds(0, CX), pl.ds(CX, CX)] = low
        ref[pl.ds(CX, CX), pl.ds(CX, CX)] = jnp.zeros((CX, CX), BF16)

    def times(value, ref):
        high, low = halves(value)
        both = jnp.dot(jnp.concatenate([high, low], axis=1), ref[...], preferred_element_type=F32)
        return both[:, 0:CX] + both[:, CX : 2 * CX]

    def planes(body, init, step=4):
        if step == Z:
            for p in range(Z):
                init = body(p, init)
            return init

        def some(i, carry):
            for k in range(step):
                carry = body(i * step + k, carry)
            return carry

        return lax.fori_loop(0, Z // step, some, init)

    def pack_columns(read):
        def body(p, total):
            turned = pltpu.roll(read(p), 8 * p + 4, 1)
            return jnp.where(plane_of == p, turned, total)

        return planes(body, jnp.zeros((CY, CX), F32), Z)

    def copies(r):
        made = []
        for k, (dy, dx) in enumerate(SIDES):
            if dx == 0:
                src = send_y.at[r, 0 if dy < 0 else 1]
                dst = recv_y.at[r, 1 if dy < 0 else 0]
            else:
                start, size = {-1: (0, 8), 0: (8, CY), 1: (8 + CY, 8)}[dy]
                land = {-1: 8 + CY, 0: 8, 1: 0}[dy]
                src = send_x.at[r, pl.ds(start, size), :]
                dst = recv_x.at[r, 1 if dx < 0 else 0, pl.ds(land, size), :]
            made.append(
                pltpu.make_async_remote_copy(
                    src_ref=src, dst_ref=dst,
                    send_sem=send_sem.at[r, k], recv_sem=recv_sem.at[r, k],
                    device_id=at(dy, dx), device_id_type=MESH,
                )
            )
        return made

    def send_columns(r):
        made = copies(r)
        for k in (4, 5, 6, 7, 2, 3):
            made[k].start()
        return made

    def send_rows(made):
        for k in (0, 1):
            made[k].start()
        return made

    def wait_rows(made):
        made[0].wait_recv()
        made[1].wait_recv()

    def wait_columns(made):
        for k in (2, 3, 4, 5, 6, 7):
            made[k].wait_recv()

    border = (lane < 4) | (lane >= CX - 4)

    def mixing(taps):
        limits = {1: (sub8 <= 0, 5), 2: (sub8 <= 1, 6), 3: (sub8 <= 2, 7), 5: (sub8 >= 5, 1), 6: (sub8 >= 6, 2), 7: (sub8 >= 7, 3)}
        weights = {s: jnp.where(mask, taps[b], 0.0) for s, (mask, b) in limits.items()}
        weights[4] = jnp.where(low_half, taps[8], taps[0])
        return weights

    def put_rows(rows, first, second):
        for q in range(8):
            a, b = rows[q], pltpu.roll(rows[q + 8], 4, 0)
            first[q] = jnp.where(low_half, a, b)
            second[q] = jnp.where(low_half, b, a)

    def get_rows(first, second, no_first, no_second):
        near, far = [], []
        for q in range(8):
            a = jnp.where(no_first, 0.0, first[q])
            b = jnp.where(no_second, 0.0, second[q])
            near.append(jnp.where(low_half, a, b))
            far.append(pltpu.roll(jnp.where(low_half, b, a), 4, 0))
        return near + far

    def cross(rows, taps, transposed, ref):
        for p in range(Z):
            twice[p, pl.ds(0, 8), :] = rows[p]
            twice[p, pl.ds(8, 8), :] = rows[p]
        weights = mixing(taps)
        mixed = []
        for p in range(Z):
            total = weights[4] * twice[p, pl.ds(4, 8), :]
            for s in (1, 2, 3, 5, 6, 7):
                total = total + weights[s] * twice[p, pl.ds(8 - s, 8), :]
            mixed.append(total)
        return times(jnp.concatenate(depth_sum(mixed, transposed), axis=0), ref)

    def edge_rows(read):
        return [jnp.where(low_half, read(p, 0), read(p, CY - 8)) for p in range(Z)]

    def halo_send(r, rows, edge):
        send_x[r, pl.ds(8, CY), :] = edge
        send_x[r, pl.ds(0, 8), :] = edge[0:8]
        send_x[r, pl.ds(8 + CY, 8), :] = edge[CY - 8 : CY]
        made = send_columns(r)
        put_rows(rows(), send_y.at[r, 0], send_y.at[r, 1])
        return send_rows(made)

    def halo_fix(r, made, ext, halo, between=None):
        wait_rows(made)
        rows = get_rows(recv_y.at[r, 1], recv_y.at[r, 0], last_row, first_row)
        for p in range(Z):
            ext[p, pl.ds(0, 8), :] = rows[p]
            ext[p, pl.ds(8 + CY, 8), :] = rows[p]
        y_fix[...] = cross(rows, along, False, fwd)
        if between is not None:
            made[2].wait_recv()
            made[3].wait_recv()
            halo[pl.ds(8, CY), :] = sides(r, place < 4, 8, CY)
            between()
            for k in (4, 5, 6, 7):
                made[k].wait_recv()
        else:
            wait_columns(made)
        halo[...] = sides(r, place < 4)
        edge = along[0] * halo[pl.ds(8 + RADIUS, CY), :]
        for b in range(1, TAPS):
            edge = edge + along[b] * halo[pl.ds(8 + RADIUS - b, CY), :]
        x_fix[...] = times(edge, side_fwd)

    def spill_send(r, rows, edge):
        edge_pad[pl.ds(16, CY), :] = times(edge, side_bwd)
        total = along[0] * edge_pad[pl.ds(4, EXT), :]
        for b in range(1, TAPS):
            total = total + along[b] * edge_pad[pl.ds(4 + b, EXT), :]
        send_x[r] = total
        made = send_columns(r)
        spilled = cross(rows(), along[::-1], True, bwd)
        put_rows([spilled[8 * p : 8 * p + 8] for p in range(Z)], send_y.at[r, 1], send_y.at[r, 0])
        return send_rows(made)

    def spill_fix(r, made):
        wait_rows(made)
        rows = get_rows(recv_y.at[r, 0], recv_y.at[r, 1], first_row, last_row)
        y_fix[...] = jnp.concatenate(rows, axis=0)
        wait_columns(made)
        both = sides(r, place >= 4)
        x_fix[pl.ds(0, 8), :] = both[8:16] + both[0:8]
        x_fix[pl.ds(8, 16), :] = both[16:CY]
        x_fix[pl.ds(24, 8), :] = both[CY : CY + 8] + both[CY + 8 : CY + 16]

    def packed_rows_fix():
        packed = jnp.zeros((8, CX), F32)
        for p in range(Z):
            packed = jnp.where(plane_of == p, pltpu.roll(y_fix[pl.ds(8 * p, 8), :], 8 * p + 4, 1), packed)
        return packed

    def fixed_columns(edge):
        packed = packed_rows_fix()
        edge = edge + x_fix[...]
        top = edge[0:8] + jnp.where(low_half, packed, 0.0)
        low = edge[CY - 8 : CY] + jnp.where(low_half, 0.0, packed)
        return jnp.concatenate([top, edge[8 : CY - 8], low], axis=0)

    def fixed_rows(read):
        ends = jnp.where(low_half, x_fix[pl.ds(0, 8), :], x_fix[pl.ds(CY - 8, 8), :])
        rows = edge_rows(read)
        for p in range(Z):
            extra = jnp.where(border, pltpu.roll(ends, 124 - 8 * p, 1), 0.0)
            rows[p] = rows[p] + y_fix[pl.ds(8 * p, 8), :] + extra
        return rows

    def with_fix(add):
        extra = x_fix[...]
        for p in range(Z):
            e = jnp.where(border, pltpu.roll(extra, 124 - 8 * p, 1), 0.0)
            y = y_fix[pl.ds(8 * p, 8), :]
            top = e[0:8] + jnp.where(low_half, y, 0.0)
            low = e[CY - 8 : CY] + jnp.where(low_half, 0.0, y)
            add(p, jnp.concatenate([top, e[8 : CY - 8], low], axis=0))

    def sides(r, from_left, start=0, size=EXT):
        left = jnp.where(first_col, 0.0, recv_x[r, 0, pl.ds(start, size), :])
        right = jnp.where(last_col, 0.0, recv_x[r, 1, pl.ds(start, size), :])
        both = jnp.where(from_left, left, right)
        if size < EXT:
            return both
        at_row = lax.broadcasted_iota(jnp.int32, (EXT, CX), 0)
        both = jnp.where(first_row & (at_row < 8), 0.0, both)
        return jnp.where(last_row & (at_row >= 8 + CY), 0.0, both)

    def depth_sum(value, transposed):
        out = []
        for p in range(Z):
            total = None
            for a in range(TAPS):
                source = p - RADIUS + a if transposed else p + RADIUS - a
                if 0 <= source < Z:
                    term = depth[a] * value[source]
                    total = term if total is None else total + term
            out.append(total)
        return out

    def clear_border(ext):
        for p in range(Z):
            ext[p, pl.ds(0, 8), :] = jnp.zeros((8, CX), F32)
            ext[p, pl.ds(8 + CY, 8), :] = jnp.zeros((8, CX), F32)

    def blur_inside(ext, write):
        for group in range(4):
            rows = []
            for p in range(4 * group, 4 * group + 4):
                total = along[0] * ext[p, pl.ds(8 + RADIUS, CY), :]
                for b in range(1, TAPS):
                    total = total + along[b] * ext[p, pl.ds(8 + RADIUS - b, CY), :]
                rows.append(total)
            blur_y[pl.ds(group * 128, 128), :] = times(jnp.concatenate(rows, axis=0), fwd)
        for t in range(CY // 8):
            value = [blur_y[pl.ds(p * CY + t * 8, 8), :] for p in range(Z)]
            for p, total in enumerate(depth_sum(value, False)):
                write(p, t, total)

    def spread_inside(field, write):
        for t in range(CY // 8):
            value = [field[p, pl.ds(t * 8, 8), :] for p in range(Z)]
            out = times(jnp.concatenate(depth_sum(value, True), axis=0), bwd)
            for p in range(Z):
                back[p, pl.ds(16 + t * 8, 8), :] = out[8 * p : 8 * p + 8]

        for p in range(Z):
            total = along[0] * back[p, pl.ds(12, CY), :]
            for b in range(1, TAPS):
                total = total + along[b] * back[p, pl.ds(12 + b, CY), :]
            write(p, total)

    zero8 = jnp.zeros((8, CX), F32)
    main = pl.ds(8, CY)
    rows40 = lax.broadcasted_iota(jnp.int32, (40, CX), 0)
    rows32 = lax.broadcasted_iota(jnp.int32, (CY, CX), 0)
    no_row_diff = last_row & (rows40 == 39)
    no_row_flux = first_row & (rows40 == 7)
    no_col_diff = last_col & (lane == CX - 1)

    def inverse_size(dx, dy, dz):
        return lax.rsqrt(dx * dx + dy * dy + dz * dz + SMOOTHING * SMOOTHING)

    def variation(ext, halo, edges, write):
        here = halo[pl.ds(8, CY), :]
        dx = pltpu.roll(edges, CX - 1, 1) - here
        dy = halo[pl.ds(9, CY), :] - here
        dy = jnp.where(last_row & (rows32 == CY - 1), 0.0, dy)
        dz = jnp.where(plane_of == Z - 1, 0.0, pltpu.roll(here, CX - 8, 1) - here)
        side = jnp.where(first_col, 0.0, dx * inverse_size(dx, dy, dz))
        around = halo[pl.ds(0, 40), :]

        def body(p, before):
            u = ext[p, pl.ds(0, 40), :]
            dy = jnp.where(no_row_diff, 0.0, ext[p, pl.ds(1, 40), :] - u)
            beyond = pltpu.roll(around, 124 - 8 * p, 1)
            dx = pltpu.roll(jnp.where(lane == 0, beyond, u), CX - 1, 1) - u
            dx = jnp.where(no_col_diff, 0.0, dx)
            after = ext[min(p + 1, Z - 1) if isinstance(p, int) else jnp.minimum(p + 1, Z - 1), pl.ds(0, 40), :]
            dz = after - u
            inverse = inverse_size(dx, dy, dz)
            fy = jnp.where(no_row_flux, 0.0, dy * inverse)
            flux[...] = fy
            fx = (dx * inverse)[8:40]
            fz = (dz * inverse)[8:40]
            fx_side = pltpu.roll(side, 124 - 8 * p, 1)
            fx_before = pltpu.roll(jnp.where(lane == CX - 1, fx_side, fx), 1, 1)
            slope = (before - fz) + (flux[pl.ds(7, CY), :] - fy[8:40]) + (fx_before - fx)
            write(p, slope)
            return fz

        planes(body, jnp.zeros((CY, CX), F32), 4)

    def rows8(value):
        return value[0:8] + value[8:16] + value[16:24] + value[24:32]

    final_lane = lane == CX - 1
    next_lane = final_lane & jnp.logical_not(last_col)
    next_row = (sub8 == 7) & jnp.logical_not(last_row)

    def tension_inside():
        around = ux[pl.ds(8, CY), :]

        def body(p, total):
            u, g = u_ext[p, main, :], g_ext[p, main, :]
            after = min(p + 1, Z - 1) if isinstance(p, int) else jnp.minimum(p + 1, Z - 1)
            dz = u_ext[after, main, :] - u
            ez = g_ext[after, main, :] - g
            dy = jnp.where(last_row & (rows32 == CY - 1), 0.0, u_ext[p, pl.ds(9, CY), :] - u)
            ey = jnp.where(rows32 == CY - 1, 0.0, g_ext[p, pl.ds(9, CY), :] - g)
            beyond = pltpu.roll(around, 124 - 8 * p, 1)
            dx = pltpu.roll(jnp.where(lane == 0, beyond, u), CX - 1, 1) - u
            dx = jnp.where(no_col_diff, 0.0, dx)
            ex = jnp.where(final_lane, 0.0, pltpu.roll(g, CX - 1, 1) - g)
            across_u[p] = dx
            square[p] = dx * dx + dy * dy + dz * dz + SMOOTHING * SMOOTHING
            product[p] = dx * ex + dy * ey + dz * ez
            growth[p] = ex * ex + ey * ey + ez * ez
            return total[0] + rows8(g * g), total[1] + rows8(g * tv[p])

        return planes(body, (zero8, zero8))

    def tension_border():
        around = gx_halo[pl.ds(8, CY), :]
        for p in range(Z):
            ex = jnp.where(next_lane, pltpu.roll(around, 123 - 8 * p, 1) - g_ext[p, main, :], 0.0)
            product[p] = product[p] + across_u[p] * ex
            growth[p] = growth[p] + ex * ex
            bottom = pl.ds(CY - 8, 8)
            ey = jnp.where(next_row, g_ext[p, pl.ds(CY + 1, 8), :] - g_ext[p, pl.ds(CY, 8), :], 0.0)
            dy = u_ext[p, pl.ds(CY + 1, 8), :] - u_ext[p, pl.ds(CY, 8), :]
            product[p, bottom, :] = product[p, bottom, :] + dy * ey
            growth[p, bottom, :] = growth[p, bottom, :] + ey * ey

    def tension_sum(step):
        total = zero8
        for p in range(Z):
            part_ = product[p] - step * growth[p]
            size = square[p] - step * (product[p] + part_)
            size = jnp.maximum(size, SMOOTHING * SMOOTHING)
            total = total + rows8(part_ * lax.rsqrt(size))
        return total

    def fold(values):
        total = jnp.zeros((1, CX), F32)
        for i, value in enumerate(values):
            v = jnp.sum(value, axis=0, keepdims=True)
            v = v + pltpu.roll(v, 64, 1)
            v = v + pltpu.roll(v, 32, 1)
            total = jnp.where(lane // 32 == i, v, total)
        return total

    def far_first_x():
        if nx != 32:
            return [lax.rem(col + i, nx) for i in range(1, nx)]
        x, y, core = col // 8, lax.rem(col // 2, 4), lax.rem(col, 2)
        xs = [lax.rem(x + i, 4) * 8 for i in range(4)]
        ys = [lax.rem(y + i, 4) * 2 for i in range(4)]
        cores = [core, 1 - core]
        ring = (0, 1, 2, 1)
        moves = [(i, j, k) for i in range(4) for j in range(4) for k in range(2)][1:]
        moves.sort(key=lambda m: -(ring[m[0]] + ring[m[1]] + 0.3 * m[2]))
        return [xs[i] + ys[j] + cores[k] for i, j, k in moves]

    def reduce_start(a, values):
        mine = fold(values)
        part[a] = mine
        all_x[a, pl.ds(col, 1)] = mine.reshape(1, 1, CX)

        for peer in far_first_x():
            pltpu.make_async_remote_copy(
                src_ref=part.at[a], dst_ref=all_x.at[a, col],
                send_sem=ar_send.at[a, 0], recv_sem=ar_recv.at[a, 0],
                device_id={"gy": row, "gx": peer}, device_id_type=MESH,
            ).start()

    def reduce_middle(a):
        got = all_x.at[a, pl.ds(0, nx - 1)]
        pltpu.make_async_copy(got, got, ar_recv.at[a, 0]).wait()
        mine = jnp.sum(all_x[a], axis=0)
        part_y[a] = mine
        all_y[a, pl.ds(row, 1)] = mine.reshape(1, 1, CX)

        for i in sorted(range(1, ny), key=lambda i: -min(i, ny - i)):
            pltpu.make_async_remote_copy(
                src_ref=part_y.at[a], dst_ref=all_y.at[a, row],
                send_sem=ar_send.at[a, 1], recv_sem=ar_recv.at[a, 1],
                device_id=at(i, 0), device_id_type=MESH,
            ).start()

    def reduce_end(a):
        got = all_y.at[a, pl.ds(0, ny - 1)]
        pltpu.make_async_copy(got, got, ar_recv.at[a, 1]).wait()
        total = jnp.sum(all_y[a], axis=0)
        return [jnp.sum(jnp.where(lane // 32 == i, total, 0.0), axis=1, keepdims=True) for i in range(3)]

    def tell(level, distance, axes=(0, 1)):
        for axis, n in enumerate((ny, nx)):
            if axis in axes and n // 2 > distance:
                for d in (-distance, distance):
                    pl.semaphore_signal(
                        known.at[axis, level], inc=1,
                        device_id=at(d, 0) if axis == 0 else at(0, d), device_id_type=MESH,
                    )

    def hear(level, distance, axes=(0, 1)):
        for axis, n in enumerate((ny, nx)):
            if axis in axes and n // 2 > distance:
                pl.semaphore_wait(known.at[axis, level], 2)

    def keep_tv(p, slope):
        tv[p] = slope

    def advance(step):
        def body(p, c):
            u_ext[p] = u_ext[p] - step * g_ext[p]
            return c

        planes(body, 0)
        ux[...] = ux[...] - step * gx_halo[...]
        own_edge[0] = own_edge[0] - step * own_edge[1]

    def read_main(ext):
        return lambda p, start: ext[p, pl.ds(8 + start, 8), :]

    def read_field(field):
        return lambda p, start: field[p, pl.ds(start, 8), :]

    def packed_main(ext):
        return pack_columns(lambda p: ext[p, main, :])

    def add_main(p, extra):
        g_ext[p, main, :] = g_ext[p, main, :] + extra

    def finish_blur():
        sums = []

        def add(p, extra):
            h = grad[p] + extra
            grad[p] = h
            sums.append(rows8(h * h))

        with_fix(add)
        while len(sums) > 1:
            sums = [x + y for x, y in zip(sums[::2], sums[1::2])]
        return sums[0]

    def add_resid(p, extra):
        resid[p] = resid[p] + extra

    def keep_grad(p, t, value):
        grad[p, pl.ds(t * 8, 8), :] = value

    def keep_spread(p, value):
        spread[p] = value

    def gradient_inside():
        def body(p, c):
            g_ext[p, main, :] = spread[p] + WEIGHT_TV * tv[p] + DAMPING * u_ext[p, main, :]
            return c

        planes(body, 0)

    def send_gradient(r, edge):
        edge = fixed_columns(edge)
        own_edge[1] = edge
        return halo_send(r, lambda: fixed_rows(read_main(g_ext)), edge)

    def spread_and_slope(field):
        spread_inside(field, keep_spread)
        variation(u_ext, ux, own_edge[0], keep_tv)

    waiting = []
    clear_border(u_ext)
    edge = packed_main(u_ext)
    own_edge[0] = edge
    pl.semaphore_wait(barrier, len(SIDES))
    made = halo_send(0, lambda: edge_rows(read_main(u_ext)), edge)
    waiting += made
    table_loads[0].wait()
    table_loads[1].wait()
    number = tiles[row, col]
    depth = [prof[a, 0, number] for a in range(TAPS)]
    along = [prof[a, 1, number] for a in range(TAPS)]
    across = [prof[a, 2, number] for a in range(TAPS)]
    prepare()

    def keep_residual(p, t, value):
        resid[p, pl.ds(t * 8, 8), :] = value - u_ext[p, pl.ds(8 + t * 8, 8), :]

    blur_inside(u_ext, keep_residual)
    edge = pack_columns(lambda p: resid[p])
    halo_fix(0, made, u_ext, ux)
    made = spill_send(1, lambda: fixed_rows(read_field(resid)), fixed_columns(edge))
    waiting += made
    tell(0, 2)
    with_fix(add_resid)
    spread_and_slope(resid)
    gradient_inside()
    edge = packed_main(g_ext)
    spill_fix(1, made)
    made = send_gradient(2, edge)
    waiting += made
    hear(0, 2)
    tell(1, 4)
    with_fix(add_main)
    clear_border(g_ext)
    blur_inside(g_ext, keep_grad)
    gg, gt = tension_inside()
    hear(1, 4, (1,))
    tell(2, 8)
    sums = []

    def tension():
        tension_border()
        sums.append(tension_sum(START_STEP))

    halo_fix(2, made, g_ext, gx_halo, tension)
    hh = finish_blur()
    gt = sums[0] - gt
    hear(2, 8)
    reduce_start(0, (gg, hh, gt))

    def next_residual(p, c):
        resid[p] = resid[p] - START_STEP * grad[p]
        return c

    planes(next_residual, 0)
    made = spill_send(3, lambda: edge_rows(read_field(resid)), pack_columns(lambda p: resid[p]))
    waiting += made
    advance(START_STEP)
    spread_and_slope(resid)
    gradient_inside()
    edge = packed_main(g_ext)
    hear(1, 4, (0,))
    reduce_middle(0)
    spill_fix(3, made)
    made = send_gradient(4, edge)
    waiting += made

    def keep_pulled(p, extra):
        add_main(p, extra)
        resid[p] = spread[p] + extra

    with_fix(keep_pulled)
    clear_border(g_ext)
    blur_inside(g_ext, keep_grad)
    gg, gt = tension_inside()
    halo_fix(4, made, g_ext, gx_halo, tension_border)
    hh = finish_blur()
    g2, h2, t2 = reduce_end(0)
    change_sq = START_STEP * START_STEP * g2
    change_growth = START_STEP * START_STEP * (h2 + DAMPING * g2) - START_STEP * WEIGHT_TV * t2
    step = change_sq / change_growth

    gt = tension_sum(step) - gt
    reduce_start(1, (gg, hh, gt))

    made = spill_send(5, lambda: edge_rows(read_field(grad)), pack_columns(lambda p: grad[p]))
    waiting += made
    advance(step)
    spread_and_slope(grad)
    reduce_middle(1)
    spill_fix(5, made)

    def last(p, extra):
        pulled = resid[p] - step * (spread[p] + extra)
        u = u_ext[p, main, :]
        u_out[p] = u
        g_out[p] = pulled + WEIGHT_TV * tv[p] + DAMPING * u

    with_fix(last)
    for c in waiting:
        c.wait_send()
    for a in range(2):
        got = all_x.at[a, pl.ds(0, nx - 1)]
        pltpu.make_async_copy(got, got, ar_send.at[a, 0]).wait()
        got = all_y.at[a, pl.ds(0, ny - 1)]
        pltpu.make_async_copy(got, got, ar_send.at[a, 1]).wait()
    g2, h2, t2 = reduce_end(1)
    change_sq = step * step * g2
    change_growth = step * step * (h2 + DAMPING * g2) - step * WEIGHT_TV * t2
    step_out[...] = jnp.broadcast_to(change_sq / change_growth, (1, CX))


def per_device(ny, nx, observed, profiles, tile_index):
    field = pltpu.VMEM((Z, CY, CX), F32)
    extended = pltpu.VMEM((Z, EXT, CX), F32)
    matrix = pltpu.VMEM((2 * CX, 2 * CX), BF16)
    rounds = 6
    scratch = [
        pltpu.SMEM((TAPS, 3, profiles.shape[0]), F32), pltpu.SMEM((ny, nx), jnp.int32),
        extended, extended, field, field, field,
        pltpu.VMEM((Z, CY + 32, CX), F32), field,
        pltpu.VMEM((Z * CY, CX), F32), pltpu.VMEM((40, CX), F32),
        matrix, matrix, matrix, matrix,
        pltpu.VMEM((Z, 16, CX), F32), pltpu.VMEM((Z * 8, CX), F32), pltpu.VMEM((CY, CX), F32),
        field, field, field, field,
        pltpu.VMEM((EXT, CX), F32), pltpu.VMEM((EXT, CX), F32),
        pltpu.VMEM((2, CY, CX), F32), pltpu.VMEM((CY + 32, CX), F32),
        pltpu.VMEM((rounds, 2, 8, 8, CX), F32), pltpu.VMEM((rounds, 2, 8, 8, CX), F32),
        pltpu.VMEM((rounds, EXT, CX), F32), pltpu.VMEM((rounds, 2, EXT, CX), F32),
        pltpu.VMEM((2, 1, CX), F32), pltpu.VMEM((2, nx, 1, CX), F32),
        pltpu.VMEM((2, 1, CX), F32), pltpu.VMEM((2, ny, 1, CX), F32),
        pltpu.SemaphoreType.DMA, pltpu.SemaphoreType.DMA((2,)),
        pltpu.SemaphoreType.DMA((rounds, 8)), pltpu.SemaphoreType.DMA((rounds, 8)),
        pltpu.SemaphoreType.DMA((2, 2)), pltpu.SemaphoreType.DMA((2, 2)),
        pltpu.SemaphoreType.REGULAR((2, 3)),
    ]
    whole = pltpu.VMEM((Z, CY, CX), F32)
    estimate, gradient, step = pl.pallas_call(
        functools.partial(kernel, ny, nx),
        out_shape=(whole, whole, pltpu.VMEM((1, CX), F32)),
        in_specs=[pl.BlockSpec(memory_space=pltpu.HBM)] * 3,
        out_specs=(pl.BlockSpec(memory_space=pltpu.VMEM),) * 3,
        scratch_shapes=scratch,
        compiler_params=pltpu.CompilerParams(
            collective_id=0, has_side_effects=True
        ),
    )(observed, jnp.transpose(profiles, (2, 1, 0)), tile_index)
    return pl.pallas_call(
        last_update,
        out_shape=jax.ShapeDtypeStruct((Z, CY, CX), F32),
        in_specs=[pl.BlockSpec(memory_space=pltpu.VMEM)] * 3,
        out_specs=pl.BlockSpec(memory_space=pltpu.VMEM),
        compiler_params=pltpu.CompilerParams(vmem_limit_bytes=24 << 20),
    )(estimate, gradient, step)


def last_update(u, g, step, out_ref):
    t = step[...]
    for p in range(Z):
        out_ref[p] = u[p] - t * g[p]


def solution(mesh):
    ny, nx = mesh.shape["gy"], mesh.shape["gx"]
    return jax.shard_map(
        functools.partial(per_device, ny, nx), mesh=mesh,
        in_specs=(P(None, "gy", "gx"), P(), P()),
        out_specs=P(None, "gy", "gx"), check_vma=False,
    )
```

```python
import functools

import jax
import jax.numpy as jnp
from jax import lax
from jax.experimental import pallas as pl
from jax.experimental.pallas import tpu as pltpu
from jax.sharding import PartitionSpec as P

WEIGHT_TV = 0.02
SMOOTHING = 0.1
DAMPING = 0.05
START_STEP = 0.5
RADIUS = 4
TAPS = 9
Z, CY, CX = 16, 32, 128
EXT = CY + 16
MESH = pl.DeviceIdType.MESH
F32 = jnp.float32
BF16 = jnp.bfloat16
SIDES = ((-1, 0), (1, 0), (0, -1), (0, 1), (-1, -1), (-1, 1), (1, -1), (1, 1))


def kernel(
    ny, nx,
    obs_hbm, prof_hbm, tiles_hbm, u_out, g_out, step_out,
    prof, tiles,
    u_ext, g_ext, grad, tv, resid, back, spread, blur_y, flux,
    fwd, bwd, side_fwd, side_bwd, twice, y_fix, x_fix,
    across_u, square, product, growth,
    ux, gx_halo, own_edge, edge_pad,
    send_y, recv_y, send_x, recv_x,
    part, all_x, part_y, all_y,
    load_sem, table_sem, send_sem, recv_sem, ar_send, ar_recv, known,
):
    row = lax.axis_index("gy")
    col = lax.axis_index("gx")

    def at(dy, dx):
        return {
            "gy": lax.rem(row + dy + ny, ny),
            "gx": lax.rem(col + dx + nx, nx),
        }

    load = pltpu.make_async_copy(obs_hbm, u_ext.at[:, pl.ds(8, CY), :], load_sem)
    load.start()
    table_loads = (
        pltpu.make_async_copy(prof_hbm, prof, table_sem.at[0]),
        pltpu.make_async_copy(tiles_hbm, tiles, table_sem.at[1]),
    )
    table_loads[0].start()
    table_loads[1].start()

    barrier = pltpu.get_barrier_semaphore()

    for dy, dx in SIDES[::-1]:
        pl.semaphore_signal(barrier, inc=1, device_id=at(dy, dx), device_id_type=MESH)

    lane = lax.broadcasted_iota(jnp.int32, (1, CX), 1)
    sub8 = lax.broadcasted_iota(jnp.int32, (8, CX), 0)
    low_half = sub8 < 4
    plane_of = lane // 8
    place = lane - plane_of * 8
    first_row, last_row = row == 0, row == ny - 1
    first_col, last_col = col == 0, col == nx - 1

    back[:, pl.ds(0, 16), :] = jnp.zeros((Z, 16, CX), F32)
    back[:, pl.ds(16 + CY, 16), :] = jnp.zeros((Z, 16, CX), F32)
    edge_pad[pl.ds(0, 16), :] = jnp.zeros((16, CX), F32)
    edge_pad[pl.ds(16 + CY, 16), :] = jnp.zeros((16, CX), F32)
    load.wait()

    def halves(value):
        high = value.astype(BF16)
        return high, (value - high.astype(F32)).astype(BF16)

    def prepare():
        mk = lax.broadcasted_iota(jnp.int32, (CX, CX), 0)
        mn = lax.broadcasted_iota(jnp.int32, (CX, CX), 1)

        def band(diff, taps, keep=None):
            total = jnp.zeros((CX, CX), F32)
            for c in range(TAPS):
                total = jnp.where(diff == c - RADIUS, taps[c], total)
            return total if keep is None else jnp.where(keep, total, 0.0)

        ahead = mn - mk
        planes_ahead = mn // 8 - mk // 8
        places_ahead = ahead - 8 * planes_ahead
        crossing = (mn // 4 + mk // 4) % 2 == 1
        for ref, sign in ((fwd, 1), (bwd, -1)):
            split_matrix(ref, band(sign * ahead, across))
        for ref, sign in ((side_fwd, 1), (side_bwd, -1)):
            split_matrix(
                ref, band(sign * planes_ahead, depth) * band(sign * places_ahead, across, crossing)
            )

    def split_matrix(ref, w):
        high, low = halves(w)
        ref[pl.ds(0, CX), pl.ds(0, CX)] = high
        ref[pl.ds(CX, CX), pl.ds(0, CX)] = high
        ref[pl.ds(0, CX), pl.ds(CX, CX)] = low
        ref[pl.ds(CX, CX), pl.ds(CX, CX)] = jnp.zeros((CX, CX), BF16)

    def times(value, ref):
        high, low = halves(value)
        both = jnp.dot(jnp.concatenate([high, low], axis=1), ref[...], preferred_element_type=F32)
        return both[:, 0:CX] + both[:, CX : 2 * CX]

    def planes(body, init, step=4):
        if step == Z:
            for p in range(Z):
                init = body(p, init)
            return init

        def some(i, carry):
            for k in range(step):
                carry = body(i * step + k, carry)
            return carry

        return lax.fori_loop(0, Z // step, some, init)

    def pack_columns(read):
        def body(p, total):
            turned = pltpu.roll(read(p), 8 * p + 4, 1)
            return jnp.where(plane_of == p, turned, total)

        return planes(body, jnp.zeros((CY, CX), F32), Z)

    def copies(r):
        made = []
        for k, (dy, dx) in enumerate(SIDES):
            if dx == 0:
                src = send_y.at[r, 0 if dy < 0 else 1]
                dst = recv_y.at[r, 1 if dy < 0 else 0]
            else:
                start, size = {-1: (0, 8), 0: (8, CY), 1: (8 + CY, 8)}[dy]
                land = {-1: 8 + CY, 0: 8, 1: 0}[dy]
                src = send_x.at[r, pl.ds(start, size), :]
                dst = recv_x.at[r, 1 if dx < 0 else 0, pl.ds(land, size), :]
            made.append(
                pltpu.make_async_remote_copy(
                    src_ref=src, dst_ref=dst,
                    send_sem=send_sem.at[r, k], recv_sem=recv_sem.at[r, k],
                    device_id=at(dy, dx), device_id_type=MESH,
                )
            )
        return made

    def send_columns(r):
        made = copies(r)
        for k in (4, 5, 6, 7, 2, 3):
            made[k].start()
        return made

    def send_rows(made):
        for k in (0, 1):
            made[k].start()
        return made

    def wait_rows(made):
        made[0].wait_recv()
        made[1].wait_recv()

    def wait_columns(made):
        for k in (2, 3, 4, 5, 6, 7):
            made[k].wait_recv()

    border = (lane < 4) | (lane >= CX - 4)

    def mixing(taps):
        limits = {1: (sub8 <= 0, 5), 2: (sub8 <= 1, 6), 3: (sub8 <= 2, 7), 5: (sub8 >= 5, 1), 6: (sub8 >= 6, 2), 7: (sub8 >= 7, 3)}
        weights = {s: jnp.where(mask, taps[b], 0.0) for s, (mask, b) in limits.items()}
        weights[4] = jnp.where(low_half, taps[8], taps[0])
        return weights

    def put_rows(rows, first, second):
        for q in range(8):
            a, b = rows[q], pltpu.roll(rows[q + 8], 4, 0)
            first[q] = jnp.where(low_half, a, b)
            second[q] = jnp.where(low_half, b, a)

    def get_rows(first, second, no_first, no_second):
        near, far = [], []
        for q in range(8):
            a = jnp.where(no_first, 0.0, first[q])
            b = jnp.where(no_second, 0.0, second[q])
            near.append(jnp.where(low_half, a, b))
            far.append(pltpu.roll(jnp.where(low_half, b, a), 4, 0))
        return near + far

    def cross(rows, taps, transposed, ref):
        for p in range(Z):
            twice[p, pl.ds(0, 8), :] = rows[p]
            twice[p, pl.ds(8, 8), :] = rows[p]
        weights = mixing(taps)
        mixed = []
        for p in range(Z):
            total = weights[4] * twice[p, pl.ds(4, 8), :]
            for s in (1, 2, 3, 5, 6, 7):
                total = total + weights[s] * twice[p, pl.ds(8 - s, 8), :]
            mixed.append(total)
        return times(jnp.concatenate(depth_sum(mixed, transposed), axis=0), ref)

    def edge_rows(read):
        return [jnp.where(low_half, read(p, 0), read(p, CY - 8)) for p in range(Z)]

    def halo_send(r, rows, edge):
        send_x[r, pl.ds(8, CY), :] = edge
        send_x[r, pl.ds(0, 8), :] = edge[0:8]
        send_x[r, pl.ds(8 + CY, 8), :] = edge[CY - 8 : CY]
        made = send_columns(r)
        put_rows(rows(), send_y.at[r, 0], send_y.at[r, 1])
        return send_rows(made)

    def halo_fix(r, made, ext, halo, between=None):
        wait_rows(made)
        rows = get_rows(recv_y.at[r, 1], recv_y.at[r, 0], last_row, first_row)
        for p in range(Z):
            ext[p, pl.ds(0, 8), :] = rows[p]
            ext[p, pl.ds(8 + CY, 8), :] = rows[p]
        y_fix[...] = cross(rows, along, False, fwd)
        packed_fix[:] = [packed_rows_fix()]
        if between is not None:
            made[2].wait_recv()
            made[3].wait_recv()
            halo[pl.ds(8, CY), :] = sides(r, place < 4, 8, CY)
            between()
            for k in (4, 5, 6, 7):
                made[k].wait_recv()
        else:
            wait_columns(made)
        halo[...] = sides(r, place < 4)
        edge = along[0] * halo[pl.ds(8 + RADIUS, CY), :]
        for b in range(1, TAPS):
            edge = edge + along[b] * halo[pl.ds(8 + RADIUS - b, CY), :]
        x_fix[...] = times(edge, side_fwd)

    def spill_send(r, rows, edge):
        edge_pad[pl.ds(16, CY), :] = times(edge, side_bwd)
        total = along[0] * edge_pad[pl.ds(4, EXT), :]
        for b in range(1, TAPS):
            total = total + along[b] * edge_pad[pl.ds(4 + b, EXT), :]
        send_x[r] = total
        made = send_columns(r)
        spilled = cross(rows(), along[::-1], True, bwd)
        put_rows([spilled[8 * p : 8 * p + 8] for p in range(Z)], send_y.at[r, 1], send_y.at[r, 0])
        return send_rows(made)

    def spill_fix(r, made):
        wait_rows(made)
        rows = get_rows(recv_y.at[r, 0], recv_y.at[r, 1], first_row, last_row)
        y_fix[...] = jnp.concatenate(rows, axis=0)
        packed_fix[:] = [packed_rows_fix()]
        wait_columns(made)
        both = sides(r, place >= 4)
        x_fix[pl.ds(0, 8), :] = both[8:16] + both[0:8]
        x_fix[pl.ds(8, 16), :] = both[16:CY]
        x_fix[pl.ds(24, 8), :] = both[CY : CY + 8] + both[CY + 8 : CY + 16]

    packed_fix = []

    def packed_rows_fix():
        packed = jnp.zeros((8, CX), F32)
        for p in range(Z):
            packed = jnp.where(plane_of == p, pltpu.roll(y_fix[pl.ds(8 * p, 8), :], 8 * p + 4, 1), packed)
        return packed

    def fixed_columns(edge):
        packed = packed_fix[0]
        edge = edge + x_fix[...]
        top = edge[0:8] + jnp.where(low_half, packed, 0.0)
        low = edge[CY - 8 : CY] + jnp.where(low_half, 0.0, packed)
        return jnp.concatenate([top, edge[8 : CY - 8], low], axis=0)

    def fixed_rows(read):
        ends = jnp.where(low_half, x_fix[pl.ds(0, 8), :], x_fix[pl.ds(CY - 8, 8), :])
        rows = edge_rows(read)
        for p in range(Z):
            extra = jnp.where(border, pltpu.roll(ends, 124 - 8 * p, 1), 0.0)
            rows[p] = rows[p] + y_fix[pl.ds(8 * p, 8), :] + extra
        return rows

    def with_fix(add):
        extra = x_fix[...]
        for p in range(Z):
            e = jnp.where(border, pltpu.roll(extra, 124 - 8 * p, 1), 0.0)
            y = y_fix[pl.ds(8 * p, 8), :]
            top = e[0:8] + jnp.where(low_half, y, 0.0)
            low = e[CY - 8 : CY] + jnp.where(low_half, 0.0, y)
            add(p, jnp.concatenate([top, e[8 : CY - 8], low], axis=0))

    def sides(r, from_left, start=0, size=EXT):
        left = jnp.where(first_col, 0.0, recv_x[r, 0, pl.ds(start, size), :])
        right = jnp.where(last_col, 0.0, recv_x[r, 1, pl.ds(start, size), :])
        both = jnp.where(from_left, left, right)
        if size < EXT:
            return both
        at_row = lax.broadcasted_iota(jnp.int32, (EXT, CX), 0)
        both = jnp.where(first_row & (at_row < 8), 0.0, both)
        return jnp.where(last_row & (at_row >= 8 + CY), 0.0, both)

    def depth_sum(value, transposed):
        out = []
        for p in range(Z):
            total = None
            for a in range(TAPS):
                source = p - RADIUS + a if transposed else p + RADIUS - a
                if 0 <= source < Z:
                    term = depth[a] * value[source]
                    total = term if total is None else total + term
            out.append(total)
        return out

    def clear_border(ext):
        for p in range(Z):
            ext[p, pl.ds(0, 8), :] = jnp.zeros((8, CX), F32)
            ext[p, pl.ds(8 + CY, 8), :] = jnp.zeros((8, CX), F32)

    def blur_inside(ext, write):
        for group in range(4):
            rows = []
            for p in range(4 * group, 4 * group + 4):
                total = along[0] * ext[p, pl.ds(8 + RADIUS, CY), :]
                for b in range(1, TAPS):
                    total = total + along[b] * ext[p, pl.ds(8 + RADIUS - b, CY), :]
                rows.append(total)
            blur_y[pl.ds(group * 128, 128), :] = times(jnp.concatenate(rows, axis=0), fwd)
        for t in range(CY // 8):
            value = [blur_y[pl.ds(p * CY + t * 8, 8), :] for p in range(Z)]
            for p, total in enumerate(depth_sum(value, False)):
                write(p, t, total)

    def spread_inside(field, write):
        for t in range(CY // 8):
            value = [field[p, pl.ds(t * 8, 8), :] for p in range(Z)]
            out = times(jnp.concatenate(depth_sum(value, True), axis=0), bwd)
            for p in range(Z):
                back[p, pl.ds(16 + t * 8, 8), :] = out[8 * p : 8 * p + 8]

        for p in range(Z):
            total = along[0] * back[p, pl.ds(12, CY), :]
            for b in range(1, TAPS):
                total = total + along[b] * back[p, pl.ds(12 + b, CY), :]
            write(p, total)

    zero8 = jnp.zeros((8, CX), F32)
    main = pl.ds(8, CY)
    rows40 = lax.broadcasted_iota(jnp.int32, (40, CX), 0)
    rows32 = lax.broadcasted_iota(jnp.int32, (CY, CX), 0)
    no_row_diff = last_row & (rows40 == 39)
    no_row_flux = first_row & (rows40 == 7)
    no_col_diff = last_col & (lane == CX - 1)

    def inverse_size(dx, dy, dz):
        return lax.rsqrt(dx * dx + dy * dy + dz * dz + SMOOTHING * SMOOTHING)

    def variation(ext, halo, edges, write):
        here = halo[pl.ds(8, CY), :]
        dx = pltpu.roll(edges, CX - 1, 1) - here
        dy = halo[pl.ds(9, CY), :] - here
        dy = jnp.where(last_row & (rows32 == CY - 1), 0.0, dy)
        dz = jnp.where(plane_of == Z - 1, 0.0, pltpu.roll(here, CX - 8, 1) - here)
        side = jnp.where(first_col, 0.0, dx * inverse_size(dx, dy, dz))
        around = halo[pl.ds(0, 40), :]

        def body(p, before):
            u = ext[p, pl.ds(0, 40), :]
            dy = jnp.where(no_row_diff, 0.0, ext[p, pl.ds(1, 40), :] - u)
            beyond = pltpu.roll(around, 124 - 8 * p, 1)
            dx = pltpu.roll(jnp.where(lane == 0, beyond, u), CX - 1, 1) - u
            dx = jnp.where(no_col_diff, 0.0, dx)
            after = ext[min(p + 1, Z - 1) if isinstance(p, int) else jnp.minimum(p + 1, Z - 1), pl.ds(0, 40), :]
            dz = after - u
            inverse = inverse_size(dx, dy, dz)
            fy = jnp.where(no_row_flux, 0.0, dy * inverse)
            flux[...] = fy
            fx = (dx * inverse)[8:40]
            fz = (dz * inverse)[8:40]
            fx_side = pltpu.roll(side, 124 - 8 * p, 1)
            fx_before = pltpu.roll(jnp.where(lane == CX - 1, fx_side, fx), 1, 1)
            slope = (before - fz) + (flux[pl.ds(7, CY), :] - fy[8:40]) + (fx_before - fx)
            write(p, slope)
            return fz

        planes(body, jnp.zeros((CY, CX), F32), 4)

    def rows8(value):
        return value[0:8] + value[8:16] + value[16:24] + value[24:32]

    final_lane = lane == CX - 1
    next_lane = final_lane & jnp.logical_not(last_col)
    next_row = (sub8 == 7) & jnp.logical_not(last_row)

    def tension_inside():
        around = ux[pl.ds(8, CY), :]

        def body(p, total):
            u, g = u_ext[p, main, :], g_ext[p, main, :]
            after = min(p + 1, Z - 1) if isinstance(p, int) else jnp.minimum(p + 1, Z - 1)
            dz = u_ext[after, main, :] - u
            ez = g_ext[after, main, :] - g
            dy = jnp.where(last_row & (rows32 == CY - 1), 0.0, u_ext[p, pl.ds(9, CY), :] - u)
            ey = jnp.where(rows32 == CY - 1, 0.0, g_ext[p, pl.ds(9, CY), :] - g)
            beyond = pltpu.roll(around, 124 - 8 * p, 1)
            dx = pltpu.roll(jnp.where(lane == 0, beyond, u), CX - 1, 1) - u
            dx = jnp.where(no_col_diff, 0.0, dx)
            ex = jnp.where(final_lane, 0.0, pltpu.roll(g, CX - 1, 1) - g)
            across_u[p] = dx
            square[p] = dx * dx + dy * dy + dz * dz + SMOOTHING * SMOOTHING
            product[p] = dx * ex + dy * ey + dz * ez
            growth[p] = ex * ex + ey * ey + ez * ez
            return total[0] + rows8(g * g), total[1] + rows8(g * tv[p])

        return planes(body, (zero8, zero8))

    def tension_border():
        around = gx_halo[pl.ds(8, CY), :]
        for p in range(Z):
            ex = jnp.where(next_lane, pltpu.roll(around, 123 - 8 * p, 1) - g_ext[p, main, :], 0.0)
            product[p] = product[p] + across_u[p] * ex
            growth[p] = growth[p] + ex * ex
            bottom = pl.ds(CY - 8, 8)
            ey = jnp.where(next_row, g_ext[p, pl.ds(CY + 1, 8), :] - g_ext[p, pl.ds(CY, 8), :], 0.0)
            dy = u_ext[p, pl.ds(CY + 1, 8), :] - u_ext[p, pl.ds(CY, 8), :]
            product[p, bottom, :] = product[p, bottom, :] + dy * ey
            growth[p, bottom, :] = growth[p, bottom, :] + ey * ey

    def tension_sum(step):
        total = zero8
        for p in range(Z):
            part_ = product[p] - step * growth[p]
            size = square[p] - step * (product[p] + part_)
            size = jnp.maximum(size, SMOOTHING * SMOOTHING)
            total = total + rows8(part_ * lax.rsqrt(size))
        return total

    def fold(values):
        total = jnp.zeros((1, CX), F32)
        for i, value in enumerate(values):
            v = jnp.sum(value, axis=0, keepdims=True)
            v = v + pltpu.roll(v, 64, 1)
            v = v + pltpu.roll(v, 32, 1)
            total = jnp.where(lane // 32 == i, v, total)
        return total

    def far_first_x():
        if nx != 32:
            return [lax.rem(col + i, nx) for i in range(1, nx)]
        x, y, core = col // 8, lax.rem(col // 2, 4), lax.rem(col, 2)
        xs = [lax.rem(x + i, 4) * 8 for i in range(4)]
        ys = [lax.rem(y + i, 4) * 2 for i in range(4)]
        cores = [core, 1 - core]
        ring = (0, 1, 2, 1)
        moves = [(i, j, k) for i in range(4) for j in range(4) for k in range(2)][1:]
        moves.sort(key=lambda m: -(ring[m[0]] + ring[m[1]] + 0.3 * m[2]))
        return [xs[i] + ys[j] + cores[k] for i, j, k in moves]

    def reduce_start(a, values):
        mine = fold(values)
        part[a] = mine
        all_x[a, pl.ds(col, 1)] = mine.reshape(1, 1, CX)

        for peer in far_first_x():
            pltpu.make_async_remote_copy(
                src_ref=part.at[a], dst_ref=all_x.at[a, col],
                send_sem=ar_send.at[a, 0], recv_sem=ar_recv.at[a, 0],
                device_id={"gy": row, "gx": peer}, device_id_type=MESH,
            ).start()

    def reduce_middle(a):
        got = all_x.at[a, pl.ds(0, nx - 1)]
        pltpu.make_async_copy(got, got, ar_recv.at[a, 0]).wait()
        mine = jnp.sum(all_x[a], axis=0)
        part_y[a] = mine
        all_y[a, pl.ds(row, 1)] = mine.reshape(1, 1, CX)

        for i in sorted(range(1, ny), key=lambda i: -min(i, ny - i)):
            pltpu.make_async_remote_copy(
                src_ref=part_y.at[a], dst_ref=all_y.at[a, row],
                send_sem=ar_send.at[a, 1], recv_sem=ar_recv.at[a, 1],
                device_id=at(i, 0), device_id_type=MESH,
            ).start()

    def reduce_end(a):
        got = all_y.at[a, pl.ds(0, ny - 1)]
        pltpu.make_async_copy(got, got, ar_recv.at[a, 1]).wait()
        total = jnp.sum(all_y[a], axis=0)
        return [jnp.sum(jnp.where(lane // 32 == i, total, 0.0), axis=1, keepdims=True) for i in range(3)]

    def tell(level, distance, axes=(0, 1)):
        for axis, n in enumerate((ny, nx)):
            if axis in axes and n // 2 > distance:
                for d in (-distance, distance):
                    pl.semaphore_signal(
                        known.at[axis, level], inc=1,
                        device_id=at(d, 0) if axis == 0 else at(0, d), device_id_type=MESH,
                    )

    def hear(level, distance, axes=(0, 1)):
        for axis, n in enumerate((ny, nx)):
            if axis in axes and n // 2 > distance:
                pl.semaphore_wait(known.at[axis, level], 2)

    def keep_tv(p, slope):
        tv[p] = slope

    def advance(step):
        def body(p, c):
            u_ext[p] = u_ext[p] - step * g_ext[p]
            return c

        planes(body, 0)
        ux[...] = ux[...] - step * gx_halo[...]
        own_edge[0] = own_edge[0] - step * own_edge[1]

    def read_main(ext):
        return lambda p, start: ext[p, pl.ds(8 + start, 8), :]

    def read_field(field):
        return lambda p, start: field[p, pl.ds(start, 8), :]

    def packed_main(ext):
        return pack_columns(lambda p: ext[p, main, :])

    def add_main(p, extra):
        g_ext[p, main, :] = g_ext[p, main, :] + extra

    def finish_blur():
        sums = []

        def add(p, extra):
            h = grad[p] + extra
            grad[p] = h
            sums.append(rows8(h * h))

        with_fix(add)
        while len(sums) > 1:
            sums = [x + y for x, y in zip(sums[::2], sums[1::2])]
        return sums[0]

    def add_resid(p, extra):
        resid[p] = resid[p] + extra

    def keep_grad(p, t, value):
        grad[p, pl.ds(t * 8, 8), :] = value

    def keep_spread(p, value):
        spread[p] = value

    def gradient_inside():
        def body(p, c):
            g_ext[p, main, :] = spread[p] + WEIGHT_TV * tv[p] + DAMPING * u_ext[p, main, :]
            return c

        planes(body, 0)

    def send_gradient(r, edge):
        edge = fixed_columns(edge)
        own_edge[1] = edge
        return halo_send(r, lambda: fixed_rows(read_main(g_ext)), edge)

    def spread_and_slope(field):
        spread_inside(field, keep_spread)
        variation(u_ext, ux, own_edge[0], keep_tv)

    waiting = []
    clear_border(u_ext)
    edge = packed_main(u_ext)
    own_edge[0] = edge
    pl.semaphore_wait(barrier, len(SIDES))
    made = halo_send(0, lambda: edge_rows(read_main(u_ext)), edge)
    waiting += made
    table_loads[0].wait()
    table_loads[1].wait()
    number = tiles[row, col]
    depth = [prof[a, 0, number] for a in range(TAPS)]
    along = [prof[a, 1, number] for a in range(TAPS)]
    across = [prof[a, 2, number] for a in range(TAPS)]
    prepare()

    def keep_residual(p, t, value):
        resid[p, pl.ds(t * 8, 8), :] = value - u_ext[p, pl.ds(8 + t * 8, 8), :]

    blur_inside(u_ext, keep_residual)
    edge = pack_columns(lambda p: resid[p])
    halo_fix(0, made, u_ext, ux)
    made = spill_send(1, lambda: fixed_rows(read_field(resid)), fixed_columns(edge))
    waiting += made
    tell(0, 2)
    with_fix(add_resid)
    spread_and_slope(resid)
    gradient_inside()
    edge = packed_main(g_ext)
    spill_fix(1, made)
    made = send_gradient(2, edge)
    waiting += made
    hear(0, 2)
    tell(1, 4)
    with_fix(add_main)
    clear_border(g_ext)
    blur_inside(g_ext, keep_grad)
    gg, gt = tension_inside()
    hear(1, 4, (1,))
    tell(2, 8)
    sums = []

    def tension():
        tension_border()
        sums.append(tension_sum(START_STEP))

    halo_fix(2, made, g_ext, gx_halo, tension)
    hh = finish_blur()
    gt = sums[0] - gt
    hear(2, 8)
    reduce_start(0, (gg, hh, gt))

    def next_residual(p, c):
        resid[p] = resid[p] - START_STEP * grad[p]
        return c

    planes(next_residual, 0)
    made = spill_send(3, lambda: edge_rows(read_field(resid)), pack_columns(lambda p: resid[p]))
    waiting += made
    advance(START_STEP)
    spread_and_slope(resid)
    gradient_inside()
    edge = packed_main(g_ext)
    hear(1, 4, (0,))
    reduce_middle(0)
    spill_fix(3, made)
    made = send_gradient(4, edge)
    waiting += made

    def keep_pulled(p, extra):
        add_main(p, extra)
        resid[p] = spread[p] + extra

    with_fix(keep_pulled)
    clear_border(g_ext)
    blur_inside(g_ext, keep_grad)
    gg, gt = tension_inside()
    halo_fix(4, made, g_ext, gx_halo, tension_border)
    hh = finish_blur()
    g2, h2, t2 = reduce_end(0)
    change_sq = START_STEP * START_STEP * g2
    change_growth = START_STEP * START_STEP * (h2 + DAMPING * g2) - START_STEP * WEIGHT_TV * t2
    step = change_sq / change_growth

    gt = tension_sum(step) - gt
    reduce_start(1, (gg, hh, gt))

    made = spill_send(5, lambda: edge_rows(read_field(grad)), pack_columns(lambda p: grad[p]))
    waiting += made
    advance(step)
    spread_and_slope(grad)
    reduce_middle(1)
    spill_fix(5, made)

    def last(p, extra):
        pulled = resid[p] - step * (spread[p] + extra)
        u = u_ext[p, main, :]
        u_out[p] = u
        g_out[p] = pulled + WEIGHT_TV * tv[p] + DAMPING * u

    with_fix(last)
    for c in waiting:
        c.wait_send()
    for a in range(2):
        got = all_x.at[a, pl.ds(0, nx - 1)]
        pltpu.make_async_copy(got, got, ar_send.at[a, 0]).wait()
        got = all_y.at[a, pl.ds(0, ny - 1)]
        pltpu.make_async_copy(got, got, ar_send.at[a, 1]).wait()
    g2, h2, t2 = reduce_end(1)
    change_sq = step * step * g2
    change_growth = step * step * (h2 + DAMPING * g2) - step * WEIGHT_TV * t2
    step_out[...] = jnp.broadcast_to(change_sq / change_growth, (1, CX))


def per_device(ny, nx, observed, profiles, tile_index):
    field = pltpu.VMEM((Z, CY, CX), F32)
    extended = pltpu.VMEM((Z, EXT, CX), F32)
    matrix = pltpu.VMEM((2 * CX, 2 * CX), BF16)
    rounds = 6
    scratch = [
        pltpu.SMEM((TAPS, 3, profiles.shape[0]), F32), pltpu.SMEM((ny, nx), jnp.int32),
        extended, extended, field, field, field,
        pltpu.VMEM((Z, CY + 32, CX), F32), field,
        pltpu.VMEM((Z * CY, CX), F32), pltpu.VMEM((40, CX), F32),
        matrix, matrix, matrix, matrix,
        pltpu.VMEM((Z, 16, CX), F32), pltpu.VMEM((Z * 8, CX), F32), pltpu.VMEM((CY, CX), F32),
        field, field, field, field,
        pltpu.VMEM((EXT, CX), F32), pltpu.VMEM((EXT, CX), F32),
        pltpu.VMEM((2, CY, CX), F32), pltpu.VMEM((CY + 32, CX), F32),
        pltpu.VMEM((rounds, 2, 8, 8, CX), F32), pltpu.VMEM((rounds, 2, 8, 8, CX), F32),
        pltpu.VMEM((rounds, EXT, CX), F32), pltpu.VMEM((rounds, 2, EXT, CX), F32),
        pltpu.VMEM((2, 1, CX), F32), pltpu.VMEM((2, nx, 1, CX), F32),
        pltpu.VMEM((2, 1, CX), F32), pltpu.VMEM((2, ny, 1, CX), F32),
        pltpu.SemaphoreType.DMA, pltpu.SemaphoreType.DMA((2,)),
        pltpu.SemaphoreType.DMA((rounds, 8)), pltpu.SemaphoreType.DMA((rounds, 8)),
        pltpu.SemaphoreType.DMA((2, 2)), pltpu.SemaphoreType.DMA((2, 2)),
        pltpu.SemaphoreType.REGULAR((2, 3)),
    ]
    whole = pltpu.VMEM((Z, CY, CX), F32)
    estimate, gradient, step = pl.pallas_call(
        functools.partial(kernel, ny, nx),
        out_shape=(whole, whole, pltpu.VMEM((1, CX), F32)),
        in_specs=[pl.BlockSpec(memory_space=pltpu.HBM)] * 3,
        out_specs=(pl.BlockSpec(memory_space=pltpu.VMEM),) * 3,
        scratch_shapes=scratch,
        compiler_params=pltpu.CompilerParams(
            collective_id=0, has_side_effects=True
        ),
    )(observed, jnp.transpose(profiles, (2, 1, 0)), tile_index)
    return pl.pallas_call(
        last_update,
        out_shape=jax.ShapeDtypeStruct((Z, CY, CX), F32),
        in_specs=[pl.BlockSpec(memory_space=pltpu.VMEM)] * 3,
        out_specs=pl.BlockSpec(memory_space=pltpu.VMEM),
        compiler_params=pltpu.CompilerParams(vmem_limit_bytes=24 << 20),
    )(estimate, gradient, step)


def last_update(u, g, step, out_ref):
    t = step[...]
    for p in range(Z):
        out_ref[p] = u[p] - t * g[p]


def solution(mesh):
    ny, nx = mesh.shape["gy"], mesh.shape["gx"]
    return jax.shard_map(
        functools.partial(per_device, ny, nx), mesh=mesh,
        in_specs=(P(None, "gy", "gx"), P(), P()),
        out_specs=P(None, "gy", "gx"), check_vma=False,
    )
```
